32 devices in a mesh: fsdp: 4 (over z), ctx: 4 (over y, x), tp: 2 (over core).
Axes of the slice: x: 2, y: 2, z: 4, core: 2. Of those that a mesh axis runs over, the one named last changes fastest.
Arguments:
- tokens: bfloat16 [2, 4, 4, 256, 1024], P(None, None, 'ctx', 'fsdp'), may hold values from -6 to 6
- cotangent: bfloat16 [2, 4, 4, 256, 1024], P(None, None, 'ctx', 'fsdp'), may hold values from -6 to 6
- lengths: int32 [2, 4], replicated, may hold values from 256 to 1024, as said below
- owners: int32 [2, 4], replicated, may hold values from 0 to 3, each once within a row
- norm_attn: bfloat16 [1024], P(('fsdp', 'ctx')), may hold values from 0.099609375 to 1.8984375
- norm_mlp: bfloat16 [1024], P(('fsdp', 'ctx')), may hold values from 0.099609375 to 1.8984375
- w_qkv: bfloat16 [1024, 3, 1024], P(('fsdp', 'ctx'), None, 'tp'), may hold values from -0.1875 to 0.1875
- w_out: bfloat16 [1024, 1024], P('tp', ('fsdp', 'ctx')), may hold values from -3 to 3
- w_in: bfloat16 [1024, 2, 2624], P(('fsdp', 'ctx'), None, 'tp'), may hold values from -0.1875 to 0.1875
- w_down: bfloat16 [2624, 1024], P('tp', ('fsdp', 'ctx')), may hold values from -0.15625 to 0.15625
Outputs:
- output: bfloat16 [2, 4, 4, 256, 1024], P(None, None, 'ctx', 'fsdp')
- grad_tokens: bfloat16 [2, 4, 4, 256, 1024], P(None, None, 'ctx', 'fsdp')
- grad_norm_attn: float32 [1024], P(('fsdp', 'ctx'))
- grad_norm_mlp: float32 [1024], P(('fsdp', 'ctx'))
- grad_w_qkv: float32 [1024, 3, 1024], P(('fsdp', 'ctx'), None, 'tp')
- grad_w_out: float32 [1024, 1024], P('tp', ('fsdp', 'ctx'))
- grad_w_in: float32 [1024, 2, 2624], P(('fsdp', 'ctx'), None, 'tp')
- grad_w_down: float32 [2624, 1024], P('tp', ('fsdp', 'ctx'))
The draws below stay inside these ranges and needn't reach their ends.
Inputs may be any that keep to these rules, and one draw needn't show every extreme that they name: Each row of owners names every owner slot once; sequence s of micro-batch m belongs to slot owners[m, s], and slot j is worked on by index j of fsdp. lengths[m, j] counts the live positions of the sequence in owner slot j; every micro-batch has one sequence of exactly 1024 and one of exactly 256 positions.
All inputs are finite; a program needn't handle non-finite values.
Results may differ from the reference program's by a relative error of at most 0.023.
Values may be sent and summed in bfloat16 or wider, within the bound.
A program may use at most 192 MiB of HBM per device.

```python
import jax
import jax.numpy as jnp
from jax import lax

D = 1024
HEADS = 16
HEAD_DIM = 64
FF = 2624
SPAN = 256
MICRO = 2
SEQS = 4
SLOT = 1024
N_CTX = 4


def draw_lengths(key, part):
    drawn = jax.random.randint(jax.random.fold_in(key, 1), (MICRO, SEQS), SLOT // 4, SLOT + 1)
    longest = jax.random.randint(jax.random.fold_in(key, 2), (MICRO,), 0, SEQS)
    offset = jax.random.randint(jax.random.fold_in(key, 3), (MICRO,), 1, SEQS)
    shortest = (longest + offset) % SEQS
    micro_rows = jnp.arange(MICRO)
    drawn = drawn.at[micro_rows, longest].set(SLOT)
    drawn = drawn.at[micro_rows, shortest].set(SLOT // 4)
    return drawn.astype(jnp.int32)


def steps_of(own_key, dims, split, least, high):
    factor_of = 1.0
    for dim, parts in split:
        draws = jax.random.uniform(jax.random.fold_in(jax.random.fold_in(own_key, 6), dim), (parts,), jnp.float32, least / len(split), high / len(split))
        factor_of = factor_of * jnp.repeat(jnp.exp(draws), dims[dim] // parts).reshape((-1,) + (1,) * (len(dims) - 1 - dim))
    return factor_of


def normal_values(stream_key, dims, scale, reach, split=(), kind=jnp.bfloat16):
    entries = jax.random.normal(stream_key, dims, jnp.float32) * scale
    if len(split) > 0:
        entries = steps_of(stream_key, dims, split, -0.22, 0.18) * entries
    return jnp.clip(entries, min=-reach, max=reach).astype(kind)


def setup_inputs(seed: int = 0) -> dict:
    streams_of = jax.random.split(jax.random.key(seed), 11)
    tokens = normal_values(streams_of[0], (MICRO, SEQS, N_CTX, SPAN, D), 1.0, 6.0, ((2, 4), (3, 4)))
    cotangent = normal_values(streams_of[1], (MICRO, SEQS, N_CTX, SPAN, D), 1.0, 6.0, ((2, 4), (3, 4)))
    lengths = draw_lengths(jax.random.fold_in(streams_of[10], 71), 0)
    owners = jax.vmap(lambda own: jax.random.permutation(own, SEQS))(jax.random.split(streams_of[3], MICRO)).reshape((MICRO, SEQS)).astype(jnp.int32)
    norm_attn = jnp.clip(1.0 + 0.18 * jax.random.normal(streams_of[4], (D,), jnp.float32), 0.099609375, 1.8984375).astype(jnp.bfloat16)
    norm_mlp = jnp.clip(1.0 + 0.18 * jax.random.normal(streams_of[5], (D,), jnp.float32), 0.099609375, 1.8984375).astype(jnp.bfloat16)
    w_qkv = normal_values(streams_of[6], (D, 3, D), D ** -0.5, 0.1875, ((0, 16), (2, 2)))
    w_out = normal_values(streams_of[7], (D, D), (4 * D // SLOT) ** -0.5, 3.0, ((0, 2), (1, 16)))
    w_in = normal_values(streams_of[8], (D, 2, FF), D ** -0.5, 0.1875, ((0, 16), (2, 2)))
    w_down = normal_values(streams_of[9], (FF, D), (FF // 2) ** -0.5, 0.15625, ((0, 2), (1, 16)))
    return {"tokens": tokens, "cotangent": cotangent, "lengths": lengths, "owners": owners, "norm_attn": norm_attn, "norm_mlp": norm_mlp, "w_qkv": w_qkv, "w_out": w_out, "w_in": w_in, "w_down": w_down}


@jax.custom_vjp
def low(v):
    return lax.optimization_barrier(v.astype(jnp.bfloat16)).astype(jnp.float32)

@jax.custom_vjp
def low_back(v):
    return v

def low_keep(v):
    return (low(v), None)

def low_pass(kept, grad):
    return (grad,)

def back_keep(v):
    return (v, None)

def back_low(kept, grad):
    return (low(grad),)
low.defvjp(low_keep, low_pass)
low_back.defvjp(back_keep, back_low)
norm_eps = 1e-05
rope_base = 160000.0
masked_score = -1e+30

def highest(left, right):
    return jnp.dot(left, right, precision=lax.Precision.HIGHEST)

def layer_norm(values, norm_gain):
    center = values - lax.optimization_barrier(jnp.mean(values, axis=-1, keepdims=True))
    spread = lax.optimization_barrier(jnp.mean(center * center, axis=-1, keepdims=True))
    return center * lax.rsqrt(spread + norm_eps) * norm_gain

def rope_tables(positions):
    inverse = rope_base ** (-jnp.arange(0, HEAD_DIM, 2).astype(jnp.float32) / HEAD_DIM)
    angles = positions.astype(jnp.float32)[:, None] * inverse[None, :]
    return (jnp.cos(angles)[:, None, :], jnp.sin(angles)[:, None, :])

def rotary(values, cosine_table, sine_table):
    half_dim = values.shape[-1] // 2
    first_half = values[..., :half_dim]
    second_half = values[..., half_dim:]
    return jnp.concatenate([first_half * cosine_table - second_half * sine_table, second_half * cosine_table + first_half * sine_table], axis=-1)

def forward(seq_tokens, live_count, gain_attn, gain_mlp, qkv_weight, out_weight, in_weight, down_weight):
    row_count = seq_tokens.shape[0]
    first_low = low(layer_norm(seq_tokens, gain_attn))
    joined_proj = low_back(highest(first_low, qkv_weight.reshape(D, 3 * D))).reshape(row_count, 3, HEADS, HEAD_DIM)
    cosine_table, sine_table = rope_tables(jnp.arange(row_count, dtype=jnp.int32))
    queries = low(rotary(joined_proj[:, 0], cosine_table, sine_table))
    key_rows = low(rotary(joined_proj[:, 1], cosine_table, sine_table))
    values = low(joined_proj[:, 2])
    live_keys = jnp.arange(row_count, dtype=jnp.int32) < live_count

    def attend(query_block):
        scores = low_back(jnp.einsum('qhd,khd->hqk', query_block, key_rows, precision=lax.Precision.HIGHEST) * HEAD_DIM ** (-0.5))
        scores = jnp.where(live_keys[None, None, :], scores, masked_score)
        attn_probs = low(jax.nn.softmax(scores, axis=-1))
        return jnp.einsum('hqk,khd->qhd', attn_probs, values, precision=lax.Precision.HIGHEST)
    query_rows = min(512, row_count)
    blocks = queries.reshape(row_count // query_rows, query_rows, HEADS, HEAD_DIM)
    mixed_heads = lax.map(jax.checkpoint(attend), blocks).reshape(row_count, D)
    attended = low_back(highest(low(low_back(mixed_heads)), out_weight))
    hidden_in = seq_tokens + attended
    second = low(layer_norm(hidden_in, gain_mlp))
    gate_up = low_back(highest(second, in_weight.reshape(D, 2 * FF)))
    activated = low(jax.nn.gelu(gate_up[:, :FF], approximate=False) * gate_up[:, FF:])
    return hidden_in + low_back(highest(activated, down_weight))

def reference(tokens, cotangent, lengths, owners, norm_attn, norm_mlp, w_qkv, w_out, w_in, w_down):
    seqs_tokens = tokens.reshape(MICRO * SEQS, SLOT, D)
    seqs_cot = cotangent.reshape(MICRO * SEQS, SLOT, D)
    live_counts = jnp.take_along_axis(lengths, owners, axis=1).reshape(MICRO * SEQS).astype(jnp.int32)
    float_weights = tuple((weight_item.astype(jnp.float32) for weight_item in (norm_attn, norm_mlp, w_qkv, w_out, w_in, w_down)))

    def one_sequence(totals, inputs):
        seq_tokens, seq_cot, live_count = inputs

        def closed(token_values, *params):
            return forward(token_values, live_count, *params)
        result, pullback = jax.vjp(closed, seq_tokens.astype(jnp.float32), *float_weights)
        all_grads = pullback(seq_cot.astype(jnp.float32))
        new_totals = tuple((total_part + grad_part for total_part, grad_part in zip(totals, all_grads[1:])))
        return (new_totals, (result.astype(jnp.bfloat16), all_grads[0].astype(jnp.bfloat16)))
    zero_totals = tuple((jnp.zeros(weight_item.shape, jnp.float32) for weight_item in float_weights))
    totals, (outputs, input_grads) = lax.scan(one_sequence, zero_totals, (seqs_tokens, seqs_cot, live_counts))
    return (outputs.reshape(tokens.shape), input_grads.reshape(tokens.shape), totals[0], totals[1], totals[2], totals[3], totals[4], totals[5])
```

```python
import functools

import jax
import jax.numpy as jnp
from jax import lax
from jax.experimental import pallas as pl
from jax.experimental.pallas import tpu as pltpu
from jax.sharding import PartitionSpec as P

D = 1024
HEAD_DIM = 64
norm_eps = 1e-05
rope_base = 160000.0
masked_score = -1e30
MESH = pl.DeviceIdType.MESH
BF = jnp.bfloat16
F32 = jnp.float32
VLIMIT = 56 << 20


def nn(a, b):
    return lax.dot_general(a, b, (((1,), (0,)), ((), ())), preferred_element_type=F32)


def nt(a, b):
    return lax.dot_general(a, b, (((1,), (1,)), ((), ())), preferred_element_type=F32)


def tn(a, b):
    return lax.dot_general(a, b, (((0,), (0,)), ((), ())), preferred_element_type=F32)


def norm_stats(values):
    center = values - jnp.mean(values, axis=-1, keepdims=True)
    spread = jnp.mean(center * center, axis=-1, keepdims=True)
    inverse_std = lax.rsqrt(spread + norm_eps)
    return center * inverse_std, inverse_std


def norm_back(upstream, normed, inverse_std, gain):
    scaled = upstream * gain
    adjusted = (
        scaled
        - jnp.mean(scaled, axis=-1, keepdims=True)
        - normed * jnp.mean(scaled * normed, axis=-1, keepdims=True)
    )
    return adjusted * inverse_std


def here():
    return lax.axis_index("fsdp"), lax.axis_index("ctx"), lax.axis_index("tp")


def remote(src, dst, sems, i, where):
    return pltpu.make_async_remote_copy(
        src_ref=src,
        dst_ref=dst,
        send_sem=sems.at[0, i],
        recv_sem=sems.at[1, i],
        device_id=where,
        device_id_type=MESH,
    )


def greet(peers):
    bar = pltpu.get_barrier_semaphore()
    for p in peers:
        pl.semaphore_signal(bar, inc=1, device_id=p, device_id_type=MESH)
    pl.semaphore_wait(bar, len(peers))


def plane_gather(full, sems, base=0):
    f, c, t = here()
    px, py, po = (f, c ^ 1, t), (f, c ^ 2, t), (f, c, 1 - t)
    cx, cy, cd = c ^ 1, c ^ 2, c ^ 3

    def cp(i, view, where):
        return remote(view, view, sems, base + i, where)

    sends = [
        cp(0, full.at[t, c], px),
        cp(1, full.at[t, c], py),
        cp(2, full.at[t, c], po),
    ]
    for s in sends:
        s.start()
    sends[0].wait_recv()
    more = [cp(3, full.at[t, cx, 1], py), cp(4, full.at[t, cx], po)]
    for s in more:
        s.start()
    sends[1].wait_recv()
    more += [cp(5, full.at[t, cy, 0], px), cp(6, full.at[t, cy], po)]
    for s in more[2:]:
        s.start()
    more[0].wait_recv()
    more[2].wait_recv()
    last = cp(7, full.at[t, cd], po)
    last.start()
    for s in (sends[2], more[1], more[3], last):
        s.wait_recv()
    for s in sends + more + [last]:
        s.wait_send()


GATHER_SEMS = 8
REDUCE_SEMS = 10


def plane_reduce(make, part, r0, rx, ry, sems, base=0):
    f, c, t = here()
    px, py, po = (f, c ^ 1, t), (f, c ^ 2, t), (f, c, 1 - t)
    cx, cy, cd = c ^ 1, c ^ 2, c ^ 3
    order = (cd, cx, cy, c)
    cross = []
    for i, span in enumerate(order):
        make(1 - t, span)
        s = remote(part.at[1 - t, span], r0.at[i], sems, base + i, po)
        s.start()
        cross.append(s)
    for span in order:
        make(t, span)

    def add(i, span):
        cross[i].wait_recv()
        part[t, span] = (part[t, span].astype(F32) + r0[i].astype(F32)).astype(BF)

    add(0, cd)
    a0 = remote(part.at[t, cd, 0], rx.at[0], sems, base + 4, px)
    b0 = remote(part.at[t, cd, 1], ry.at[0], sems, base + 5, py)
    a0.start()
    b0.start()
    add(1, cx)
    a1 = remote(part.at[t, cx, 0], rx.at[1], sems, base + 6, px)
    a1.start()
    add(2, cy)
    b1 = remote(part.at[t, cy, 1], ry.at[1], sems, base + 7, py)
    b1.start()
    a0.wait_recv()
    part[t, cy, 0] = (part[t, cy, 0].astype(F32) + rx[0].astype(F32)).astype(BF)
    b2 = remote(part.at[t, cy, 0], ry.at[2], sems, base + 8, py)
    b2.start()
    b0.wait_recv()
    part[t, cx, 1] = (part[t, cx, 1].astype(F32) + ry[0].astype(F32)).astype(BF)
    a2 = remote(part.at[t, cx, 1], rx.at[2], sems, base + 9, px)
    a2.start()
    cross[3].wait_recv()
    own = part[t, c].astype(F32) + r0[3].astype(F32)
    a1.wait_recv()
    b1.wait_recv()
    b2.wait_recv()
    top = own[0] + rx[1].astype(F32) + ry[2].astype(F32)
    a2.wait_recv()
    bottom = own[1] + ry[1].astype(F32) + rx[2].astype(F32)
    for s in cross + [a0, b0, a1, b1, a2, b2]:
        s.wait_send()
    return jnp.concatenate([top, bottom], axis=0)


def reduce_scratch(rows):
    return [
        pltpu.VMEM((2, 4, 2, rows, D), BF),
        pltpu.VMEM((4, 2, rows, D), BF),
        pltpu.VMEM((3, rows, D), BF),
        pltpu.VMEM((3, rows, D), BF),
    ]


def vm():
    return pl.BlockSpec(memory_space=pltpu.VMEM)


def shaped(shape, dtype):
    return jax.ShapeDtypeStruct(shape, dtype)


def comm_call(kernel, out_shape, scratch, n_sems, cid, n_in):
    return pl.pallas_call(
        kernel,
        out_shape=out_shape,
        in_specs=[vm()] * n_in,
        out_specs=jax.tree.map(lambda _: vm(), out_shape),
        scratch_shapes=scratch + [pltpu.SemaphoreType.DMA((2, n_sems))],
        compiler_params=pltpu.CompilerParams(
            collective_id=cid, has_side_effects=True, vmem_limit_bytes=VLIMIT
        ),
    )


def start_kernel(
    n_f, tok, cot, gains, w1, w2, w3, tok_o, cot_o, gains_o, w1_o, w2_o, w3_o, low_o, gz, gp, sems
):
    f, c, t = here()
    plane = [(f, c ^ 1, t), (f, c ^ 2, t), (f, c ^ 3, t)]
    zs = [(lax.rem(f + k, n_f), c, t) for k in range(1, n_f)]
    greet(plane + zs + [(f, c, 1 - t)])
    n_z = n_f - 1
    toks = [remote(tok.at[zs[k][0]], tok_o.at[f], sems, k, zs[k]) for k in range(n_z)]
    gs = [remote(gains, gz.at[f], sems, n_z + k, zs[k]) for k in range(n_z)]
    for k in range(n_z):
        gs[k].start()
        toks[k].start()
    base = 2 * n_z
    ws = []
    for k in range(3):
        for j, (src, dst) in enumerate(((w1, w1_o), (w2, w2_o), (w3, w3_o))):
            ws.append(remote(src.at[plane[k][1]], dst.at[c], sems, base + 3 * k + j, plane[k]))
            ws[-1].start()
    base += 9
    for src, dst in ((w1, w1_o), (w2, w2_o), (w3, w3_o)):
        dst[c] = src[c]
    tok_o[f] = tok[f]
    cot_o[f] = cot[f]
    gz[f] = gains[...]
    for g in gs:
        g.wait_recv()
    gp[c] = jnp.sum(gz[...], axis=0)
    gps = [remote(gp.at[c], gp.at[c], sems, base + k, plane[k]) for k in range(3)]
    for g in gps:
        g.start()
    base += 3
    for s in toks:
        s.wait_recv()
    cots = [remote(cot.at[zs[k][0]], cot_o.at[f], sems, base + k, zs[k]) for k in range(n_z)]
    for s in cots:
        s.start()
    base += n_z
    for g in gps:
        g.wait_recv()
    gains_o[...] = jnp.sum(gp[...], axis=0)
    rows = tok_o[...].reshape(-1, D).astype(F32)
    hat, _ = norm_stats(rows)
    low_o[t, c] = (hat * gains_o[0:1, :]).astype(BF).reshape(2, -1, D)
    plane_gather(low_o, sems, base)
    for s in ws + cots:
        s.wait_recv()
    for s in toks + gs + ws + gps + cots:
        s.wait_send()


def mid1_kernel(mixed, w_out, tok, gains, hidden_o, low_o, part, r0, rx, ry, sems):
    f, c, t = here()
    greet([(f, c ^ 1, t), (f, c ^ 2, t), (f, c, 1 - t)])
    half = part.shape[3]

    def make(m, span):
        part[m, span] = nt(mixed[m, span], w_out[...]).astype(BF).reshape(2, half, D)

    summed = plane_reduce(make, part, r0, rx, ry, sems)
    hidden = tok[...].reshape(-1, D).astype(F32) + summed
    hidden_o[...] = hidden
    hat, _ = norm_stats(hidden)
    low_o[t, c] = (hat * gains[1:2, :]).astype(BF).reshape(2, half, D)
    plane_gather(low_o, sems, REDUCE_SEMS)


def mlp_kernel(activated, w_down, hidden, out_o, part, r0, rx, ry, sems):
    f, c, t = here()
    greet([(f, c ^ 1, t), (f, c ^ 2, t), (f, c, 1 - t)])
    half = part.shape[3]

    def make(m, span):
        part[m, span] = nt(activated[m, span], w_down[...]).astype(BF).reshape(2, half, D)

    summed = plane_reduce(make, part, r0, rx, ry, sems)
    out_o[...] = (hidden[...] + summed).astype(BF).reshape(out_o.shape)


def mid2_kernel(
    gate_grad, w_in, hidden, cot, gains, hg_o, gain_o, low_o, part, r0, rx, ry, sems
):
    f, c, t = here()
    greet([(f, c ^ 1, t), (f, c ^ 2, t), (f, c, 1 - t)])
    half = part.shape[3]

    def make(m, span):
        part[m, span] = nt(gate_grad[m, span], w_in[...]).astype(BF).reshape(2, half, D)

    grad = plane_reduce(make, part, r0, rx, ry, sems)
    hat, inv = norm_stats(hidden[...])
    gain_o[...] = jnp.broadcast_to(jnp.sum(grad * hat, axis=0, keepdims=True), gain_o.shape)
    hg = cot[...].reshape(-1, D).astype(F32) + norm_back(grad, hat, inv, gains[1:2, :])
    hg_o[...] = hg
    low_o[t, c] = hg.astype(BF).reshape(2, half, D)
    plane_gather(low_o, sems, REDUCE_SEMS)


def end_kernel(
    n_f, joined, w_qkv, tok, hg, gains, gain2, out_rows,
    out_o, grad_o, gain_o, grad_rows, part, r0, rx, ry, gz, gp, gt, sems,
):
    f, c, t = here()
    plane = [(f, c ^ 1, t), (f, c ^ 2, t), (f, c ^ 3, t)]
    zs = [(lax.rem(f + k, n_f), c, t) for k in range(1, n_f)]
    po = (f, c, 1 - t)
    greet(plane + zs + [po])
    n_z = n_f - 1
    half = part.shape[3]
    outs = [remote(out_rows.at[zs[k][0]], out_o.at[f], sems, k, zs[k]) for k in range(n_z)]
    for s in outs:
        s.start()
    base = n_z
    out_o[f] = out_rows[f]

    def make(m, span):
        part[m, span] = nt(joined[m, span], w_qkv[...]).astype(BF).reshape(2, half, D)

    grad = plane_reduce(make, part, r0, rx, ry, sems, base)
    base += REDUCE_SEMS
    hat, inv = norm_stats(tok[...].reshape(-1, D).astype(F32))
    gain1 = jnp.sum(grad * hat, axis=0, keepdims=True)
    rows = hg[...] + norm_back(grad, hat, inv, gains[0:1, :])
    grad_rows[...] = rows.astype(BF).reshape(grad_rows.shape)
    grads = [remote(grad_rows.at[zs[k][0]], grad_o.at[f], sems, base + k, zs[k]) for k in range(n_z)]
    for s in grads:
        s.start()
    base += n_z
    grad_o[f] = grad_rows[f]
    row = lax.broadcasted_iota(jnp.int32, gain2.shape, 0)
    gt[0] = jnp.where(row == 0, gain1, jnp.where(row == 1, gain2[...], 0.0))
    s0 = remote(gt.at[0], gt.at[1], sems, base, po)
    s0.start()
    s0.wait_recv()
    gp[c] = gt[0] + gt[1]
    base += 1
    gps = [remote(gp.at[c], gp.at[c], sems, base + k, plane[k]) for k in range(3)]
    for s in gps:
        s.start()
    for s in gps:
        s.wait_recv()
    base += 3
    gz[f] = jnp.sum(gp[...], axis=0)
    gzs = [remote(gz.at[f], gz.at[f], sems, base + k, zs[k]) for k in range(n_z)]
    for s in gzs:
        s.start()
    for s in gzs:
        s.wait_recv()
    gain_o[...] = jnp.sum(gz[...], axis=0)
    for s in outs + grads:
        s.wait_recv()
    for s in outs + grads + [s0] + gps + gzs:
        s.wait_send()


def swap_kernel(src, dst, sems):
    f, c, t = here()
    plane = [(f, c ^ 1, t), (f, c ^ 2, t), (f, c ^ 3, t)]
    greet(plane)
    cps = [remote(src.at[p[1]], dst.at[c], sems, k, p) for k, p in enumerate(plane)]
    for s in cps:
        s.start()
    dst[c] = src[c]
    for s in cps:
        s.wait_recv()
    for s in cps:
        s.wait_send()


QB = 256


def rotate(u, cos, sin, lane, sign):
    partner = jnp.where(lane % HEAD_DIM < HEAD_DIM // 2, pltpu.roll(u, 96, 1), pltpu.roll(u, 32, 1))
    return u * cos + partner * (sin * sign)


def attend_kernel(live_ref, low, w, cos, sin, q_o, k_o, v_o, mixed_o, out_o, lse_o):
    live = live_ref[pl.program_id(0)]
    rows = low.shape[1]
    joined = nn(low[0], w[...])
    lane = lax.broadcasted_iota(jnp.int32, (rows, 128), 1)
    q_o[0] = (rotate(joined[:, 0:128], cos[...], sin[...], lane, 1.0).astype(BF) * BF(0.125))
    k_o[0] = rotate(joined[:, 128:256], cos[...], sin[...], lane, 1.0).astype(BF)
    v = joined[:, 256:384]
    v_o[0] = v.astype(BF)
    v_t = v.T.astype(BF)
    head_lane = lax.broadcasted_iota(jnp.int32, (QB, 128), 1) < HEAD_DIM
    alive = lax.broadcasted_iota(jnp.int32, (rows, QB), 0) < live

    def block(b, carry):
        at = pl.ds(pl.multiple_of(b * QB, QB), QB)
        qb = q_o[0, at, :]
        for h in range(2):
            qh = jnp.where(head_lane if h == 0 else ~head_lane, qb, BF(0.0))
            s = jnp.where(alive, nt(k_o[0], qh), masked_score)
            top = jnp.max(s, axis=0, keepdims=True)
            p = jnp.exp(s - top)
            total = jnp.sum(p, axis=0, keepdims=True)
            o = nn(v_t[h * HEAD_DIM : (h + 1) * HEAD_DIM], p.astype(BF)) / total
            out_o[0, h * HEAD_DIM : (h + 1) * HEAD_DIM, at] = o
            lse_o[0, h : h + 1, at] = top + jnp.log(total)
        return carry

    lax.fori_loop(0, rows // QB, block, 0)
    mixed_o[0] = out_o[0].T.astype(BF)


def attend(live, low, w, cos, sin):
    m, rows, _ = low.shape
    one = lambda *shape: pl.BlockSpec((1,) + shape, lambda i, live: (i, 0, 0))
    whole = lambda *shape: pl.BlockSpec(shape, lambda i, live: (0, 0))
    return pl.pallas_call(
        attend_kernel,
        out_shape=[shaped((m, rows, 128), BF)] * 4
        + [shaped((m, 128, rows), F32), shaped((m, 8, rows), F32)],
        grid_spec=pltpu.PrefetchScalarGridSpec(
            num_scalar_prefetch=1,
            grid=(m,),
            in_specs=[one(rows, D), whole(D, 384), whole(rows, 128), whole(rows, 128)],
            out_specs=[one(rows, 128)] * 4 + [one(128, rows), one(8, rows)],
        ),
        compiler_params=pltpu.CompilerParams(vmem_limit_bytes=VLIMIT),
    )(live, low, w, cos, sin)


def back_kernel(
    live_ref, low, w_out, q, k, v, out, lse, cos, sin, joined_o, dk, dv, dq_t, mg, delta
):
    live = live_ref[pl.program_id(0)]
    rows = low.shape[1]
    grad = nn(low[0], w_out[...]).astype(BF)
    mg[...] = grad
    weighted = grad.astype(F32).T * out[0]
    delta[0:1, :] = jnp.sum(weighted[:HEAD_DIM], axis=0, keepdims=True)
    delta[1:2, :] = jnp.sum(weighted[HEAD_DIM:], axis=0, keepdims=True)
    k_t = k[0].astype(F32).T.astype(BF)
    dk[...] = jnp.zeros_like(dk)
    dv[...] = jnp.zeros_like(dv)
    head_lane = lax.broadcasted_iota(jnp.int32, (QB, 128), 1) < HEAD_DIM
    alive = lax.broadcasted_iota(jnp.int32, (rows, QB), 0) < live

    def block(b, carry):
        at = pl.ds(pl.multiple_of(b * QB, QB), QB)
        qb = q[0, at, :]
        gb = mg[at, :]
        for h in range(2):
            keep = head_lane if h == 0 else ~head_lane
            qh = jnp.where(keep, qb, BF(0.0))
            gh = jnp.where(keep, gb, BF(0.0))
            s = nt(k[0], qh)
            p = jnp.where(alive, jnp.exp(s - lse[0, h : h + 1, at]), 0.0)
            dp = nt(v[0], gh)
            ds = (p * (dp - delta[h : h + 1, at])).astype(BF)
            dv[...] += nn(p.astype(BF), gh)
            dk[...] += nn(ds, qh)
            dq_t[h * HEAD_DIM : (h + 1) * HEAD_DIM, at] = nn(
                k_t[h * HEAD_DIM : (h + 1) * HEAD_DIM], ds
            )
        return carry

    lax.fori_loop(0, rows // QB, block, 0)
    lane = lax.broadcasted_iota(jnp.int32, (rows, 128), 1)
    dq = dq_t[...].T * 0.125
    joined_o[0, :, 0:128] = rotate(dq, cos[...], sin[...], lane, -1.0).astype(BF)
    joined_o[0, :, 128:256] = rotate(dk[...], cos[...], sin[...], lane, -1.0).astype(BF)
    joined_o[0, :, 256:384] = dv[...].astype(BF)


def attend_back(live, low, w_out, q, k, v, out, lse, cos, sin):
    m, rows, _ = low.shape
    one = lambda *shape: pl.BlockSpec((1,) + shape, lambda i, live: (i, 0, 0))
    whole = lambda *shape: pl.BlockSpec(shape, lambda i, live: (0, 0))
    return pl.pallas_call(
        back_kernel,
        out_shape=shaped((m, rows, 384), BF),
        grid_spec=pltpu.PrefetchScalarGridSpec(
            num_scalar_prefetch=1,
            grid=(m,),
            in_specs=[one(rows, D), whole(D, 128), one(rows, 128), one(rows, 128), one(rows, 128),
                      one(128, rows), one(8, rows), whole(rows, 128), whole(rows, 128)],
            out_specs=one(rows, 384),
            scratch_shapes=[
                pltpu.VMEM((rows, 128), F32),
                pltpu.VMEM((rows, 128), F32),
                pltpu.VMEM((128, rows), F32),
                pltpu.VMEM((rows, 128), BF),
                pltpu.VMEM((8, rows), F32),
            ],
        ),
        compiler_params=pltpu.CompilerParams(vmem_limit_bytes=VLIMIT),
    )(live, low, w_out, q, k, v, out, lse, cos, sin)


def rope_tables(rows):
    lane = jnp.arange(128, dtype=jnp.int32)
    exponent = (2 * (lane % (HEAD_DIM // 2))).astype(F32)
    inverse = rope_base ** (-exponent / HEAD_DIM)
    angles = jnp.arange(rows, dtype=jnp.int32).astype(F32)[:, None] * inverse[None, :]
    sign = jnp.where(lane % HEAD_DIM < HEAD_DIM // 2, -1.0, 1.0)
    return jnp.cos(angles), jnp.sin(angles) * sign[None, :]


def per_device(n_f, n_c, n_t, tokens, cotangent, lengths, owners,
               norm_attn, norm_mlp, w_qkv, w_out, w_in, w_down):
    f, c, t = here()
    micro, seqs, _, piece, _ = tokens.shape
    assert n_c == 4 and n_t == 2 and micro == 2 and seqs == n_f
    span = piece * n_f
    half = span // 2
    rows = span * n_c
    total = micro * rows
    wr = w_qkv.shape[0]
    hid = w_in.shape[2] // n_c
    hp = -(-hid // 128) * 128
    heads = w_qkv.shape[2] // n_c

    inverse_order = jnp.argsort(owners, axis=1).astype(jnp.int32)
    my_order = lax.dynamic_index_in_dim(inverse_order, t, axis=0, keepdims=False)
    sent_tok = lax.dynamic_index_in_dim(tokens, t, 0, keepdims=False)[:, 0][my_order]
    sent_cot = lax.dynamic_index_in_dim(cotangent, t, 0, keepdims=False)[:, 0][my_order]
    live = lax.dynamic_index_in_dim(lengths, f, axis=1, keepdims=False)

    place = (f * n_c + c) * wr
    gains_own = jnp.stack([norm_attn, norm_mlp]).astype(F32)
    gains_row = lax.dynamic_update_slice(jnp.zeros((8, D), F32), gains_own, (0, place))

    def quarters(a):
        return a.transpose(2, 0, 1, 3).reshape(n_c, wr, -1)

    pad = [(0, 0)] * 3 + [(0, hp - hid)]
    p_qkv = quarters(w_qkv.reshape(wr, 3, n_c, heads))
    p_out = w_out.reshape(n_c, heads, wr).transpose(0, 2, 1)
    p1 = jnp.concatenate([p_qkv, p_out], axis=2)
    p2 = quarters(jnp.pad(w_in.reshape(wr, 2, n_c, hid), pad))
    p3 = jnp.pad(w_down.reshape(n_c, hid, wr).transpose(0, 2, 1), pad[1:])
    n1, n2, n3 = p1.shape[2], p2.shape[2], p3.shape[2]

    full_shape = (micro, n_c, 2, half, D)
    tok, cot, gains, q1, q2, q3, first_low = comm_call(
        functools.partial(start_kernel, n_f),
        [
            shaped((n_f, piece, D), BF), shaped((n_f, piece, D), BF), shaped((8, D), F32),
            shaped((n_c, wr, n1), BF), shaped((n_c, wr, n2), BF), shaped((n_c, wr, n3), BF),
            shaped(full_shape, BF),
        ],
        [pltpu.VMEM((n_f, 8, D), F32), pltpu.VMEM((n_c, 8, D), F32)],
        3 * (n_f - 1) + 12 + GATHER_SEMS, 0, 6,
    )(sent_tok, sent_cot, gains_row, p1, p2, p3)
    W1, W2, W3 = (
        lax.all_gather(q, "fsdp", axis=0, tiled=True).reshape(D, -1) for q in (q1, q2, q3)
    )
    wq, wo = W1[:, : 3 * heads], W1[:, 3 * heads :]
    cos, sin = rope_tables(rows)

    low3 = first_low.reshape(micro, rows, D)
    q, k, v, mixed, out_t, lse = attend(live, low3, wq, cos, sin)
    hidden, second_low = comm_call(
        mid1_kernel,
        [shaped((span, D), F32), shaped(full_shape, BF)],
        reduce_scratch(half), REDUCE_SEMS + GATHER_SEMS, 1, 4,
    )(mixed.reshape(micro, n_c, span, 128), wo, tok, gains)

    cot_full = lax.all_gather(
        lax.all_gather(cot.reshape(span, D), "ctx", axis=0, tiled=True), "tp", axis=0, tiled=True
    )
    flat = second_low.reshape(total, D)
    gate_up = nn(flat, W2)
    u, g = gate_up[:, :hp], gate_up[:, hp:]
    gelu, gelu_back = jax.vjp(lambda a: jax.nn.gelu(a, approximate=False), u)
    activated = (gelu * g).astype(BF)
    act_grad = nn(cot_full, W3)
    gate_grad = jnp.concatenate(
        [gelu_back(act_grad * g)[0], act_grad * gelu], axis=1
    ).astype(BF)
    hg, gain2, attn_low = comm_call(
        mid2_kernel,
        [shaped((span, D), F32), shaped((8, D), F32), shaped(full_shape, BF)],
        reduce_scratch(half), REDUCE_SEMS + GATHER_SEMS, 2, 5,
    )(gate_grad.reshape(micro, n_c, span, 2 * hp), W2, hidden, cot, gains)
    g_down = tn(cot_full, activated)
    g_in = tn(flat, gate_grad)
    early = jnp.concatenate([g_in, g_down], axis=1).astype(BF)
    early = lax.psum_scatter(early, "fsdp", scatter_dimension=0, tiled=True)

    out_rows = comm_call(
        mlp_kernel, shaped((n_f, piece, D), BF), reduce_scratch(half), REDUCE_SEMS, 3, 3
    )(activated.reshape(micro, n_c, span, hp), W3, hidden)

    attn_flat = attn_low.reshape(total, D)
    joined = attend_back(
        live, attn_low.reshape(micro, rows, D), wo, q, k, v, out_t, lse, cos, sin
    )
    g_out = tn(attn_flat, mixed.reshape(total, 128))
    g_qkv = tn(low3.reshape(total, D), joined.reshape(total, 384))
    late = jnp.concatenate([g_qkv, g_out], axis=1).astype(BF)
    late = lax.psum_scatter(late, "fsdp", scatter_dimension=0, tiled=True)

    outs, grads, gain_grads = comm_call(
        functools.partial(end_kernel, n_f),
        [shaped((n_f, piece, D), BF), shaped((n_f, piece, D), BF), shaped((8, D), F32)],
        [pltpu.VMEM((n_f, piece, D), BF)]
        + reduce_scratch(half)
        + [pltpu.VMEM((n_f, 8, D), F32), pltpu.VMEM((n_c, 8, D), F32), pltpu.VMEM((2, 8, D), F32)],
        3 * (n_f - 1) + REDUCE_SEMS + 4, 4, 7,
    )(joined.reshape(micro, n_c, span, 384), wq, tok, hg, gains, gain2, out_rows)

    shares = jnp.concatenate([late, early], axis=1).reshape(n_c, wr, -1)
    shares = comm_call(swap_kernel, shaped(shares.shape, BF), [], 3, 5, 1)(shares).astype(F32)
    grad_qkv = shares[:, :, : 3 * heads].reshape(n_c, wr, 3, heads).transpose(1, 2, 0, 3)
    grad_qkv = grad_qkv.reshape(wr, 3, n_c * heads)
    grad_out = shares[:, :, 3 * heads : n1].transpose(0, 2, 1).reshape(n_c * heads, wr)
    grad_in = shares[:, :, n1 : n1 + n2].reshape(n_c, wr, 2, hp)[..., :hid]
    grad_in = grad_in.transpose(1, 2, 0, 3).reshape(wr, 2, n_c * hid)
    grad_down = shares[:, :, n1 + n2 : n1 + n2 + hid].transpose(0, 2, 1).reshape(n_c * hid, wr)

    both_o = lax.all_gather(outs, "tp", axis=0, tiled=False)
    both_g = lax.all_gather(grads, "tp", axis=0, tiled=False)
    index = jnp.arange(micro, dtype=jnp.int32)[:, None]
    output = both_o[index, owners][:, :, None]
    grad_tokens = both_g[index, owners][:, :, None]
    mine = lax.dynamic_slice(gain_grads, (0, place), (2, wr))
    return (output, grad_tokens, mine[0], mine[1], grad_qkv, grad_out, grad_in, grad_down)


def solution(mesh):
    rows = P(None, None, "ctx", "fsdp", None)
    gain = P(("fsdp", "ctx"))
    tall = P(("fsdp", "ctx"), None, "tp")
    wide = P("tp", ("fsdp", "ctx"))
    return jax.shard_map(
        functools.partial(per_device, mesh.shape["fsdp"], mesh.shape["ctx"], mesh.shape["tp"]),
        mesh=mesh,
        in_specs=(rows, rows, P(), P(), gain, gain, tall, wide, tall, wide),
        out_specs=(rows, rows, gain, gain, tall, wide, tall, wide),
        check_vma=False,
    )
```

```python
import functools

import jax
import jax.numpy as jnp
from jax import lax
from jax.experimental import pallas as pl
from jax.experimental.pallas import tpu as pltpu
from jax.sharding import PartitionSpec as P

D = 1024
HEAD_DIM = 64
norm_eps = 1e-05
rope_base = 160000.0
masked_score = -1e30
MESH = pl.DeviceIdType.MESH
BF = jnp.bfloat16
F32 = jnp.float32
VLIMIT = 56 << 20


def nn(a, b):
    return lax.dot_general(a, b, (((1,), (0,)), ((), ())), preferred_element_type=F32)


def nt(a, b):
    return lax.dot_general(a, b, (((1,), (1,)), ((), ())), preferred_element_type=F32)


def tn(a, b):
    return lax.dot_general(a, b, (((0,), (0,)), ((), ())), preferred_element_type=F32)


def norm_stats(values):
    center = values - jnp.mean(values, axis=-1, keepdims=True)
    spread = jnp.mean(center * center, axis=-1, keepdims=True)
    inverse_std = lax.rsqrt(spread + norm_eps)
    return center * inverse_std, inverse_std


def norm_back(upstream, normed, inverse_std, gain):
    scaled = upstream * gain
    adjusted = (
        scaled
        - jnp.mean(scaled, axis=-1, keepdims=True)
        - normed * jnp.mean(scaled * normed, axis=-1, keepdims=True)
    )
    return adjusted * inverse_std


def here():
    return lax.axis_index("fsdp"), lax.axis_index("ctx"), lax.axis_index("tp")


def remote(src, dst, sems, i, where, j=None):
    return pltpu.make_async_remote_copy(
        src_ref=src,
        dst_ref=dst,
        send_sem=sems.at[0, i],
        recv_sem=sems.at[1, i if j is None else j],
        device_id=where,
        device_id_type=MESH,
    )


def greet(peers):
    bar = pltpu.get_barrier_semaphore()
    for p in peers:
        pl.semaphore_signal(bar, inc=1, device_id=p, device_id_type=MESH)
    pl.semaphore_wait(bar, len(peers))


class Ids:
    def __init__(self):
        self.next = 0

    def take(self, count):
        self.next += count
        return self.next - count


def each(copies, what):
    for copy in copies:
        getattr(copy, what)()


class Gather:
    def __init__(self, full, m, sems, ids):
        f, c, t = here()
        px, py, po = (f, c ^ 1, t), (f, c ^ 2, t), (f, c, 1 - t)
        cx, cy, cd = c ^ 1, c ^ 2, c ^ 3
        base = ids.take(10)

        def cp(i, view, where):
            return remote(view, view, sems, base + i, where)

        self.bx = cp(0, full.at[m, c, t, 1], px)
        self.ay = cp(1, full.at[m, c, t, 0], py)
        self.ax = cp(2, full.at[m, c, t, 0], px)
        self.by = cp(3, full.at[m, c, t, 1], py)
        self.oo = cp(4, full.at[m, c, t], po)
        self.fy = cp(5, full.at[m, cx, t, 1], py)
        self.fx = cp(6, full.at[m, cy, t, 0], px)
        self.ox = cp(7, full.at[m, cx, t], po)
        self.oy = cp(8, full.at[m, cy, t], po)
        self.od = cp(9, full.at[m, cd, t], po)

    def s0(self):
        each([self.bx, self.ay, self.ax, self.by, self.oo], "start")

    def s1(self):
        self.bx.wait_recv()
        self.fy.start()
        self.ay.wait_recv()
        self.fx.start()

    def s2(self):
        self.ax.wait_recv()
        self.ox.start()
        self.by.wait_recv()
        self.oy.start()

    def s3(self):
        self.fy.wait_recv()
        self.fx.wait_recv()
        self.od.start()

    def s4(self):
        each([self.oo, self.ox, self.oy, self.od], "wait_recv")

    def rest(self):
        self.s2()
        self.s3()
        self.s4()

    def end(self):
        each(
            [self.bx, self.ay, self.ax, self.by, self.oo, self.fy, self.fx, self.ox, self.oy,
             self.od],
            "wait_send",
        )


class Reduce:
    def __init__(self, part, r0, rx, ry, sems, ids):
        f, c, t = here()
        px, py, self.po = (f, c ^ 1, t), (f, c ^ 2, t), (f, c, 1 - t)
        cx, cy, cd = c ^ 1, c ^ 2, c ^ 3
        self.base = ids.take(10)
        self.part, self.r0, self.rx, self.ry, self.sems = part, r0, rx, ry, sems
        self.own, self.t, self.cx, self.cy, self.cd = c, t, cx, cy, cd

        def cp(i, src, dst, where):
            return remote(src, dst, sems, self.base + i, where)

        self.cross = [self.crossing(i) for i in range(4)]
        self.a0 = cp(4, part.at[cd, t, 0], rx.at[0], px)
        self.b0 = cp(5, part.at[cd, t, 1], ry.at[0], py)
        self.a1 = cp(6, part.at[cx, t, 0], rx.at[1], px)
        self.b1 = cp(7, part.at[cy, t, 1], ry.at[1], py)
        self.b2 = cp(8, part.at[cy, t, 0], ry.at[2], py)
        self.a2 = cp(9, part.at[cx, t, 1], rx.at[2], px)

    def span(self, i):
        return self.own ^ (3 - i - jnp.where(jnp.int32(i) == 1, 1, 0) + jnp.where(jnp.int32(i) == 2, 1, 0))

    def crossing(self, i):
        return remote(
            self.part.at[self.span(i), 1 - self.t], self.r0.at[i], self.sems, self.base + i, self.po
        )

    def add(self, i, span):
        self.cross[i].wait_recv()
        part, t = self.part, self.t
        part[span, t] = (part[span, t].astype(F32) + self.r0[i].astype(F32)).astype(BF)

    def s1(self):
        self.add(0, self.cd)
        self.a0.start()
        self.b0.start()

    def s2(self):
        self.add(1, self.cx)
        self.a1.start()
        self.add(2, self.cy)
        self.b1.start()

    def s3(self):
        part, t = self.part, self.t
        self.a0.wait_recv()
        part[self.cy, t, 0] = (part[self.cy, t, 0].astype(F32) + self.rx[0].astype(F32)).astype(BF)
        self.b2.start()
        self.b0.wait_recv()
        part[self.cx, t, 1] = (part[self.cx, t, 1].astype(F32) + self.ry[0].astype(F32)).astype(BF)
        self.a2.start()

    def s4(self):
        self.cross[3].wait_recv()
        own = self.part[self.own, self.t].astype(F32) + self.r0[3].astype(F32)
        each([self.a1, self.b1, self.b2, self.a2], "wait_recv")
        top = own[0] + self.rx[1].astype(F32) + self.ry[2].astype(F32)
        bottom = own[1] + self.ry[1].astype(F32) + self.rx[2].astype(F32)
        return jnp.concatenate([top, bottom], axis=0)

    def end(self):
        each(self.cross + [self.a0, self.b0, self.a1, self.b1, self.b2, self.a2], "wait_send")


def reduce_scratch(half):
    return [
        pltpu.VMEM((2, 4, 2, 2, half, D), BF),
        pltpu.VMEM((2, 4, 2, half, D), BF),
        pltpu.VMEM((2, 3, half, D), BF),
        pltpu.VMEM((2, 3, half, D), BF),
    ]


class Spread:
    def __init__(self, ref, n_f, sems, ids):
        f, c, t = here()
        self.f, self.n_f, self.ref = f, n_f, ref
        if n_f == 4:
            base = ids.take(5)
            self.steps = (-1, -2, 1, 2)
            self.copies = [
                remote(ref.at[f], ref.at[f], sems, base + i, (lax.rem(f - d + n_f, n_f), c, t))
                for i, d in enumerate(self.steps)
            ]
            self.far = remote(
                ref.at[jnp.where(f == 2, 0, 3)], ref.at[jnp.where(f == 2, 0, 3)], sems, base + 4,
                (jnp.where(f == 2, 3, 0), c, t),
            )
        else:
            base = ids.take(1)
            self.copies = [
                remote(ref.at[f], ref.at[f], sems, base, (lax.rem(f + k, n_f), c, t))
                for k in range(1, n_f)
            ]
            most = ref.at[pl.ds(0, n_f - 1)]
            self.all = remote(most, most, sems, base, (f, c, 1 - t))

    def start(self):
        if self.n_f != 4:
            return each(self.copies, "start")
        for d, cp in zip(self.steps, self.copies):
            pl.when((self.f - d >= 0) & (self.f - d < 4))(cp.start)

    def relay(self):
        if self.n_f != 4:
            return

        @pl.when(self.f == 2)
        def _():
            self.copies[1].wait_recv()
            self.far.start()

        @pl.when(self.f == 1)
        def _():
            self.copies[3].wait_recv()
            self.far.start()

    def wait(self):
        if self.n_f != 4:
            return self.all.wait_recv()
        f = self.f
        pl.when(f >= 1)(self.copies[0].wait_recv)
        pl.when(f == 3)(self.copies[1].wait_recv)
        pl.when(f <= 2)(self.copies[2].wait_recv)
        pl.when(f == 0)(self.copies[3].wait_recv)
        pl.when((f == 0) | (f == 3))(self.far.wait_recv)

    def end(self):
        if self.n_f != 4:
            return self.all.wait_send()
        for d, cp in zip(self.steps, self.copies):
            pl.when((self.f - d >= 0) & (self.f - d < 4))(cp.wait_send)
        pl.when((self.f == 1) | (self.f == 2))(self.far.wait_send)


class Collect:
    def __init__(self, ref, got, n_f, sems, ids):
        f, c, t = here()
        self.f, self.n_f, self.ref, self.got = f, n_f, ref, got
        if n_f == 4:
            base = ids.take(5)
            self.steps = (-1, -2, 1, 2)
            self.copies = []
            for i, d in enumerate(self.steps):
                j = lax.rem(f - d + n_f, n_f)
                self.copies.append(remote(ref.at[j], got.at[i], sems, base + i, (j, c, t)))
            away = jnp.where(f == 0, 3, 0)
            self.far = remote(
                ref.at[away], got.at[4], sems, base + 4, (jnp.where(f == 0, 1, 2), c, t)
            )
        else:
            base = ids.take(1)
            self.copies = []
            for k in range(1, n_f):
                j = lax.rem(f + k, n_f)
                self.copies.append(remote(ref.at[j], got.at[k - 1], sems, base, (j, c, t)))
            most = ref.at[pl.ds(0, n_f - 1)]
            self.all = remote(most, got, sems, base, (f, c, 1 - t))

    def there(self, d):
        return (self.f - d >= 0) & (self.f - d < 4)

    def late(self, d):
        if d == 2:
            return self.f == 2
        if d == -2:
            return self.f == 1
        return self.f < 0

    def start(self):
        if self.n_f != 4:
            return each(self.copies, "start")
        pl.when((self.f == 0) | (self.f == 3))(self.far.start)
        for d, cp in zip(self.steps, self.copies):
            pl.when(self.there(d) & ~self.late(d))(cp.start)

    def relay(self):
        if self.n_f != 4:
            return
        for d, cp, j in ((2, self.copies[3], 0), (-2, self.copies[1], 3)):

            @pl.when(self.late(d))
            def _():
                self.far.wait_recv()
                self.ref[j] = (self.ref[j].astype(F32) + self.got[4].astype(F32)).astype(BF)
                cp.start()

    def total(self, acc):
        acc[...] = self.ref[self.f].astype(F32)
        if self.n_f != 4:
            self.all.wait_recv()
            for k in range(self.n_f - 1):
                acc[...] += self.got[k].astype(F32)
            return
        for i, d in enumerate(self.steps):

            @pl.when((self.f + d >= 0) & (self.f + d < 4))
            def _():
                self.copies[i].wait_recv()
                acc[...] += self.got[i].astype(F32)

    def end(self):
        if self.n_f != 4:
            return self.all.wait_send()
        for d, cp in zip(self.steps, self.copies):
            pl.when(self.there(d))(cp.wait_send)
        pl.when((self.f == 0) | (self.f == 3))(self.far.wait_send)


def collect_slots(n_f):
    return 5 if n_f == 4 else n_f - 1


class Deal:
    def __init__(self, stage, own, n_f, sems, ids):
        f, c, t = here()
        n_h = n_f // 2
        self.base = ids.take(2 * n_f)
        self.f, self.t, self.n_h, self.own, self.sems = f, t, n_h, own, sems
        side, at = f // n_h, lax.rem(f, n_h)
        recv = self.base + t * n_h + at
        self.away = [
            remote(stage.at[lax.rem(f + k, n_f)], own.at[t, at], sems, self.base + k,
                   (lax.rem(f + k, n_f), c, side), recv)
            for k in range(1, n_f)
        ]
        self.over = remote(stage.at[f], own.at[t, at], sems, self.base, (f, c, 1 - t), recv)
        self.keep = pltpu.make_async_copy(stage.at[f], own.at[t, at], sems.at[1, recv])
        self.mine = side == t

    def start(self):
        each(self.away, "start")
        pl.when(self.mine)(self.keep.start)
        pl.when(~self.mine)(self.over.start)

    def wait(self, m):
        for j in range(self.n_h):
            i = self.base + m * self.n_h + j
            view = self.own.at[m, j]
            local = (self.t == m) & (self.f == self.t * self.n_h + j)
            f, c, t = here()
            pl.when(local)(pltpu.make_async_copy(view, view, self.sems.at[1, i]).wait)
            pl.when(~local)(remote(view, view, self.sems, i, (f, c, 1 - t)).wait_recv)

    def end(self):
        each(self.away, "wait_send")
        pl.when(~self.mine)(self.over.wait_send)


class Return:
    def __init__(self, own, back, other, n_f, sems, ids):
        f, c, t = here()
        n_h = n_f // 2
        self.base = ids.take(2 * n_f + 1)
        self.f, self.t, self.n_f, self.back, self.sems = f, t, n_f, back, sems
        self.moves = []
        for m in range(2):
            for j in range(n_h):
                to = t * n_h + j
                i = self.base + m * n_h + j
                far = remote(own.at[m, j], back.at[f], sems, i, (to, c, m), self.base + f)
                keep = pltpu.make_async_copy(own.at[m, j], back.at[f], sems.at[1, self.base + f])
                self.moves.append((m, (to == f) & (t == m), far, keep))
        self.swap = remote(back, other, sems, self.base + 2 * n_f, (f, c, 1 - t))

    def start(self, m):
        for which, local, far, keep in self.moves:
            if which == m:
                pl.when(local)(keep.start)
                pl.when(~local)(far.start)

    def wait(self):
        n_h = self.n_f // 2
        f, c, t = here()
        for s in range(self.n_f):
            local = (f == s) & (f // n_h == t)
            view = self.back.at[s]
            i = self.base + s
            pl.when(local)(pltpu.make_async_copy(view, view, self.sems.at[1, i]).wait)
            pl.when(~local)(remote(view, view, self.sems, i, (f, c, 1 - t)).wait_recv)
        self.swap.start()

    def end(self):
        self.swap.wait_recv()
        for _, local, far, _ in self.moves:
            pl.when(~local)(far.wait_send)
        self.swap.wait_send()


class Swap:
    def __init__(self, src, dst, sems, ids):
        f, c, t = here()
        base = ids.take(3)
        self.src, self.dst, self.c = src, dst, c
        self.copies = [
            remote(src.at[c ^ k], dst.at[c], sems, base + k - 1, (f, c ^ k, t)) for k in (1, 2, 3)
        ]

    def start(self):
        each(self.copies, "start")

    def keep(self):
        self.dst[self.c] = self.src[self.c]

    def wait(self):
        each(self.copies, "wait_recv")

    def end(self):
        each(self.copies, "wait_send")


def everyone(n_f):
    f, c, t = here()
    peers = [(f, c ^ 1, t), (f, c ^ 2, t), (f, c ^ 3, t), (f, c, 1 - t)]
    for k in range(1, n_f):
        for core in range(2):
            peers.append((lax.rem(f + k, n_f), c, core))
    return peers


def vm():
    return pl.BlockSpec(memory_space=pltpu.VMEM)


def sm():
    return pl.BlockSpec(memory_space=pltpu.SMEM)


def hb():
    return pl.BlockSpec(memory_space=pl.ANY)


def shaped(shape, dtype):
    return jax.ShapeDtypeStruct(shape, dtype)


def comm_call(kernel, outs, ins, scratch, n_sems, n_local, cid, flops):
    return pl.pallas_call(
        kernel,
        out_shape=[s for s, _ in outs],
        in_specs=ins,
        out_specs=[b for _, b in outs],
        scratch_shapes=scratch
        + [pltpu.SemaphoreType.DMA((2, n_sems)), pltpu.SemaphoreType.DMA((n_local,))],
        compiler_params=pltpu.CompilerParams(
            collective_id=cid, has_side_effects=True, vmem_limit_bytes=VLIMIT
        ),
        cost_estimate=pl.CostEstimate(flops=flops, bytes_accessed=1 << 20, transcendentals=0),
    )


def rotate(u, cos, sin, sign):
    lane = lax.broadcasted_iota(jnp.int32, u.shape, 1)
    partner = jnp.where(lane % HEAD_DIM < HEAD_DIM // 2, pltpu.roll(u, 96, 1), pltpu.roll(u, 32, 1))
    return u * cos + partner * (sin * sign)


def first_kernel(
    n_f, order, live, tok, cot, gains, pq, po, p2, p3, cos, sin,
    tok_o, cot_o, gains_o, wq, wo, w2, q3, first_h, cot_h, q_o, k_o, v_o, mixed_o, out_o, lse_o,
    hidden_o, second_o,
    stok, scot, gz, gp, first, cotf, part, r0, rx, ry, v_t, sems, lsem,
):
    f, c, t = here()
    ids = Ids()
    plane = [(f, c ^ k, t) for k in (1, 2, 3)]
    zs = [(lax.rem(f + k, n_f), c, t) for k in range(1, n_f)]
    half = first.shape[4]
    rows = 4 * 2 * 2 * half

    deal_tok = Deal(stok, tok_o, n_f, sems, ids)
    deal_cot = Deal(scot, cot_o, n_f, sems, ids)
    base = ids.take(n_f - 1)
    gs = [remote(gains, gz.at[f], sems, base + k, zs[k]) for k in range(n_f - 1)]
    base = ids.take(3)
    gps = [remote(gp.at[c], gp.at[c], sems, base + k, plane[k]) for k in range(3)]
    swaps = [Swap(src, dst, sems, ids)
             for src, dst in ((pq, wq.at[f]), (po, wo.at[f]), (p2, w2.at[f]), (p3, q3))]
    spreads = [Spread(w, n_f, sems, ids) for w in (wq, wo, w2)]
    g1 = [Gather(first, m, sems, ids) for m in range(2)]
    gc = [Gather(cotf, m, sems, ids) for m in range(2)]
    red = [Reduce(part.at[m], r0.at[m], rx.at[m], ry.at[m], sems, ids) for m in range(2)]
    local = [pltpu.make_async_copy(first, first_h, lsem.at[0]),
             pltpu.make_async_copy(cotf, cot_h, lsem.at[1])]

    for j in range(n_f):
        stok[j] = tok[t, order[t, j]]
    greet(everyone(n_f))
    each(gs, "start")
    deal_tok.start()
    each(swaps, "start")
    each(swaps, "keep")
    for j in range(n_f):
        scot[j] = cot[t, order[t, j]]
    gz[f] = gains[...]
    each(gs, "wait_recv")
    gp[c] = jnp.sum(gz[...], axis=0)
    each(gps, "start")
    swaps[0].wait()
    spreads[0].start()
    each(gps, "wait_recv")
    gains_o[...] = jnp.sum(gp[...], axis=0)

    def norm1(m):
        deal_tok.wait(m)
        hat, _ = norm_stats(tok_o[m].reshape(-1, D).astype(F32))
        first[m, c, t] = (hat * gains_o[0:1, :]).astype(BF).reshape(2, half, D)

    norm1(0)
    g1[0].s0()
    norm1(1)
    spreads[0].relay()
    g1[0].s1()
    g1[1].s0()
    swaps[1].wait()
    spreads[1].start()
    deal_cot.start()
    g1[0].s2()
    g1[0].s3()
    swaps[2].wait()
    spreads[2].start()
    g1[0].s4()
    spreads[0].wait()

    def attend(m, hooks):
        joined = nn(first[m].reshape(rows, D), wq[...].reshape(D, -1))
        q_o[m] = rotate(joined[:, 0:128], cos[...], sin[...], 1.0).astype(BF) * BF(0.125)
        k_o[m] = rotate(joined[:, 128:256], cos[...], sin[...], 1.0).astype(BF)
        v = joined[:, 256:384]
        v_o[m] = v.astype(BF)
        v_t[...] = v.T.astype(BF)
        lane = lax.broadcasted_iota(jnp.int32, (rows, 128), 1)
        alive = lax.broadcasted_iota(jnp.int32, (rows, rows), 0) < live[m]

        def head(h, carry):
            at = pl.ds(pl.multiple_of(h * HEAD_DIM, HEAD_DIM), HEAD_DIM)
            qh = jnp.where(lane // HEAD_DIM == h, q_o[m], BF(0.0))
            s = jnp.where(alive, nt(k_o[m], qh), masked_score)
            top = jnp.max(s, axis=0, keepdims=True)
            p = jnp.exp(s - top)
            total = jnp.sum(p, axis=0, keepdims=True)
            out_o[m, at, :] = nn(v_t[at, :], p.astype(BF)) / total
            lse_o[m, pl.ds(h, 1), :] = top + jnp.log(total)
            for i, hook in enumerate(hooks):
                pl.when(h == i)(hook)
            return carry

        lax.fori_loop(0, 2, head, 0)
        mixed_o[m] = out_o[m].T.astype(BF)

    def product(m):
        def step(i, carry):
            span = red[m].span(i)
            block = mixed_o[m, pl.ds(pl.multiple_of(span * 4 * half, 4 * half), 4 * half), :]
            part[m, span] = nt(block, wo[...].reshape(D, -1)).astype(BF).reshape(2, 2, half, D)
            red[m].crossing(i).start()
            return carry

        lax.fori_loop(0, 4, step, 0)

    def norm2(m):
        hidden = tok_o[m].reshape(-1, D).astype(F32) + red[m].s4()
        hidden_o[m] = hidden
        hat, _ = norm_stats(hidden)
        second_o[m] = (hat * gains_o[1:2, :]).astype(BF).reshape(2, half, D)

    g1[1].s1()

    def hook0():
        g1[1].s2()
        spreads[1].relay()

    attend(0, (hook0, g1[1].s3))
    g1[1].s4()
    local[0].start()
    spreads[1].wait()
    product(0)
    red[0].s1()
    deal_cot.wait(0)
    deal_cot.wait(1)
    for m in range(2):
        cotf[m, c, t] = cot_o[m].reshape(2, half, D)
    red[0].s2()

    def hook1():
        red[0].s3()
        gc[0].s0()

    def hook2():
        spreads[2].relay()

    attend(1, (hook1, hook2))
    product(1)
    red[1].s1()
    red[1].s2()
    norm2(0)
    red[1].s3()
    gc[0].s1()
    gc[1].s0()
    gc[0].s2()
    gc[0].s3()
    norm2(1)
    gc[1].s1()
    gc[1].rest()
    gc[0].s4()
    local[1].start()
    swaps[3].wait()
    spreads[2].wait()
    each(gs + gps, "wait_send")
    for x in [deal_tok, deal_cot] + swaps + spreads + g1 + gc + red:
        x.end()
    each(local, "wait")


def second_kernel(
    n_f, second, w2, q3, cot_h, cot_own, hidden, gains,
    hg_o, attn_o, act_o, gain_o, w3, gi_o, gd_o,
    full, cotf, gg, gd, got, acc, part, r0, rx, ry, sems, lsem,
):
    f, c, t = here()
    ids = Ids()
    half = full.shape[4]
    hp = w3.shape[3]
    rows = 16 * half
    g2 = [Gather(full, m, sems, ids) for m in range(2)]
    red = [Reduce(part.at[m], r0.at[m], rx.at[m], ry.at[m], sems, ids) for m in range(2)]
    spread = Spread(w3, n_f, sems, ids)
    collect = Collect(gd, got, n_f, sems, ids)
    load = pltpu.make_async_copy(cot_h, cotf, lsem.at[0])
    load.start()
    w3[f] = q3[...]
    for m in range(2):
        full[m, c, t] = second[m]
    greet(everyone(n_f))
    g2[0].s0()
    spread.start()
    g2[0].s1()
    g2[1].s0()
    spread.relay()
    g2[0].rest()
    load.wait()
    spread.wait()
    g2[1].s1()

    def mlp(m, hooks):
        def step(i, carry):
            span = red[m].span(i)
            low = full[m, span].reshape(4 * half, D)
            win = w2[...].reshape(D, 2 * hp)
            u = nn(low, win[:, :hp])
            g = nn(low, win[:, hp:])
            a = nn(cotf[m, span].reshape(4 * half, D), w3[...].reshape(D, hp))
            phi = 0.5 * (1.0 + lax.erf(u * 0.7071067811865476))
            gelu = u * phi
            slope = phi + u * (jnp.exp(-0.5 * u * u) * 0.3989422804014327)
            act_o[m, span] = (gelu * g).astype(BF)
            gg[m, span, :, 0:hp] = (a * g * slope).astype(BF)
            gg[m, span, :, hp:] = (a * gelu).astype(BF)
            part[m, span] = nt(gg[m, span], win).astype(BF).reshape(2, 2, half, D)
            red[m].crossing(i).start()
            for j, hook in enumerate(hooks):
                pl.when(i == j)(hook)
            return carry

        lax.fori_loop(0, 4, step, 0)

    mlp(0, (g2[1].s2, g2[1].s3))
    red[0].s1()
    g2[1].s4()
    mlp(1, (red[0].s2, red[0].s3))
    red[1].s1()
    flat_act = act_o[...].reshape(2 * rows, hp)
    flat_gg = gg[...].reshape(2 * rows, 2 * hp)
    n_d = 256

    def down(b, carry):
        x = cotf[:, :, :, :, :, pl.ds(pl.multiple_of(b * n_d, n_d), n_d)].reshape(2 * rows, n_d)
        blk = n_d // gd.shape[1] if gd.shape[1] < n_d else 1
        gd_view = tn(x, flat_act).astype(BF)
        if gd.shape[1] == n_d:
            gd[b] = gd_view
        else:
            gd[pl.ds(b * blk, blk)] = gd_view.reshape(blk, gd.shape[1], hp)
        return carry

    lax.fori_loop(0, D // n_d, down, 0)
    collect.start()
    red[1].s2()

    def norm3(m):
        grad = red[m].s4()
        hat, inv = norm_stats(hidden[m])
        hg = cot_own[m].reshape(-1, D).astype(F32) + norm_back(grad, hat, inv, gains[1:2, :])
        hg_o[m] = hg
        attn_o[m] = hg.astype(BF).reshape(2, half, D)
        return jnp.sum(grad * hat, axis=0, keepdims=True)

    gain = norm3(0)
    red[1].s3()

    def inner(b, carry):
        x = full[:, :, :, :, :, pl.ds(pl.multiple_of(b * n_d, n_d), n_d)].reshape(2 * rows, n_d)
        gi_o[pl.ds(pl.multiple_of(b * n_d, n_d), n_d), :] = tn(x, flat_gg).astype(BF)
        return carry

    lax.fori_loop(0, D // n_d, inner, 0)
    collect.relay()
    gain = gain + norm3(1)
    gain_o[...] = jnp.broadcast_to(gain, gain_o.shape)
    collect.total(acc)
    gd_o[...] = acc[...].astype(BF)
    for x in g2 + red + [spread, collect]:
        x.end()


def third_kernel(
    n_f, owners, live, attn, wo, wq, w3, act, q, k, v, mixed, out, lse, first_h, hg, hidden, tok,
    gains, gain2, gi, gd, cos, sin,
    out_o, grad_o, gain_o, share_o,
    full, first, dk, dv, dq_t, mg, delta, k_t, joined, part, r0, rx, ry, r0b, rxb, ryb,
    gl, gotl, gotg, accl, accg, ssend, orow, grow, oback, gback, oother, gother, gz, gp, gt,
    sems, lsem,
):
    f, c, t = here()
    ids = Ids()
    half = full.shape[4]
    rows = 16 * half
    hp = w3.shape[3]
    nl, ng = accl.shape[1], accg.shape[1]
    plane = [(f, c ^ k_, t) for k_ in (1, 2, 3)]
    zs = [(lax.rem(f + k_, n_f), c, t) for k_ in range(1, n_f)]
    po = (f, c, 1 - t)
    g3 = [Gather(full, m, sems, ids) for m in range(2)]
    red4 = [Reduce(part.at[m], r0.at[m], rx.at[m], ry.at[m], sems, ids) for m in range(2)]
    red3 = [Reduce(part.at[m], r0b.at[m], rxb.at[m], ryb.at[m], sems, ids) for m in range(2)]
    collect_g = Collect(gi, gotg, n_f, sems, ids)
    collect_l = Collect(gl, gotl, n_f, sems, ids)
    ret_o = Return(orow, oback, oother, n_f, sems, ids)
    ret_g = Return(grow, gback, gother, n_f, sems, ids)
    swap = Swap(ssend, share_o, sems, ids)
    base = ids.take(1 + 3 + n_f - 1)
    s0 = remote(gt.at[0], gt.at[1], sems, base, po)
    gps = [remote(gp.at[c], gp.at[c], sems, base + 1 + j, plane[j]) for j in range(3)]
    gzs = [remote(gz.at[f], gz.at[f], sems, base + 4 + j, zs[j]) for j in range(n_f - 1)]
    load = pltpu.make_async_copy(first_h, first, lsem.at[0])
    load.start()
    for m in range(2):
        full[m, c, t] = attn[m]
    greet(everyone(n_f))
    g3[0].s0()
    collect_g.start()

    def product(red, m, source, weight):
        def step(i, carry):
            span = red[m].span(i)
            part[m, span] = nt(source(m, span), weight()).astype(BF).reshape(2, 2, half, D)
            red[m].crossing(i).start()
            return carry

        lax.fori_loop(0, 4, step, 0)

    def act_rows(m, span):
        return act[m, span]

    def joined_rows(m, span):
        return joined[m, pl.ds(pl.multiple_of(span * 4 * half, 4 * half), 4 * half), :]

    g3[0].s1()
    g3[1].s0()
    product(red4, 0, act_rows, lambda: w3[...].reshape(D, hp))
    product(red4, 1, act_rows, lambda: w3[...].reshape(D, hp))
    g3[0].rest()
    collect_g.relay()
    QB = 512

    def attend_back(m, hooks):
        grad = nn(full[m].reshape(rows, D), wo[...].reshape(D, -1)).astype(BF)
        mg[...] = grad
        weighted = grad.astype(F32).T * out[m]
        delta[0:1, :] = jnp.sum(weighted[:HEAD_DIM], axis=0, keepdims=True)
        delta[1:2, :] = jnp.sum(weighted[HEAD_DIM:], axis=0, keepdims=True)
        k_t[...] = k[m].astype(F32).T.astype(BF)
        dk[...] = jnp.zeros_like(dk)
        dv[...] = jnp.zeros_like(dv)
        lane = lax.broadcasted_iota(jnp.int32, (QB, 128), 1)
        alive = lax.broadcasted_iota(jnp.int32, (rows, QB), 0) < live[m]
        n_b = rows // QB

        def block(i, carry):
            h = i // n_b
            at = pl.ds(pl.multiple_of(lax.rem(i, n_b) * QB, QB), QB)
            hs = pl.ds(pl.multiple_of(h * HEAD_DIM, HEAD_DIM), HEAD_DIM)
            keep = lane // HEAD_DIM == h
            qh = jnp.where(keep, q[m, at, :], BF(0.0))
            gh = jnp.where(keep, mg[at, :], BF(0.0))
            s = nt(k[m], qh)
            p = jnp.where(alive, jnp.exp(s - lse[m, pl.ds(h, 1), at]), 0.0)
            dp = nt(v[m], gh)
            ds = (p * (dp - delta[pl.ds(h, 1), at])).astype(BF)
            dv[...] += nn(p.astype(BF), gh)
            dk[...] += nn(ds, qh)
            dq_t[hs, at] = nn(k_t[hs, :], ds)
            for j, hook in enumerate(hooks):
                pl.when(i == j)(hook)
            return carry

        lax.fori_loop(0, 2 * n_b, block, 0)
        dq = dq_t[...].T * 0.125
        joined[m, :, 0:128] = rotate(dq, cos[...], sin[...], -1.0).astype(BF)
        joined[m, :, 128:256] = rotate(dk[...], cos[...], sin[...], -1.0).astype(BF)
        joined[m, :, 256:384] = dv[...].astype(BF)

    def nothing():
        pass

    def h0():
        g3[1].s1()
        red4[0].s1()

    def h1():
        g3[1].s2()
        red4[0].s2()

    def h2():
        g3[1].s3()
        red4[0].s3()

    def h3():
        red4[1].s1()

    attend_back(0, (h0, h1, h2, h3))
    g3[1].s4()

    def finish_out(m):
        rows_out = hidden[m] + red4[m].s4()
        orow[m] = rows_out.astype(BF).reshape(orow.shape[1:])
        ret_o.start(m)
        red4[m].end()

    finish_out(0)
    product(red3, 0, joined_rows, lambda: wq[...].reshape(D, -1))

    def k0():
        red4[1].s2()
        red3[0].s1()

    def k1():
        red4[1].s3()
        red3[0].s2()

    def k2():
        red3[0].s3()

    attend_back(1, (k0, k1, k2))
    finish_out(1)
    product(red3, 1, joined_rows, lambda: wq[...].reshape(D, -1))
    red3[1].s1()
    load.wait()
    flat_j = joined[...].reshape(2 * rows, -1)
    flat_m = mixed[...].reshape(2 * rows, -1)
    n_d = 256

    def late(b, carry):
        at = pl.ds(pl.multiple_of(b * n_d, n_d), n_d)
        x = first[:, :, :, :, :, at].reshape(2 * rows, n_d)
        y = full[:, :, :, :, :, at].reshape(2 * rows, n_d)
        gq = tn(x, flat_j).astype(BF)
        go = tn(y, flat_m).astype(BF)
        if gl.shape[1] == n_d:
            gl[b, :, 0:384] = gq
            gl[b, :, 384:512] = go
        else:
            blk = n_d // gl.shape[1]
            gl[pl.ds(b * blk, blk), :, 0:384] = gq.reshape(blk, gl.shape[1], 384)
            gl[pl.ds(b * blk, blk), :, 384:512] = go.reshape(blk, gl.shape[1], 128)
        return carry

    lax.fori_loop(0, D // n_d, late, 0)
    collect_l.start()
    red3[1].s2()

    def norm4(m):
        grad = red3[m].s4()
        hat, inv = norm_stats(tok[m].reshape(-1, D).astype(F32))
        new = hg[m] + norm_back(grad, hat, inv, gains[0:1, :])
        grow[m] = new.astype(BF).reshape(grow.shape[1:])
        ret_g.start(m)
        return jnp.sum(grad * hat, axis=0, keepdims=True)

    gain1 = norm4(0)
    red3[1].s3()
    collect_g.total(accg)
    collect_l.relay()
    gain1 = gain1 + norm4(1)
    row = lax.broadcasted_iota(jnp.int32, gain2.shape, 0)
    gt[0] = jnp.where(row == 0, gain1, jnp.where(row == 1, gain2[...], 0.0))
    s0.start()
    ret_o.wait()
    s0.wait_recv()
    gp[c] = gt[0] + gt[1]
    each(gps, "start")
    collect_l.total(accl)
    ssend[:, :, 0:nl] = accl[...].astype(BF).reshape(4, -1, nl)
    ssend[:, :, nl : nl + ng] = accg[...].astype(BF).reshape(4, -1, ng)
    ssend[:, :, nl + ng :] = gd[...].reshape(4, -1, hp)
    swap.start()
    each(gps, "wait_recv")
    gz[f] = jnp.sum(gp[...], axis=0)
    each(gzs, "start")
    swap.keep()
    ret_g.wait()
    ret_o.end()

    def unpack(dst, back, other):
        for s in range(n_f):
            dst[t, s] = back[owners[t, s]]
            dst[1 - t, s] = other[owners[1 - t, s]]

    unpack(out_o, oback, oother)
    each(gzs, "wait_recv")
    gain_o[...] = jnp.sum(gz[...], axis=0)
    ret_g.end()
    unpack(grad_o, gback, gother)
    swap.wait()
    each([s0] + gps + gzs, "wait_send")
    for x in g3 + red3 + [collect_g, collect_l, swap]:
        x.end()


def rope_tables(rows):
    lane = jnp.arange(128, dtype=jnp.int32)
    exponent = (2 * (lane % (HEAD_DIM // 2))).astype(F32)
    inverse = rope_base ** (-exponent / HEAD_DIM)
    angles = jnp.arange(rows, dtype=jnp.int32).astype(F32)[:, None] * inverse[None, :]
    sign = jnp.where(lane % HEAD_DIM < HEAD_DIM // 2, -1.0, 1.0)
    return jnp.cos(angles), jnp.sin(angles) * sign[None, :]


def per_device(n_f, n_c, n_t, tokens, cotangent, lengths, owners,
               norm_attn, norm_mlp, w_qkv, w_out, w_in, w_down):
    f, c, t = here()
    micro, seqs, _, piece, _ = tokens.shape
    assert n_c == 4 and n_t == 2 and micro == 2 and seqs == n_f
    span = piece * n_f
    half = span // 4
    rows = span * n_c
    n_h = n_f // 2
    wr = w_qkv.shape[0]
    hid = w_in.shape[2]
    hp = -(-hid // (n_c * 128)) * 128
    heads = w_qkv.shape[2] // n_c
    wb = n_c * wr

    order = jnp.argsort(owners, axis=1).astype(jnp.int32)
    live = lax.dynamic_index_in_dim(lengths, f, axis=1, keepdims=False)
    place = (f * n_c + c) * wr
    gains_own = jnp.stack([norm_attn, norm_mlp]).astype(F32)
    gains_row = lax.dynamic_update_slice(jnp.zeros((8, D), F32), gains_own, (0, place))

    def quarters(a):
        return a.transpose(2, 0, 1, 3).reshape(n_c, wr, -1)

    more = n_c * hp - hid
    p_qkv = quarters(w_qkv.reshape(wr, 3, n_c, heads))
    p_out = w_out.reshape(n_c, heads, wr).transpose(0, 2, 1)
    p_in = quarters(jnp.pad(w_in, [(0, 0), (0, 0), (0, more)]).reshape(wr, 2, n_c, hp))
    p_down = jnp.pad(w_down, [(0, more), (0, 0)]).reshape(n_c, hp, wr).transpose(0, 2, 1)
    n_q = 3 * heads
    cos, sin = rope_tables(rows)

    full_shape = (micro, n_c, 2, 2, half, D)
    own_shape = (micro, n_h, piece, D)
    row_shape = (micro, 2 * half, D)
    head_shape = (micro, rows, 128)
    V = pltpu.VMEM
    (tok, cot, gains, wq, wo, w2, q3, first_h, cot_h, q, k, v, mixed, out_t, lse, hidden,
     second) = comm_call(
        functools.partial(first_kernel, n_f),
        [
            (shaped(own_shape, BF), vm()), (shaped(own_shape, BF), vm()),
            (shaped((8, D), F32), vm()),
            (shaped((n_f, n_c, wr, n_q), BF), vm()), (shaped((n_f, n_c, wr, heads), BF), vm()),
            (shaped((n_f, n_c, wr, 2 * hp), BF), vm()), (shaped((n_c, wr, hp), BF), vm()),
            (shaped(full_shape, BF), hb()), (shaped(full_shape, BF), hb()),
        ]
        + [(shaped(head_shape, BF), vm())] * 4
        + [
            (shaped((micro, 128, rows), F32), vm()), (shaped((micro, 8, rows), F32), vm()),
            (shaped(row_shape, F32), vm()), (shaped((micro, 2, half, D), BF), vm()),
        ],
        [sm(), sm()] + [vm()] * 9,
        [
            V((n_f, piece, D), BF), V((n_f, piece, D), BF), V((n_f, 8, D), F32),
            V((n_c, 8, D), F32), V(full_shape, BF), V(full_shape, BF),
        ]
        + reduce_scratch(half)
        + [V((128, rows), BF)],
        5 * n_f + 120, 2, 0, 10**10,
    )(order, live, tokens[:, :, 0], cotangent[:, :, 0], gains_row, p_qkv, p_out, p_in, p_down,
      cos, sin)

    hg, attn, act, gain2, w3, g_in, g_down = comm_call(
        functools.partial(second_kernel, n_f),
        [
            (shaped(row_shape, F32), vm()), (shaped((micro, 2, half, D), BF), vm()),
            (shaped((micro, n_c, span, hp), BF), vm()), (shaped((8, D), F32), vm()),
            (shaped((n_f, n_c, wr, hp), BF), vm()),
            (shaped((D, 2 * hp), BF), vm()), (shaped((wb, hp), BF), vm()),
        ],
        [vm(), vm(), vm(), hb()] + [vm()] * 3,
        [
            V(full_shape, BF), V(full_shape, BF), V((micro, n_c, span, 2 * hp), BF),
            V((n_f, wb, hp), BF), V((collect_slots(n_f), wb, hp), BF), V((wb, hp), F32),
        ]
        + reduce_scratch(half),
        n_f + 60, 1, 1, 10**10,
    )(second, w2, q3, cot_h, cot, hidden, gains)

    outs, grads, gain_grads, shares = comm_call(
        functools.partial(third_kernel, n_f),
        [
            (shaped((micro, n_f, piece, D), BF), vm()), (shaped((micro, n_f, piece, D), BF), vm()),
            (shaped((8, D), F32), vm()), (shaped((n_c, wr, n_q + heads + 3 * hp), BF), vm()),
        ],
        [sm(), sm()] + [vm()] * 11 + [hb()] + [vm()] * 9,
        [
            V(full_shape, BF), V(full_shape, BF), V((rows, 128), F32), V((rows, 128), F32),
            V((128, rows), F32), V((rows, 128), BF), V((8, rows), F32), V((128, rows), BF),
            V((micro, rows, 384), BF),
        ]
        + reduce_scratch(half)
        + reduce_scratch(half)[1:]
        + [
            V((n_f, wb, n_q + heads), BF),
            V((collect_slots(n_f), wb, n_q + heads), BF), V((collect_slots(n_f), wb, 2 * hp), BF),
            V((wb, n_q + heads), F32), V((wb, 2 * hp), F32),
            V((n_c, wr, n_q + heads + 3 * hp), BF),
            V(own_shape, BF), V(own_shape, BF),
            V((n_f, piece, D), BF), V((n_f, piece, D), BF),
            V((n_f, piece, D), BF), V((n_f, piece, D), BF),
            V((n_f, 8, D), F32), V((n_c, 8, D), F32), V((2, 8, D), F32),
        ],
        6 * n_f + 100, 1, 2, 10**10,
    )(owners, live, attn, wo, wq, w3, act, q, k, v, mixed, out_t, lse, first_h, hg, hidden, tok,
      gains, gain2, g_in.reshape(n_f, wb, 2 * hp), g_down, cos, sin)

    shares = shares.astype(F32)
    n1, n2 = n_q + heads, n_q + heads + 2 * hp
    grad_qkv = shares[:, :, :n_q].reshape(n_c, wr, 3, heads).transpose(1, 2, 0, 3)
    grad_qkv = grad_qkv.reshape(wr, 3, n_c * heads)
    grad_out = shares[:, :, n_q:n1].transpose(0, 2, 1).reshape(n_c * heads, wr)
    grad_in = shares[:, :, n1:n2].reshape(n_c, wr, 2, hp)
    grad_in = grad_in.transpose(1, 2, 0, 3).reshape(wr, 2, n_c * hp)[..., :hid]
    grad_down = shares[:, :, n2:].transpose(0, 2, 1).reshape(n_c * hp, wr)[:hid]
    mine = lax.dynamic_slice(gain_grads, (0, place), (2, wr))
    return (outs[:, :, None], grads[:, :, None], mine[0], mine[1],
            grad_qkv, grad_out, grad_in, grad_down)


def solution(mesh):
    rows = P(None, None, "ctx", "fsdp", None)
    gain = P(("fsdp", "ctx"))
    tall = P(("fsdp", "ctx"), None, "tp")
    wide = P("tp", ("fsdp", "ctx"))
    return jax.shard_map(
        functools.partial(per_device, mesh.shape["fsdp"], mesh.shape["ctx"], mesh.shape["tp"]),
        mesh=mesh,
        in_specs=(rows, rows, P(), P(), gain, gain, tall, wide, tall, wide),
        out_specs=(rows, rows, gain, gain, tall, wide, tall, wide),
        check_vma=False,
    )
```

```python
import functools

import jax
import jax.numpy as jnp
from jax import lax
from jax.experimental import pallas as pl
from jax.experimental.pallas import tpu as pltpu
from jax.sharding import PartitionSpec as P

D = 1024
HEAD_DIM = 64
norm_eps = 1e-05
rope_base = 160000.0
masked_score = -1e30
MESH = pl.DeviceIdType.MESH
BF = jnp.bfloat16
F32 = jnp.float32
VLIMIT = 56 << 20


def nn(a, b):
    return lax.dot_general(a, b, (((1,), (0,)), ((), ())), preferred_element_type=F32)


def nt(a, b):
    return lax.dot_general(a, b, (((1,), (1,)), ((), ())), preferred_element_type=F32)


def tn(a, b):
    return lax.dot_general(a, b, (((0,), (0,)), ((), ())), preferred_element_type=F32)


def norm_stats(values):
    center = values - jnp.mean(values, axis=-1, keepdims=True)
    spread = jnp.mean(center * center, axis=-1, keepdims=True)
    inverse_std = lax.rsqrt(spread + norm_eps)
    return center * inverse_std, inverse_std


def norm_back(upstream, normed, inverse_std, gain):
    scaled = upstream * gain
    adjusted = (
        scaled
        - jnp.mean(scaled, axis=-1, keepdims=True)
        - normed * jnp.mean(scaled * normed, axis=-1, keepdims=True)
    )
    return adjusted * inverse_std


def here():
    return lax.axis_index("fsdp"), lax.axis_index("ctx"), lax.axis_index("tp")


def remote(src, dst, sems, i, where, j=None):
    return pltpu.make_async_remote_copy(
        src_ref=src,
        dst_ref=dst,
        send_sem=sems.at[0, i],
        recv_sem=sems.at[1, i if j is None else j],
        device_id=where,
        device_id_type=MESH,
    )


def greet(peers):
    bar = pltpu.get_barrier_semaphore()
    for p in peers:
        pl.semaphore_signal(bar, inc=1, device_id=p, device_id_type=MESH)
    pl.semaphore_wait(bar, len(peers))


class Ids:
    def __init__(self):
        self.next = 0

    def take(self, count):
        self.next += count
        return self.next - count


def each(copies, what):
    for copy in copies:
        getattr(copy, what)()


class Gather:
    def __init__(self, full, m, sems, ids):
        f, c, t = here()
        px, py, po = (f, c ^ 1, t), (f, c ^ 2, t), (f, c, 1 - t)
        cx, cy, cd = c ^ 1, c ^ 2, c ^ 3
        base = ids.take(10)

        def cp(i, view, where):
            return remote(view, view, sems, base + i, where)

        self.bx = cp(0, full.at[m, c, t, 1], px)
        self.ay = cp(1, full.at[m, c, t, 0], py)
        self.ax = cp(2, full.at[m, c, t, 0], px)
        self.by = cp(3, full.at[m, c, t, 1], py)
        self.oo = cp(4, full.at[m, c, t], po)
        self.fy = cp(5, full.at[m, cx, t, 1], py)
        self.fx = cp(6, full.at[m, cy, t, 0], px)
        self.ox = cp(7, full.at[m, cx, t], po)
        self.oy = cp(8, full.at[m, cy, t], po)
        self.od = cp(9, full.at[m, cd, t], po)

    def s0(self):
        each([self.bx, self.ay, self.ax, self.by, self.oo], "start")

    def s1(self):
        self.bx.wait_recv()
        self.fy.start()
        self.ay.wait_recv()
        self.fx.start()

    def s2(self):
        self.ax.wait_recv()
        self.ox.start()
        self.by.wait_recv()
        self.oy.start()

    def s3(self):
        self.fy.wait_recv()
        self.fx.wait_recv()
        self.od.start()

    def s4(self):
        each([self.oo, self.ox, self.oy, self.od], "wait_recv")

    def rest(self):
        self.s2()
        self.s3()
        self.s4()

    def end(self):
        each(
            [self.bx, self.ay, self.ax, self.by, self.oo, self.fy, self.fx, self.ox, self.oy,
             self.od],
            "wait_send",
        )


class Reduce:
    def __init__(self, part, r0, rx, ry, sems, ids):
        f, c, t = here()
        px, py, self.po = (f, c ^ 1, t), (f, c ^ 2, t), (f, c, 1 - t)
        cx, cy, cd = c ^ 1, c ^ 2, c ^ 3
        self.base = ids.take(10)
        self.part, self.r0, self.rx, self.ry, self.sems = part, r0, rx, ry, sems
        self.own, self.t, self.cx, self.cy, self.cd = c, t, cx, cy, cd

        def cp(i, src, dst, where):
            return remote(src, dst, sems, self.base + i, where)

        self.cross = [self.crossing(i) for i in range(4)]
        self.a0 = cp(4, part.at[cd, t, 0], rx.at[0], px)
        self.b0 = cp(5, part.at[cd, t, 1], ry.at[0], py)
        self.a1 = cp(6, part.at[cx, t, 0], rx.at[1], px)
        self.b1 = cp(7, part.at[cy, t, 1], ry.at[1], py)
        self.b2 = cp(8, part.at[cy, t, 0], ry.at[2], py)
        self.a2 = cp(9, part.at[cx, t, 1], rx.at[2], px)

    def span(self, i):
        return self.own ^ (3 - i - jnp.where(jnp.int32(i) == 1, 1, 0) + jnp.where(jnp.int32(i) == 2, 1, 0))

    def crossing(self, i):
        return remote(
            self.part.at[self.span(i), 1 - self.t], self.r0.at[i], self.sems, self.base + i, self.po
        )

    def add(self, i, span):
        self.cross[i].wait_recv()
        part, t = self.part, self.t
        part[span, t] = (part[span, t].astype(F32) + self.r0[i].astype(F32)).astype(BF)

    def s1(self):
        self.add(0, self.cd)
        self.a0.start()
        self.b0.start()

    def s2(self):
        self.add(1, self.cx)
        self.a1.start()
        self.add(2, self.cy)
        self.b1.start()

    def s3(self):
        part, t = self.part, self.t
        self.a0.wait_recv()
        part[self.cy, t, 0] = (part[self.cy, t, 0].astype(F32) + self.rx[0].astype(F32)).astype(BF)
        self.b2.start()
        self.b0.wait_recv()
        part[self.cx, t, 1] = (part[self.cx, t, 1].astype(F32) + self.ry[0].astype(F32)).astype(BF)
        self.a2.start()

    def s4(self):
        self.cross[3].wait_recv()
        own = self.part[self.own, self.t].astype(F32) + self.r0[3].astype(F32)
        each([self.a1, self.b1, self.b2, self.a2], "wait_recv")
        top = own[0] + self.rx[1].astype(F32) + self.ry[2].astype(F32)
        bottom = own[1] + self.ry[1].astype(F32) + self.rx[2].astype(F32)
        return jnp.concatenate([top, bottom], axis=0)

    def end(self):
        each(self.cross + [self.a0, self.b0, self.a1, self.b1, self.b2, self.a2], "wait_send")


def reduce_scratch(half):
    return [
        pltpu.VMEM((2, 4, 2, 2, half, D), BF),
        pltpu.VMEM((2, 4, 2, half, D), BF),
        pltpu.VMEM((2, 3, half, D), BF),
        pltpu.VMEM((2, 3, half, D), BF),
    ]


class Spread:
    def __init__(self, ref, n_f, sems, ids):
        f, c, t = here()
        self.f, self.n_f, self.ref = f, n_f, ref
        if n_f == 4:
            base = ids.take(5)
            self.steps = (-1, -2, 1, 2)
            self.copies = [
                remote(ref.at[f], ref.at[f], sems, base + i, (lax.rem(f - d + n_f, n_f), c, t))
                for i, d in enumerate(self.steps)
            ]
            self.far = remote(
                ref.at[jnp.where(f == 2, 0, 3)], ref.at[jnp.where(f == 2, 0, 3)], sems, base + 4,
                (jnp.where(f == 2, 3, 0), c, t),
            )
        else:
            base = ids.take(1)
            self.copies = [
                remote(ref.at[f], ref.at[f], sems, base, (lax.rem(f + k, n_f), c, t))
                for k in range(1, n_f)
            ]
            most = ref.at[pl.ds(0, n_f - 1)]
            self.all = remote(most, most, sems, base, (f, c, 1 - t))

    def start(self):
        if self.n_f != 4:
            return each(self.copies, "start")
        for d, cp in zip(self.steps, self.copies):
            pl.when((self.f - d >= 0) & (self.f - d < 4))(cp.start)

    def relay(self):
        if self.n_f != 4:
            return

        @pl.when(self.f == 2)
        def _():
            self.copies[1].wait_recv()
            self.far.start()

        @pl.when(self.f == 1)
        def _():
            self.copies[3].wait_recv()
            self.far.start()

    def wait(self):
        if self.n_f != 4:
            return self.all.wait_recv()
        f = self.f
        pl.when(f >= 1)(self.copies[0].wait_recv)
        pl.when(f == 3)(self.copies[1].wait_recv)
        pl.when(f <= 2)(self.copies[2].wait_recv)
        pl.when(f == 0)(self.copies[3].wait_recv)
        pl.when((f == 0) | (f == 3))(self.far.wait_recv)

    def end(self):
        if self.n_f != 4:
            return self.all.wait_send()
        for d, cp in zip(self.steps, self.copies):
            pl.when((self.f - d >= 0) & (self.f - d < 4))(cp.wait_send)
        pl.when((self.f == 1) | (self.f == 2))(self.far.wait_send)


class Collect:
    def __init__(self, ref, got, n_f, sems, ids, passed=True):
        f, c, t = here()
        n_f = n_f if passed or n_f != 4 else -n_f
        self.f, self.n_f, self.ref, self.got = f, n_f, ref, got
        if n_f == 4:
            base = ids.take(5)
            self.steps = (-1, -2, 1, 2)
            self.copies = []
            for i, d in enumerate(self.steps):
                j = lax.rem(f - d + n_f, n_f)
                self.copies.append(remote(ref.at[j], got.at[i], sems, base + i, (j, c, t)))
            away = jnp.where(f == 0, 3, 0)
            self.far = remote(
                ref.at[away], got.at[4], sems, base + 4, (jnp.where(f == 0, 1, 2), c, t)
            )
        else:
            base = ids.take(1)
            self.copies = []
            n_f = abs(n_f)
            for k in range(1, n_f):
                j = lax.rem(f + k, n_f)
                self.copies.append(remote(ref.at[j], got.at[k - 1], sems, base, (j, c, t)))
            most = ref.at[pl.ds(0, n_f - 1)]
            self.all = remote(most, got.at[pl.ds(0, n_f - 1)], sems, base, (f, c, 1 - t))

    def there(self, d):
        return (self.f - d >= 0) & (self.f - d < 4)

    def late(self, d):
        if d == 2:
            return self.f == 2
        if d == -2:
            return self.f == 1
        return self.f < 0

    def start(self):
        if self.n_f != 4:
            return each(self.copies, "start")
        pl.when((self.f == 0) | (self.f == 3))(self.far.start)
        for d, cp in zip(self.steps, self.copies):
            pl.when(self.there(d) & ~self.late(d))(cp.start)

    def relay(self):
        if self.n_f != 4:
            return
        for d, cp, j in ((2, self.copies[3], 0), (-2, self.copies[1], 3)):

            @pl.when(self.late(d))
            def _():
                self.far.wait_recv()
                self.ref[j] = (self.ref[j].astype(F32) + self.got[4].astype(F32)).astype(BF)
                cp.start()

    def total(self, acc):
        acc[...] = self.ref[self.f].astype(F32)
        if self.n_f != 4:
            self.all.wait_recv()
            for k in range(abs(self.n_f) - 1):
                acc[...] += self.got[k].astype(F32)
            return
        for i, d in enumerate(self.steps):

            @pl.when((self.f + d >= 0) & (self.f + d < 4))
            def _():
                self.copies[i].wait_recv()
                acc[...] += self.got[i].astype(F32)

    def end(self):
        if self.n_f != 4:
            return self.all.wait_send()
        for d, cp in zip(self.steps, self.copies):
            pl.when(self.there(d))(cp.wait_send)
        pl.when((self.f == 0) | (self.f == 3))(self.far.wait_send)


def collect_slots(n_f):
    return 5 if n_f == 4 else n_f - 1


class Deal:
    def __init__(self, stage, own, n_f, sems, ids):
        f, c, t = here()
        n_h = n_f // 2
        self.base = ids.take(2 * n_f)
        self.f, self.t, self.n_f, self.n_h, self.own, self.sems = f, t, n_f, n_h, own, sems
        self.side, at = f // n_h, lax.rem(f, n_h)
        self.mine = self.side == t
        self.moves = []
        for m in range(2):
            dst = self.piece(m, at, t)
            recv = self.base + (m * n_h + at) * 2 + t
            sent = self.base + m * n_f
            away = [
                remote(stage.at[m, lax.rem(f + k, n_f)], dst, sems, sent + k,
                       (lax.rem(f + k, n_f), c, self.side), recv)
                for k in range(1, n_f)
            ]
            over = remote(stage.at[m, f], dst, sems, sent, (f, c, 1 - t), recv)
            keep = pltpu.make_async_copy(stage.at[m, f], dst, sems.at[1, recv])
            self.moves.append((away, over, keep))

    def piece(self, m, j, core):
        wide = D // 2
        return self.own.at[m, j, :, pl.ds(pl.multiple_of(core * wide, wide), wide)]

    def start(self, m):
        away, over, keep = self.moves[m]
        each(away, "start")
        pl.when(self.mine)(keep.start)
        pl.when(~self.mine)(over.start)

    def wait(self, m):
        f, c, t = here()
        for j in range(self.n_h):
            for core in range(2):
                i = self.base + (m * self.n_h + j) * 2 + core
                view = self.piece(m, j, core)
                local = (t == core) & (f == t * self.n_h + j)
                pl.when(local)(pltpu.make_async_copy(view, view, self.sems.at[1, i]).wait)
                pl.when(~local)(remote(view, view, self.sems, i, (f, c, 1 - t)).wait_recv)

    def end(self):
        for away, over, _ in self.moves:
            each(away, "wait_send")
            pl.when(~self.mine)(over.wait_send)


class Return:
    def __init__(self, own, back, other, n_f, sems, ids):
        f, c, t = here()
        n_h = n_f // 2
        self.base = ids.take(2 * n_f + 1)
        self.f, self.t, self.n_f, self.back, self.sems = f, t, n_f, back, sems
        self.moves = []
        for m in range(2):
            for j in range(n_h):
                to = t * n_h + j
                i = self.base + m * n_h + j
                far = remote(own.at[m, j], back.at[f], sems, i, (to, c, m), self.base + f)
                keep = pltpu.make_async_copy(own.at[m, j], back.at[f], sems.at[1, self.base + f])
                self.moves.append((m, (to == f) & (t == m), far, keep))
        self.swap = remote(back, other, sems, self.base + 2 * n_f, (f, c, 1 - t))

    def start(self, m):
        for which, local, far, keep in self.moves:
            if which == m:
                pl.when(local)(keep.start)
                pl.when(~local)(far.start)

    def wait(self):
        n_h = self.n_f // 2
        f, c, t = here()
        for s in range(self.n_f):
            local = (f == s) & (f // n_h == t)
            view = self.back.at[s]
            i = self.base + s
            pl.when(local)(pltpu.make_async_copy(view, view, self.sems.at[1, i]).wait)
            pl.when(~local)(remote(view, view, self.sems, i, (f, c, 1 - t)).wait_recv)
        self.swap.start()

    def end(self):
        self.swap.wait_recv()
        for _, local, far, _ in self.moves:
            pl.when(~local)(far.wait_send)
        self.swap.wait_send()


class Swap:
    def __init__(self, src, dst, sems, ids):
        f, c, t = here()
        base = ids.take(3)
        self.src, self.dst, self.c = src, dst, c
        self.copies = [
            remote(src.at[c ^ k], dst.at[c], sems, base + k - 1, (f, c ^ k, t)) for k in (1, 2, 3)
        ]

    def start(self):
        each(self.copies, "start")

    def keep(self):
        self.dst[self.c] = self.src[self.c]

    def wait(self):
        each(self.copies, "wait_recv")

    def end(self):
        each(self.copies, "wait_send")


def everyone(n_f):
    f, c, t = here()
    peers = [(f, c ^ 1, t), (f, c ^ 2, t), (f, c ^ 3, t), (f, c, 1 - t)]
    for k in range(1, n_f):
        for core in range(2):
            peers.append((lax.rem(f + k, n_f), c, core))
    return peers


def vm():
    return pl.BlockSpec(memory_space=pltpu.VMEM)


def sm():
    return pl.BlockSpec(memory_space=pltpu.SMEM)


def hb():
    return pl.BlockSpec(memory_space=pl.ANY)


def shaped(shape, dtype):
    return jax.ShapeDtypeStruct(shape, dtype)


def comm_call(kernel, outs, ins, scratch, n_sems, n_local, cid, flops):
    return pl.pallas_call(
        kernel,
        out_shape=[s for s, _ in outs],
        in_specs=ins,
        out_specs=[b for _, b in outs],
        scratch_shapes=scratch
        + [pltpu.SemaphoreType.DMA((2, n_sems)), pltpu.SemaphoreType.DMA((n_local,))],
        compiler_params=pltpu.CompilerParams(
            collective_id=cid, has_side_effects=True, vmem_limit_bytes=VLIMIT
        ),
        cost_estimate=pl.CostEstimate(flops=flops, bytes_accessed=1 << 20, transcendentals=0),
    )


def rotate(u, cos, sin, sign):
    lane = lax.broadcasted_iota(jnp.int32, u.shape, 1)
    partner = jnp.where(lane % HEAD_DIM < HEAD_DIM // 2, pltpu.roll(u, 96, 1), pltpu.roll(u, 32, 1))
    return u * cos + partner * (sin * sign)


class Keep:
    def __init__(self, sems):
        self.sems, self.copies = sems, []

    def move(self, src, dst):
        copy = pltpu.make_async_copy(src, dst, self.sems.at[len(self.copies)])
        copy.start()
        self.copies.append(copy)
        return copy


def table(small, dst):
    fine_cos, fine_sin = small[2], small[3]
    steps = fine_cos.shape[0]
    for i in range(dst.shape[1] // steps):
        coarse_cos, coarse_sin = small[0, i : i + 1, :], small[1, i : i + 1, :]
        at = pl.ds(i * steps, steps)
        dst[0, at, :] = coarse_cos * fine_cos - coarse_sin * fine_sin
        dst[1, at, :] = (coarse_sin * fine_cos + coarse_cos * fine_sin) * small[4]


def front_kernel(
    n_f, order, lengths, tok, cot, gains, pq, po, p2, p3, small,
    gains_o, tok_h, hidden_h, wq_h, wo_h, w3_h, q_h, k_h, v_h, mixed_h, out_h, lse_h, first_h,
    act_h, hg_o, attn_o, gain_o, gi_o, gd_o,
    tok_o, cot_o, hidden_o, wq, wo, w2, w3, q_o, k_o, v_o, mixed_o, out_o, lse_o, act_o,
    stage, scot, gz, gp, first, cotf, full, gg, gd, got, acc, part, r0, rx, ry, v_t, turn,
    sems, lsem,
):
    f, c, t = here()
    ids = Ids()
    plane = [(f, c ^ k, t) for k in (1, 2, 3)]
    zs = [(lax.rem(f + k, n_f), c, t) for k in range(1, n_f)]
    half = first.shape[4]
    rows = 16 * half
    hp = w3.shape[3]
    wide = D // 2

    deal_tok = Deal(stage, tok_o, n_f, sems, ids)
    deal_cot = Deal(scot, cot_o, n_f, sems, ids)
    base = ids.take(n_f - 1)
    gs = [remote(gains, gz.at[f], sems, base + k, zs[k]) for k in range(n_f - 1)]
    base = ids.take(3)
    gps = [remote(gp.at[c], gp.at[c], sems, base + k, plane[k]) for k in range(3)]
    swaps = [Swap(src, w.at[f], sems, ids)
             for src, w in ((pq, wq), (po, wo), (p2, w2), (p3, w3))]
    spreads = [Spread(w, n_f, sems, ids) for w in (wq, wo, w2, w3)]
    g1, gc, g2 = ([Gather(x, m, sems, ids) for m in range(2)] for x in (first, cotf, full))
    red1, red2 = (
        [Reduce(part.at[m], r0.at[m], rx.at[m], ry.at[m], sems, ids) for m in range(2)]
        for _ in range(2)
    )
    collect = Collect(gd, got, n_f, sems, ids, passed=False)
    keep = Keep(lsem)
    mine = pl.ds(pl.multiple_of(t * wide, wide), wide)

    def stage_rows(src, dst, m):
        for j in range(n_f):
            dst[m, j] = src[m, order[m, j], :, mine]

    stage_rows(tok, stage, 0)
    greet(everyone(n_f))
    deal_tok.start(0)
    each(gs, "start")
    each(swaps[:2], "start")
    stage_rows(tok, stage, 1)
    deal_tok.start(1)
    each(swaps[2:], "start")
    each(swaps, "keep")
    gz[f] = gains[...]
    stage_rows(cot, scot, 0)
    stage_rows(cot, scot, 1)
    table(small, turn)
    each(gs, "wait_recv")
    gp[c] = jnp.sum(gz[...], axis=0)
    each(gps, "start")

    def norm1(m):
        deal_tok.wait(m)
        hat, _ = norm_stats(tok_o[m].reshape(-1, D).astype(F32))
        first[m, c, t] = (hat * gains_o[0:1, :]).astype(BF).reshape(2, half, D)

    each(gps, "wait_recv")
    gains_o[...] = jnp.sum(gp[...], axis=0)
    norm1(0)
    g1[0].s0()
    swaps[0].wait()
    norm1(1)
    spreads[0].start()
    g1[0].s1()
    g1[1].s0()
    swaps[1].wait()
    g1[0].s2()
    spreads[1].start()
    g1[0].s3()
    spreads[0].relay()
    deal_cot.start(0)
    deal_cot.start(1)
    g1[0].s4()
    spreads[0].wait()
    g1[1].s1()

    def attend(m, hooks):
        joined = nn(first[m].reshape(rows, D), wq[...].reshape(D, -1))
        q_o[m] = rotate(joined[:, 0:128], turn[0], turn[1], 1.0).astype(BF) * BF(0.125)
        k_o[m] = rotate(joined[:, 128:256], turn[0], turn[1], 1.0).astype(BF)
        v = joined[:, 256:384]
        v_o[m] = v.astype(BF)
        v_t[...] = v.T.astype(BF)
        lane = lax.broadcasted_iota(jnp.int32, (rows, 128), 1)
        alive = lax.broadcasted_iota(jnp.int32, (rows, rows), 0) < lengths[m, f]

        def head(h, carry):
            at = pl.ds(pl.multiple_of(h * HEAD_DIM, HEAD_DIM), HEAD_DIM)
            qh = jnp.where(lane // HEAD_DIM == h, q_o[m], BF(0.0))
            s = jnp.where(alive, nt(k_o[m], qh), masked_score)
            top = jnp.max(s, axis=0, keepdims=True)
            p = jnp.exp(s - top)
            total = jnp.sum(p, axis=0, keepdims=True)
            out_o[m, at, :] = nn(v_t[at, :], p.astype(BF)) / total
            lse_o[m, pl.ds(h, 1), :] = top + jnp.log(total)
            for i, hook in enumerate(hooks):
                pl.when(h == i)(hook)
            return carry

        lax.fori_loop(0, 2, head, 0)
        mixed_o[m] = out_o[m].T.astype(BF)

    def product(m):
        def step(i, carry):
            span = red1[m].span(i)
            block = mixed_o[m, pl.ds(pl.multiple_of(span * 4 * half, 4 * half), 4 * half), :]
            part[m, span] = nt(block, wo[...].reshape(D, -1)).astype(BF).reshape(2, 2, half, D)
            red1[m].crossing(i).start()
            return carry

        lax.fori_loop(0, 4, step, 0)

    def norm2(m):
        hidden = tok_o[m].reshape(-1, D).astype(F32) + red1[m].s4()
        hidden_o[m] = hidden
        hat, _ = norm_stats(hidden)
        full[m, c, t] = (hat * gains_o[1:2, :]).astype(BF).reshape(2, half, D)
        g2[m].s0()

    def hook0():
        g1[1].s2()
        spreads[1].relay()

    attend(0, (hook0, g1[1].s3))
    spreads[1].wait()
    product(0)
    g1[1].s4()
    swaps[2].wait()
    swaps[3].wait()
    spreads[2].start()
    for src, dst in ((first, first_h), (tok_o, tok_h), (wq, wq_h), (wo, wo_h)):
        keep.move(src, dst)
    red1[0].s1()

    def hook1():
        red1[0].s2()

    def hook2():
        red1[0].s3()
        deal_cot.wait(0)
        cotf[0, c, t] = cot_o[0].reshape(2, half, D)

    attend(1, (hook1, hook2))
    product(1)
    gc[0].s0()
    red1[1].s1()
    deal_cot.wait(1)
    cotf[1, c, t] = cot_o[1].reshape(2, half, D)
    norm2(0)
    red1[1].s2()
    spreads[2].relay()
    spreads[3].start()
    red1[1].s3()
    gc[0].s1()
    gc[1].s0()
    g2[0].s1()
    norm2(1)
    gc[0].s2()
    g2[0].s2()
    gc[0].s3()
    g2[0].s3()
    g2[1].s1()
    gc[1].s1()
    for m in range(2):
        red1[m].end()
    for src, dst in ((q_o, q_h), (k_o, k_h), (v_o, v_h), (mixed_o, mixed_h), (out_o, out_h),
                     (lse_o, lse_h), (hidden_o, hidden_h)):
        keep.move(src, dst)
    spreads[3].relay()
    gc[0].s4()
    g2[0].s4()
    spreads[2].wait()
    spreads[3].wait()
    keep.move(w3, w3_h)

    def mlp(m, hooks):
        def step(i, carry):
            span = red2[m].span(i)
            low = full[m, span].reshape(4 * half, D)
            win = w2[...].reshape(D, 2 * hp)
            u = nn(low, win[:, :hp])
            g = nn(low, win[:, hp:])
            a = nn(cotf[m, span].reshape(4 * half, D), w3[...].reshape(D, hp))
            phi = 0.5 * (1.0 + lax.erf(u * 0.7071067811865476))
            gelu = u * phi
            slope = phi + u * (jnp.exp(-0.5 * u * u) * 0.3989422804014327)
            act_o[m, span] = (gelu * g).astype(BF)
            gg[m, span, :, 0:hp] = (a * g * slope).astype(BF)
            gg[m, span, :, hp:] = (a * gelu).astype(BF)
            part[m, span] = nt(gg[m, span], win).astype(BF).reshape(2, 2, half, D)
            red2[m].crossing(i).start()
            for j, hook in enumerate(hooks):
                pl.when(i == j)(hook)
            return carry

        lax.fori_loop(0, 4, step, 0)

    def rest2():
        gc[1].s2()
        g2[1].s2()

    def rest3():
        gc[1].s3()
        g2[1].s3()

    mlp(0, (rest2, rest3))
    red2[0].s1()
    gc[1].s4()
    g2[1].s4()
    mlp(1, (red2[0].s2, red2[0].s3))
    red2[1].s1()
    keep.move(act_o, act_h)
    flat_act = act_o[...].reshape(2 * rows, hp)
    flat_gg = gg[...].reshape(2 * rows, 2 * hp)
    n_d = max(256, gd.shape[1])

    def down(b, carry):
        x = cotf[:, :, :, :, :, pl.ds(pl.multiple_of(b * n_d, n_d), n_d)].reshape(2 * rows, n_d)
        sums = tn(x, flat_act).astype(BF)
        if gd.shape[1] == n_d:
            gd[b] = sums
        else:
            blk = n_d // gd.shape[1]
            gd[pl.ds(b * blk, blk)] = sums.reshape(blk, gd.shape[1], hp)
        return carry

    lax.fori_loop(0, D // n_d, down, 0)
    collect.start()
    red2[1].s2()

    def norm3(m):
        grad = red2[m].s4()
        hat, inv = norm_stats(hidden_o[m])
        hg = cot_o[m].reshape(-1, D).astype(F32) + norm_back(grad, hat, inv, gains_o[1:2, :])
        hg_o[m] = hg
        attn_o[m] = hg.astype(BF).reshape(2, half, D)
        return jnp.sum(grad * hat, axis=0, keepdims=True)

    gain = norm3(0)
    red2[1].s3()

    def inner(b, carry):
        x = full[:, :, :, :, :, pl.ds(pl.multiple_of(b * n_d, n_d), n_d)].reshape(2 * rows, n_d)
        gi_o[pl.ds(pl.multiple_of(b * n_d, n_d), n_d), :] = tn(x, flat_gg).astype(BF)
        return carry

    lax.fori_loop(0, D // n_d, inner, 0)
    gain = gain + norm3(1)
    gain_o[...] = jnp.broadcast_to(gain, gain_o.shape)
    collect.total(acc)
    gd_o[...] = acc[...].astype(BF)
    each(gs + gps, "wait_send")
    for x in [deal_tok, deal_cot, collect] + swaps + spreads + g1 + gc + g2 + red2:
        x.end()
    each(keep.copies, "wait")


def third_kernel(
    n_f, owners, lengths, attn, wo_h, wq_h, w3_h, act_h, q_h, k_h, v_h, mixed_h, out_h, lse_h,
    first_h, hg_h, hidden_h, tok_h, gains, gain2, gi, gd_h, small,
    out_o, grad_o, gain_o, early_o, late_o,
    wo, wq, w3, act, q, k, v, mixed, out, lse, hg, hidden, tok, gd, turn,
    full, first, dk, dv, dq_t, mg, delta, k_t, joined, part, r0, rx, ry, r0b, rxb, ryb,
    gl, gotl, gotg, accl, accg, ssend, slate, orow, grow, oback, gback, oother, gother, gz, gp, gt,
    sems, lsem,
):
    f, c, t = here()
    ids = Ids()
    half = full.shape[4]
    rows = 16 * half
    hp = w3.shape[3]
    nl, ng = accl.shape[1], accg.shape[1]
    plane = [(f, c ^ k_, t) for k_ in (1, 2, 3)]
    zs = [(lax.rem(f + k_, n_f), c, t) for k_ in range(1, n_f)]
    po = (f, c, 1 - t)
    g3 = [Gather(full, m, sems, ids) for m in range(2)]
    red4 = [Reduce(part.at[m], r0.at[m], rx.at[m], ry.at[m], sems, ids) for m in range(2)]
    red3 = [Reduce(part.at[m], r0b.at[m], rxb.at[m], ryb.at[m], sems, ids) for m in range(2)]
    collect_g = Collect(gi, gotg, n_f, sems, ids)
    collect_l = Collect(gl, gotl, n_f, sems, ids)
    ret_o = Return(orow, oback, oother, n_f, sems, ids)
    ret_g = Return(grow, gback, gother, n_f, sems, ids)
    swap = Swap(ssend, early_o, sems, ids)
    swap_late = Swap(slate, late_o, sems, ids)
    base = ids.take(1 + 3 + n_f - 1)
    s0 = remote(gt.at[0], gt.at[1], sems, base, po)
    gps = [remote(gp.at[c], gp.at[c], sems, base + 1 + j, plane[j]) for j in range(3)]
    gzs = [remote(gz.at[f], gz.at[f], sems, base + 4 + j, zs[j]) for j in range(n_f - 1)]
    keep = Keep(lsem)
    l_act, l_w3, l_wo, l_out, l_q, l_k, l_v, l_lse, l_hidden, l_wq, l_mixed, l_first, l_tok, l_hg, l_gd = [
        keep.move(src, dst)
        for src, dst in ((act_h, act), (w3_h, w3), (wo_h, wo), (out_h, out), (q_h, q), (k_h, k),
                         (v_h, v), (lse_h, lse), (hidden_h, hidden), (wq_h, wq),
                         (mixed_h, mixed), (first_h, first), (tok_h, tok), (hg_h, hg), (gd_h, gd))
    ]
    for m in range(2):
        full[m, c, t] = attn[m]
    greet(everyone(n_f))
    g3[0].s0()
    collect_g.start()

    def product(red, m, source, weight):
        def step(i, carry):
            span = red[m].span(i)
            part[m, span] = nt(source(m, span), weight()).astype(BF).reshape(2, 2, half, D)
            red[m].crossing(i).start()
            return carry

        lax.fori_loop(0, 4, step, 0)

    def act_rows(m, span):
        return act[m, span]

    def joined_rows(m, span):
        return joined[m, pl.ds(pl.multiple_of(span * 4 * half, 4 * half), 4 * half), :]

    table(small, turn)
    l_act.wait()
    l_w3.wait()
    g3[0].s1()
    g3[1].s0()
    product(red4, 0, act_rows, lambda: w3[...].reshape(D, hp))
    product(red4, 1, act_rows, lambda: w3[...].reshape(D, hp))
    g3[0].rest()
    collect_g.relay()
    each([l_wo, l_out, l_q, l_k, l_v, l_lse], "wait")
    QB = 512

    def attend_back(m, hooks):
        grad = nn(full[m].reshape(rows, D), wo[...].reshape(D, -1)).astype(BF)
        mg[...] = grad
        weighted = grad.astype(F32).T * out[m]
        delta[0:1, :] = jnp.sum(weighted[:HEAD_DIM], axis=0, keepdims=True)
        delta[1:2, :] = jnp.sum(weighted[HEAD_DIM:], axis=0, keepdims=True)
        k_t[...] = k[m].astype(F32).T.astype(BF)
        dk[...] = jnp.zeros_like(dk)
        dv[...] = jnp.zeros_like(dv)
        lane = lax.broadcasted_iota(jnp.int32, (QB, 128), 1)
        alive = lax.broadcasted_iota(jnp.int32, (rows, QB), 0) < lengths[m, f]
        n_b = rows // QB

        def block(i, carry):
            h = i // n_b
            at = pl.ds(pl.multiple_of(lax.rem(i, n_b) * QB, QB), QB)
            hs = pl.ds(pl.multiple_of(h * HEAD_DIM, HEAD_DIM), HEAD_DIM)
            keep = lane // HEAD_DIM == h
            qh = jnp.where(keep, q[m, at, :], BF(0.0))
            gh = jnp.where(keep, mg[at, :], BF(0.0))
            s = nt(k[m], qh)
            p = jnp.where(alive, jnp.exp(s - lse[m, pl.ds(h, 1), at]), 0.0)
            dp = nt(v[m], gh)
            ds = (p * (dp - delta[pl.ds(h, 1), at])).astype(BF)
            dv[...] += nn(p.astype(BF), gh)
            dk[...] += nn(ds, qh)
            dq_t[hs, at] = nn(k_t[hs, :], ds)
            for j, hook in enumerate(hooks):
                pl.when(i == j)(hook)
            return carry

        lax.fori_loop(0, 2 * n_b, block, 0)
        dq = dq_t[...].T * 0.125
        joined[m, :, 0:128] = rotate(dq, turn[0], turn[1], -1.0).astype(BF)
        joined[m, :, 128:256] = rotate(dk[...], turn[0], turn[1], -1.0).astype(BF)
        joined[m, :, 256:384] = dv[...].astype(BF)

    def nothing():
        pass

    def h0():
        g3[1].s1()
        red4[0].s1()

    def h1():
        g3[1].s2()
        red4[0].s2()

    def h2():
        g3[1].s3()
        red4[0].s3()

    def h3():
        red4[1].s1()

    attend_back(0, (h0, h1, h2, h3))
    g3[1].s4()
    l_hidden.wait()
    l_wq.wait()

    def finish_out(m):
        rows_out = hidden[m] + red4[m].s4()
        orow[m] = rows_out.astype(BF).reshape(orow.shape[1:])
        ret_o.start(m)
        red4[m].end()

    finish_out(0)
    product(red3, 0, joined_rows, lambda: wq[...].reshape(D, -1))

    def k0():
        red4[1].s2()
        red3[0].s1()

    def k1():
        red4[1].s3()
        red3[0].s2()

    def k2():
        red3[0].s3()

    attend_back(1, (k0, k1, k2))
    finish_out(1)
    product(red3, 1, joined_rows, lambda: wq[...].reshape(D, -1))
    red3[1].s1()
    each([l_mixed, l_first, l_tok, l_hg, l_gd], "wait")
    flat_j = joined[...].reshape(2 * rows, -1)
    flat_m = mixed[...].reshape(2 * rows, -1)
    n_d = max(256, gl.shape[1])

    def late(b, carry):
        at = pl.ds(pl.multiple_of(b * n_d, n_d), n_d)
        x = first[:, :, :, :, :, at].reshape(2 * rows, n_d)
        y = full[:, :, :, :, :, at].reshape(2 * rows, n_d)
        gq = tn(x, flat_j).astype(BF)
        go = tn(y, flat_m).astype(BF)
        if gl.shape[1] == n_d:
            gl[b, :, 0:384] = gq
            gl[b, :, 384:512] = go
        else:
            blk = n_d // gl.shape[1]
            gl[pl.ds(b * blk, blk), :, 0:384] = gq.reshape(blk, gl.shape[1], 384)
            gl[pl.ds(b * blk, blk), :, 384:512] = go.reshape(blk, gl.shape[1], 128)
        return carry

    lax.fori_loop(0, D // n_d, late, 0)
    collect_l.start()
    red3[1].s2()

    def norm4(m):
        grad = red3[m].s4()
        hat, inv = norm_stats(tok[m].reshape(-1, D).astype(F32))
        new = hg[m] + norm_back(grad, hat, inv, gains[0:1, :])
        grow[m] = new.astype(BF).reshape(grow.shape[1:])
        ret_g.start(m)
        return jnp.sum(grad * hat, axis=0, keepdims=True)

    gain1 = norm4(0)
    red3[1].s3()
    collect_g.total(accg)
    ssend[:, :, 0:ng] = accg[...].astype(BF).reshape(4, -1, ng)
    ssend[:, :, ng:] = gd[...].reshape(4, -1, hp)
    swap.start()
    collect_l.relay()
    gain1 = gain1 + norm4(1)
    row = lax.broadcasted_iota(jnp.int32, gain2.shape, 0)
    gt[0] = jnp.where(row == 0, gain1, jnp.where(row == 1, gain2[...], 0.0))
    s0.start()
    ret_o.wait()
    s0.wait_recv()
    gp[c] = gt[0] + gt[1]
    each(gps, "start")
    collect_l.total(accl)
    slate[...] = accl[...].astype(BF).reshape(4, -1, nl)
    swap_late.start()
    each(gps, "wait_recv")
    gz[f] = jnp.sum(gp[...], axis=0)
    each(gzs, "start")
    swap.keep()
    swap_late.keep()
    ret_g.wait()
    ret_o.end()

    def unpack(dst, back, other):
        for s in range(n_f):
            dst[t, s] = back[owners[t, s]]
            dst[1 - t, s] = other[owners[1 - t, s]]

    unpack(out_o, oback, oother)
    each(gzs, "wait_recv")
    gain_o[...] = jnp.sum(gz[...], axis=0)
    ret_g.end()
    unpack(grad_o, gback, gother)
    swap.wait()
    swap_late.wait()
    each([s0] + gps + gzs, "wait_send")
    for x in g3 + red3 + [collect_g, collect_l, swap, swap_late]:
        x.end()


def rope_tables(rows):
    lane = jnp.arange(128, dtype=jnp.int32)
    exponent = (2 * (lane % (HEAD_DIM // 2))).astype(F32)
    inverse = rope_base ** (-exponent / HEAD_DIM)
    sign = jnp.where(lane % HEAD_DIM < HEAD_DIM // 2, -1.0, 1.0)
    fine = jnp.arange(32, dtype=jnp.int32)
    coarse = fine * (rows // 32)
    both = jnp.stack([coarse, fine]).astype(F32)[:, :, None] * inverse[None, None, :]
    cos, sin = jnp.cos(both), jnp.sin(both)
    return jnp.stack([cos[0], sin[0], cos[1], sin[1], jnp.broadcast_to(sign, cos[0].shape)])


def per_device(n_f, n_c, n_t, tokens, cotangent, lengths, owners,
               norm_attn, norm_mlp, w_qkv, w_out, w_in, w_down):
    f, c, t = here()
    micro, seqs, _, piece, _ = tokens.shape
    span = piece * n_f
    half = span // 4
    rows = span * n_c
    assert n_c == 4 and n_t == 2 and micro == 2 and seqs == n_f and rows == 1024
    n_h = n_f // 2
    wr = w_qkv.shape[0]
    hid = w_in.shape[2]
    hp = -(-hid // (n_c * 128)) * 128
    heads = w_qkv.shape[2] // n_c
    wb = n_c * wr

    slots = jnp.arange(n_f, dtype=jnp.int32)
    same = owners[:, :, None] == slots[None, None, :]
    order = jnp.sum(jnp.where(same, slots[None, :, None], 0), axis=1, dtype=jnp.int32)
    place = (f * n_c + c) * wr
    gains_own = jnp.stack([norm_attn, norm_mlp]).astype(F32)
    gains_row = lax.dynamic_update_slice(jnp.zeros((8, D), F32), gains_own, (0, place))

    def quarters(a):
        return a.transpose(2, 0, 1, 3).reshape(n_c, wr, -1)

    more = n_c * hp - hid
    p_qkv = quarters(w_qkv.reshape(wr, 3, n_c, heads))
    p_out = w_out.reshape(n_c, heads, wr).transpose(0, 2, 1)
    p_in = quarters(jnp.pad(w_in, [(0, 0), (0, 0), (0, more)]).reshape(wr, 2, n_c, hp))
    p_down = jnp.pad(w_down, [(0, more), (0, 0)]).reshape(n_c, hp, wr).transpose(0, 2, 1)
    n_q = 3 * heads
    small = rope_tables(rows)

    full_shape = (micro, n_c, 2, 2, half, D)
    own_shape = (micro, n_h, piece, D)
    row_shape = (micro, 2 * half, D)
    head_shape = (micro, rows, 128)
    act_shape = (micro, n_c, span, hp)
    stat_shape, wide_shape = (micro, 8, rows), (micro, 128, rows)
    V = pltpu.VMEM
    w_shapes = [(n_f, n_c, wr, n) for n in (n_q, heads, 2 * hp, hp)]
    send = (micro, n_f, piece, D // 2)
    (gains, tok, hidden, wq, wo, w3, q, k, v, mixed, out_t, lse, first, act, hg, attn, gain2, g_in,
     g_down) = comm_call(
        functools.partial(front_kernel, n_f),
        [(shaped((8, D), F32), vm())]
        + [
            (shaped(a, d), hb())
            for a, d in (
                (own_shape, BF), (row_shape, F32), (w_shapes[0], BF), (w_shapes[1], BF),
                (w_shapes[3], BF), (head_shape, BF), (head_shape, BF), (head_shape, BF),
                (head_shape, BF), (wide_shape, F32), (stat_shape, F32), (full_shape, BF),
                (act_shape, BF),
            )
        ]
        + [
            (shaped(row_shape, F32), vm()), (shaped((micro, 2, half, D), BF), vm()),
            (shaped((8, D), F32), vm()), (shaped((D, 2 * hp), BF), vm()),
            (shaped((wb, hp), BF), vm()),
        ],
        [sm(), sm()] + [vm()] * 8,
        [V(own_shape, BF), V(own_shape, BF), V(row_shape, F32)]
        + [V(a, BF) for a in w_shapes]
        + [V(head_shape, BF)] * 4
        + [V(wide_shape, F32), V(stat_shape, F32), V(act_shape, BF)]
        + [
            V(send, BF), V(send, BF), V((n_f, 8, D), F32), V((n_c, 8, D), F32),
            V(full_shape, BF), V(full_shape, BF), V(full_shape, BF),
            V((micro, n_c, span, 2 * hp), BF), V((n_f, wb, hp), BF),
            V((collect_slots(n_f), wb, hp), BF), V((wb, hp), F32),
        ]
        + reduce_scratch(half)
        + [V((128, rows), BF), V((2, rows, 128), F32)],
        6 * n_f + 160, 16, 0, 10**10,
    )(order, lengths, tokens[:, :, 0], cotangent[:, :, 0], gains_row, p_qkv, p_out, p_in, p_down,
      small)

    outs, grads, gain_grads, early, late = comm_call(
        functools.partial(third_kernel, n_f),
        [
            (shaped((micro, n_f, piece, D), BF), vm()), (shaped((micro, n_f, piece, D), BF), vm()),
            (shaped((8, D), F32), vm()), (shaped((n_c, wr, 3 * hp), BF), vm()),
            (shaped((n_c, wr, n_q + heads), BF), vm()),
        ],
        [sm(), sm(), vm()] + [hb()] * 14 + [vm()] * 3 + [hb(), vm()],
        [V(w_shapes[1], BF), V(w_shapes[0], BF), V(w_shapes[3], BF), V(act_shape, BF)]
        + [V(head_shape, BF)] * 4
        + [V(wide_shape, F32), V(stat_shape, F32), V(row_shape, F32), V(row_shape, F32),
           V(own_shape, BF), V((wb, hp), BF), V((2, rows, 128), F32)]
        + [
            V(full_shape, BF), V(full_shape, BF), V((rows, 128), F32), V((rows, 128), F32),
            V((128, rows), F32), V((rows, 128), BF), V((8, rows), F32), V((128, rows), BF),
            V((micro, rows, 384), BF),
        ]
        + reduce_scratch(half)
        + reduce_scratch(half)[1:]
        + [
            V((n_f, wb, n_q + heads), BF),
            V((collect_slots(n_f), wb, n_q + heads), BF), V((collect_slots(n_f), wb, 2 * hp), BF),
            V((wb, n_q + heads), F32), V((wb, 2 * hp), F32),
            V((n_c, wr, 3 * hp), BF), V((n_c, wr, n_q + heads), BF),
            V(own_shape, BF), V(own_shape, BF),
            V((n_f, piece, D), BF), V((n_f, piece, D), BF),
            V((n_f, piece, D), BF), V((n_f, piece, D), BF),
            V((n_f, 8, D), F32), V((n_c, 8, D), F32), V((2, 8, D), F32),
        ],
        6 * n_f + 100, 16, 1, 10**10,
    )(owners, lengths, attn, wo, wq, w3, act, q, k, v, mixed, out_t, lse, first, hg, hidden, tok,
      gains, gain2, g_in.reshape(n_f, wb, 2 * hp), g_down, small)

    grad_qkv = late[:, :, :n_q].astype(F32).reshape(n_c, wr, 3, heads).transpose(1, 2, 0, 3)
    grad_qkv = grad_qkv.reshape(wr, 3, n_c * heads)
    grad_out = late[:, :, n_q:].astype(F32).transpose(0, 2, 1).reshape(n_c * heads, wr)
    grad_in = early[:, :, : 2 * hp].astype(F32).reshape(n_c, wr, 2, hp)
    grad_in = grad_in.transpose(1, 2, 0, 3).reshape(wr, 2, n_c * hp)[..., :hid]
    grad_down = early[:, :, 2 * hp :].astype(F32).transpose(0, 2, 1).reshape(n_c * hp, wr)[:hid]
    mine = lax.dynamic_slice(gain_grads, (0, place), (2, wr))
    return (outs[:, :, None], grads[:, :, None], mine[0], mine[1],
            grad_qkv, grad_out, grad_in, grad_down)


def solution(mesh):
    rows = P(None, None, "ctx", "fsdp", None)
    gain = P(("fsdp", "ctx"))
    tall = P(("fsdp", "ctx"), None, "tp")
    wide = P("tp", ("fsdp", "ctx"))
    return jax.shard_map(
        functools.partial(per_device, mesh.shape["fsdp"], mesh.shape["ctx"], mesh.shape["tp"]),
        mesh=mesh,
        in_specs=(rows, rows, P(), P(), gain, gain, tall, wide, tall, wide),
        out_specs=(rows, rows, gain, gain, tall, wide, tall, wide),
        check_vma=False,
    )
```

```python
import functools

import jax
import jax.numpy as jnp
from jax import lax
from jax.experimental import pallas as pl
from jax.experimental.pallas import tpu as pltpu
from jax.sharding import PartitionSpec as P

D = 1024
HEAD_DIM = 64
norm_eps = 1e-05
rope_base = 160000.0
masked_score = -1e30
MESH = pl.DeviceIdType.MESH
BF = jnp.bfloat16
F32 = jnp.float32
VLIMIT = 56 << 20


def nn(a, b):
    return lax.dot_general(a, b, (((1,), (0,)), ((), ())), preferred_element_type=F32)


def nt(a, b):
    return lax.dot_general(a, b, (((1,), (1,)), ((), ())), preferred_element_type=F32)


def tn(a, b):
    return lax.dot_general(a, b, (((0,), (0,)), ((), ())), preferred_element_type=F32)


def norm_stats(values):
    center = values - jnp.mean(values, axis=-1, keepdims=True)
    spread = jnp.mean(center * center, axis=-1, keepdims=True)
    inverse_std = lax.rsqrt(spread + norm_eps)
    return center * inverse_std, inverse_std


def norm_back(upstream, normed, inverse_std, gain):
    scaled = upstream * gain
    adjusted = (
        scaled
        - jnp.mean(scaled, axis=-1, keepdims=True)
        - normed * jnp.mean(scaled * normed, axis=-1, keepdims=True)
    )
    return adjusted * inverse_std


def here():
    return lax.axis_index("fsdp"), lax.axis_index("ctx"), lax.axis_index("tp")


def remote(src, dst, sems, i, where, j=None):
    return pltpu.make_async_remote_copy(
        src_ref=src,
        dst_ref=dst,
        send_sem=sems.at[0, i],
        recv_sem=sems.at[1, i if j is None else j],
        device_id=where,
        device_id_type=MESH,
    )


def greet(peers):
    bar = pltpu.get_barrier_semaphore()
    for p in peers:
        pl.semaphore_signal(bar, inc=1, device_id=p, device_id_type=MESH)
    pl.semaphore_wait(bar, len(peers))


class Ids:
    def __init__(self):
        self.next = 0

    def take(self, count):
        self.next += count
        return self.next - count


def each(copies, what):
    for copy in copies:
        getattr(copy, what)()


class Gather:
    def __init__(self, full, m, sems, ids):
        f, c, t = here()
        px, py, po = (f, c ^ 1, t), (f, c ^ 2, t), (f, c, 1 - t)
        cx, cy, cd = c ^ 1, c ^ 2, c ^ 3
        base = ids.take(10)

        def cp(i, view, where):
            return remote(view, view, sems, base + i, where)

        self.bx = cp(0, full.at[m, c, t, 1], px)
        self.ay = cp(1, full.at[m, c, t, 0], py)
        self.ax = cp(2, full.at[m, c, t, 0], px)
        self.by = cp(3, full.at[m, c, t, 1], py)
        self.oo = cp(4, full.at[m, c, t], po)
        self.fy = cp(5, full.at[m, cx, t, 1], py)
        self.fx = cp(6, full.at[m, cy, t, 0], px)
        self.ox = cp(7, full.at[m, cx, t], po)
        self.oy = cp(8, full.at[m, cy, t], po)
        self.od = cp(9, full.at[m, cd, t], po)

    def s0(self):
        each([self.bx, self.ay, self.ax, self.by, self.oo], "start")

    def s1(self):
        self.bx.wait_recv()
        self.fy.start()
        self.ay.wait_recv()
        self.fx.start()

    def s2(self):
        self.ax.wait_recv()
        self.ox.start()
        self.by.wait_recv()
        self.oy.start()

    def s3(self):
        self.fy.wait_recv()
        self.fx.wait_recv()
        self.od.start()

    def s4(self):
        each([self.oo, self.ox, self.oy, self.od], "wait_recv")

    def rest(self):
        self.s2()
        self.s3()
        self.s4()

    def end(self):
        each(
            [self.bx, self.ay, self.ax, self.by, self.oo, self.fy, self.fx, self.ox, self.oy,
             self.od],
            "wait_send",
        )


class Reduce:
    def __init__(self, part, r0, rx, ry, sems, ids):
        f, c, t = here()
        px, py, self.po = (f, c ^ 1, t), (f, c ^ 2, t), (f, c, 1 - t)
        cx, cy, cd = c ^ 1, c ^ 2, c ^ 3
        self.base = ids.take(10)
        self.part, self.r0, self.rx, self.ry, self.sems = part, r0, rx, ry, sems
        self.own, self.t, self.cx, self.cy, self.cd = c, t, cx, cy, cd

        def cp(i, src, dst, where):
            return remote(src, dst, sems, self.base + i, where)

        self.cross = [self.crossing(i) for i in range(4)]
        self.a0 = cp(4, part.at[cd, t, 0], rx.at[0], px)
        self.b0 = cp(5, part.at[cd, t, 1], ry.at[0], py)
        self.a1 = cp(6, part.at[cx, t, 0], rx.at[1], px)
        self.b1 = cp(7, part.at[cy, t, 1], ry.at[1], py)
        self.b2 = cp(8, part.at[cy, t, 0], ry.at[2], py)
        self.a2 = cp(9, part.at[cx, t, 1], rx.at[2], px)

    def span(self, i):
        return self.own ^ (3 - i - jnp.where(jnp.int32(i) == 1, 1, 0) + jnp.where(jnp.int32(i) == 2, 1, 0))

    def crossing(self, i):
        return remote(
            self.part.at[self.span(i), 1 - self.t], self.r0.at[i], self.sems, self.base + i, self.po
        )

    def add(self, i, span):
        self.cross[i].wait_recv()
        part, t = self.part, self.t
        part[span, t] = (part[span, t].astype(F32) + self.r0[i].astype(F32)).astype(BF)

    def s1(self):
        self.add(0, self.cd)
        self.a0.start()
        self.b0.start()

    def s2(self):
        self.add(1, self.cx)
        self.a1.start()
        self.add(2, self.cy)
        self.b1.start()

    def s3(self):
        part, t = self.part, self.t
        self.a0.wait_recv()
        part[self.cy, t, 0] = (part[self.cy, t, 0].astype(F32) + self.rx[0].astype(F32)).astype(BF)
        self.b2.start()
        self.b0.wait_recv()
        part[self.cx, t, 1] = (part[self.cx, t, 1].astype(F32) + self.ry[0].astype(F32)).astype(BF)
        self.a2.start()

    def s4(self):
        self.cross[3].wait_recv()
        own = self.part[self.own, self.t].astype(F32) + self.r0[3].astype(F32)
        each([self.a1, self.b1, self.b2, self.a2], "wait_recv")
        top = own[0] + self.rx[1].astype(F32) + self.ry[2].astype(F32)
        bottom = own[1] + self.ry[1].astype(F32) + self.rx[2].astype(F32)
        return jnp.concatenate([top, bottom], axis=0)

    def end(self):
        each(self.cross + [self.a0, self.b0, self.a1, self.b1, self.b2, self.a2], "wait_send")


def reduce_scratch(half):
    return [
        pltpu.VMEM((2, 4, 2, 2, half, D), BF),
        pltpu.VMEM((2, 4, 2, half, D), BF),
        pltpu.VMEM((2, 3, half, D), BF),
        pltpu.VMEM((2, 3, half, D), BF),
    ]


class Spread:
    def __init__(self, ref, n_f, sems, ids):
        f, c, t = here()
        self.f, self.n_f = f, n_f
        if n_f == 4:
            base = ids.take(6)
            up, down = (lax.rem(f + 1, n_f), c, t), (lax.rem(f + n_f - 1, n_f), c, t)
            self.up, self.down = [], []
            for k in range(3):
                low, high = ref.at[lax.rem(f - k + n_f, n_f)], ref.at[lax.rem(f + k, n_f)]
                self.up.append(remote(low, low, sems, base + k, up))
                self.down.append(remote(high, high, sems, base + 3 + k, down))
        else:
            base = ids.take(1)
            self.copies = [
                remote(ref.at[f], ref.at[f], sems, base, (lax.rem(f + k, n_f), c, t))
                for k in range(1, n_f)
            ]
            most = ref.at[pl.ds(0, n_f - 1)]
            self.all = remote(most, most, sems, base, (f, c, 1 - t))

    def sends_up(self, k):
        return (self.f >= k) & (self.f <= 2)

    def sends_down(self, k):
        return (self.f <= 3 - k) & (self.f >= 1)

    def start(self):
        if self.n_f != 4:
            return each(self.copies, "start")
        pl.when(self.sends_up(0))(self.up[0].start)
        pl.when(self.sends_down(0))(self.down[0].start)

    def arrive(self, k):
        pl.when(self.f >= k + 1)(self.up[k].wait_recv)
        pl.when(self.f <= 2 - k)(self.down[k].wait_recv)

    def step(self, k):
        if self.n_f != 4:
            return
        self.arrive(k - 1)
        pl.when(self.sends_up(k))(self.up[k].start)
        pl.when(self.sends_down(k))(self.down[k].start)

    def wait(self):
        if self.n_f != 4:
            return self.all.wait_recv()
        self.arrive(2)

    def end(self):
        if self.n_f != 4:
            return self.all.wait_send()
        for k in range(3):
            pl.when(self.sends_up(k))(self.up[k].wait_send)
            pl.when(self.sends_down(k))(self.down[k].wait_send)


class Collect:
    def __init__(self, ref, got, n_f, sems, ids, passed=True):
        f, c, t = here()
        n_f = n_f if passed or n_f != 4 else -n_f
        self.f, self.n_f, self.ref, self.got = f, n_f, ref, got
        if n_f == 4:
            base = ids.take(5)
            self.steps = (-1, -2, 1, 2)
            self.copies = []
            for i, d in enumerate(self.steps):
                j = lax.rem(f - d + n_f, n_f)
                self.copies.append(remote(ref.at[j], got.at[i], sems, base + i, (j, c, t)))
            away = jnp.where(f == 0, 3, 0)
            self.far = remote(
                ref.at[away], got.at[4], sems, base + 4, (jnp.where(f == 0, 1, 2), c, t)
            )
        else:
            base = ids.take(1)
            self.copies = []
            n_f = abs(n_f)
            for k in range(1, n_f):
                j = lax.rem(f + k, n_f)
                self.copies.append(remote(ref.at[j], got.at[k - 1], sems, base, (j, c, t)))
            most = ref.at[pl.ds(0, n_f - 1)]
            self.all = remote(most, got.at[pl.ds(0, n_f - 1)], sems, base, (f, c, 1 - t))

    def there(self, d):
        return (self.f - d >= 0) & (self.f - d < 4)

    def late(self, d):
        if d == 2:
            return self.f == 2
        if d == -2:
            return self.f == 1
        return self.f < 0

    def start(self):
        if self.n_f != 4:
            return each(self.copies, "start")
        pl.when((self.f == 0) | (self.f == 3))(self.far.start)
        for d, cp in zip(self.steps, self.copies):
            pl.when(self.there(d) & ~self.late(d))(cp.start)

    def relay(self):
        if self.n_f != 4:
            return
        for d, cp, j in ((2, self.copies[3], 0), (-2, self.copies[1], 3)):

            @pl.when(self.late(d))
            def _():
                self.far.wait_recv()
                self.ref[j] = (self.ref[j].astype(F32) + self.got[4].astype(F32)).astype(BF)
                cp.start()

    def total(self, acc):
        acc[...] = self.ref[self.f].astype(F32)
        if self.n_f != 4:
            self.all.wait_recv()
            for k in range(abs(self.n_f) - 1):
                acc[...] += self.got[k].astype(F32)
            return
        for i, d in enumerate(self.steps):

            @pl.when((self.f + d >= 0) & (self.f + d < 4))
            def _():
                self.copies[i].wait_recv()
                acc[...] += self.got[i].astype(F32)

    def end(self):
        if self.n_f != 4:
            return self.all.wait_send()
        for d, cp in zip(self.steps, self.copies):
            pl.when(self.there(d))(cp.wait_send)
        pl.when((self.f == 0) | (self.f == 3))(self.far.wait_send)


def collect_slots(n_f):
    return 5 if n_f == 4 else n_f - 1


class Deal:
    def __init__(self, stage, own, n_f, sems, ids):
        f, c, t = here()
        n_h = n_f // 2
        self.base = ids.take(2 * n_f)
        self.f, self.t, self.n_f, self.n_h, self.own, self.sems = f, t, n_f, n_h, own, sems
        self.side, at = f // n_h, lax.rem(f, n_h)
        self.mine = self.side == t
        self.moves = []
        for m in range(2):
            dst = self.piece(m, at, t)
            recv = self.base + (m * n_h + at) * 2 + t
            sent = self.base + m * n_f
            away = [
                remote(stage.at[m, lax.rem(f + k, n_f)], dst, sems, sent + k,
                       (lax.rem(f + k, n_f), c, self.side), recv)
                for k in range(1, n_f)
            ]
            over = remote(stage.at[m, f], dst, sems, sent, (f, c, 1 - t), recv)
            keep = pltpu.make_async_copy(stage.at[m, f], dst, sems.at[1, recv])
            self.moves.append((away, over, keep))

    def piece(self, m, j, core):
        wide = D // 2
        return self.own.at[m, j, :, pl.ds(pl.multiple_of(core * wide, wide), wide)]

    def start(self, m):
        away, over, keep = self.moves[m]
        each(away, "start")
        pl.when(self.mine)(keep.start)
        pl.when(~self.mine)(over.start)

    def wait(self, m):
        f, c, t = here()
        for j in range(self.n_h):
            for core in range(2):
                i = self.base + (m * self.n_h + j) * 2 + core
                view = self.piece(m, j, core)
                local = (t == core) & (f == t * self.n_h + j)
                pl.when(local)(pltpu.make_async_copy(view, view, self.sems.at[1, i]).wait)
                pl.when(~local)(remote(view, view, self.sems, i, (f, c, 1 - t)).wait_recv)

    def end(self):
        for away, over, _ in self.moves:
            each(away, "wait_send")
            pl.when(~self.mine)(over.wait_send)


class Return:
    def __init__(self, own, back, other, n_f, sems, ids):
        f, c, t = here()
        n_h = n_f // 2
        self.base = ids.take(2 * n_f + 1)
        self.f, self.t, self.n_f, self.back, self.sems = f, t, n_f, back, sems
        self.moves = []
        for m in range(2):
            for j in range(n_h):
                to = t * n_h + j
                i = self.base + m * n_h + j
                far = remote(own.at[m, j], back.at[f], sems, i, (to, c, m), self.base + f)
                keep = pltpu.make_async_copy(own.at[m, j], back.at[f], sems.at[1, self.base + f])
                self.moves.append((m, (to == f) & (t == m), far, keep))
        self.swap = remote(back, other, sems, self.base + 2 * n_f, (f, c, 1 - t))

    def start(self, m):
        for which, local, far, keep in self.moves:
            if which == m:
                pl.when(local)(keep.start)
                pl.when(~local)(far.start)

    def wait(self):
        n_h = self.n_f // 2
        f, c, t = here()
        for s in range(self.n_f):
            local = (f == s) & (f // n_h == t)
            view = self.back.at[s]
            i = self.base + s
            pl.when(local)(pltpu.make_async_copy(view, view, self.sems.at[1, i]).wait)
            pl.when(~local)(remote(view, view, self.sems, i, (f, c, 1 - t)).wait_recv)
        self.swap.start()

    def end(self):
        self.swap.wait_recv()
        for _, local, far, _ in self.moves:
            pl.when(~local)(far.wait_send)
        self.swap.wait_send()


class Swap:
    def __init__(self, src, dst, sems, ids):
        f, c, t = here()
        base = ids.take(3)
        self.src, self.dst, self.c = src, dst, c
        self.copies = [
            remote(src.at[c ^ k], dst.at[c], sems, base + k - 1, (f, c ^ k, t)) for k in (1, 2, 3)
        ]

    def start(self):
        each(self.copies, "start")

    def keep(self):
        self.dst[self.c] = self.src[self.c]

    def wait(self):
        each(self.copies, "wait_recv")

    def end(self):
        each(self.copies, "wait_send")


def everyone(n_f):
    f, c, t = here()
    peers = [(f, c ^ 1, t), (f, c ^ 2, t), (f, c ^ 3, t), (f, c, 1 - t)]
    for k in range(1, n_f):
        for core in range(2):
            peers.append((lax.rem(f + k, n_f), c, core))
    return peers


def vm():
    return pl.BlockSpec(memory_space=pltpu.VMEM)


def sm():
    return pl.BlockSpec(memory_space=pltpu.SMEM)


def hb():
    return pl.BlockSpec(memory_space=pl.ANY)


def shaped(shape, dtype):
    return jax.ShapeDtypeStruct(shape, dtype)


def comm_call(kernel, outs, ins, scratch, n_sems, n_local, cid, flops):
    return pl.pallas_call(
        kernel,
        out_shape=[s for s, _ in outs],
        in_specs=ins,
        out_specs=[b for _, b in outs],
        scratch_shapes=scratch
        + [pltpu.SemaphoreType.DMA((2, n_sems)), pltpu.SemaphoreType.DMA((n_local,))],
        compiler_params=pltpu.CompilerParams(
            collective_id=cid, has_side_effects=True, vmem_limit_bytes=VLIMIT
        ),
        cost_estimate=pl.CostEstimate(flops=flops, bytes_accessed=1 << 20, transcendentals=0),
    )


def rotate(u, cos, sin, sign):
    lane = lax.broadcasted_iota(jnp.int32, u.shape, 1)
    partner = jnp.where(lane % HEAD_DIM < HEAD_DIM // 2, pltpu.roll(u, 96, 1), pltpu.roll(u, 32, 1))
    return u * cos + partner * (sin * sign)


class Keep:
    def __init__(self, sems):
        self.sems, self.copies = sems, []

    def move(self, src, dst):
        copy = pltpu.make_async_copy(src, dst, self.sems.at[len(self.copies)])
        copy.start()
        self.copies.append(copy)
        return copy


def table(small, dst):
    fine_cos, fine_sin = small[2], small[3]
    steps = fine_cos.shape[0]
    for i in range(dst.shape[1] // steps):
        coarse_cos, coarse_sin = small[0, i : i + 1, :], small[1, i : i + 1, :]
        at = pl.ds(i * steps, steps)
        dst[0, at, :] = coarse_cos * fine_cos - coarse_sin * fine_sin
        dst[1, at, :] = (coarse_sin * fine_cos + coarse_cos * fine_sin) * small[4]


def front_kernel(
    n_f, order, lengths, tok, cot, gains, pq, po, p2, p3, small,
    gains_o, tok_h, hidden_h, wq_h, wo_h, w3_h, q_h, k_h, v_h, mixed_h, out_h, lse_h, first_h,
    act_h, hg_o, attn_o, gain_o, gi_o,
    tok_o, cot_o, hidden_o, wq, wo, w2, w3, q_o, k_o, v_o, mixed_o, out_o, lse_o, act_o,
    stage, scot, gz, gp, first, cotf, full, gg, part, r0, rx, ry, v_t, turn,
    sems, lsem,
):
    f, c, t = here()
    ids = Ids()
    plane = [(f, c ^ k, t) for k in (1, 2, 3)]
    zs = [(lax.rem(f + k, n_f), c, t) for k in range(1, n_f)]
    half = first.shape[4]
    rows = 16 * half
    hp = w3.shape[3]
    wide = D // 2

    deal_tok = Deal(stage, tok_o, n_f, sems, ids)
    deal_cot = Deal(scot, cot_o, n_f, sems, ids)
    base = ids.take(n_f - 1)
    gs = [remote(gains, gz.at[f], sems, base + k, zs[k]) for k in range(n_f - 1)]
    base = ids.take(3)
    gps = [remote(gp.at[c], gp.at[c], sems, base + k, plane[k]) for k in range(3)]
    swaps = [Swap(src, w.at[f], sems, ids)
             for src, w in ((pq, wq), (po, wo), (p2, w2), (p3, w3))]
    spreads = [Spread(w, n_f, sems, ids) for w in (wq, wo, w2, w3)]
    g1, gc, g2 = ([Gather(x, m, sems, ids) for m in range(2)] for x in (first, cotf, full))
    red1, red2 = (
        [Reduce(part.at[m], r0.at[m], rx.at[m], ry.at[m], sems, ids) for m in range(2)]
        for _ in range(2)
    )
    keep = Keep(lsem)
    mine = pl.ds(pl.multiple_of(t * wide, wide), wide)

    def stage_rows(src, dst, m):
        for j in range(n_f):
            dst[m, j] = src[m, order[m, j], :, mine]

    stage_rows(tok, stage, 0)
    greet(everyone(n_f))
    deal_tok.start(0)
    each(gs, "start")
    each(swaps[:2], "start")
    stage_rows(tok, stage, 1)
    deal_tok.start(1)
    each(swaps[2:], "start")
    each(swaps, "keep")
    gz[f] = gains[...]
    stage_rows(cot, scot, 0)
    stage_rows(cot, scot, 1)
    table(small, turn)
    each(gs, "wait_recv")
    gp[c] = jnp.sum(gz[...], axis=0)
    each(gps, "start")

    def norm1(m):
        deal_tok.wait(m)
        hat, _ = norm_stats(tok_o[m].reshape(-1, D).astype(F32))
        first[m, c, t] = (hat * gains_o[0:1, :]).astype(BF).reshape(2, half, D)

    each(gps, "wait_recv")
    gains_o[...] = jnp.sum(gp[...], axis=0)
    norm1(0)
    g1[0].s0()
    swaps[0].wait()
    norm1(1)
    spreads[0].start()
    g1[0].s1()
    g1[1].s0()
    spreads[0].step(1)
    swaps[1].wait()
    spreads[1].start()
    g1[0].s2()
    g1[0].s3()
    spreads[0].step(2)
    deal_cot.start(0)
    deal_cot.start(1)
    g1[0].s4()
    spreads[1].step(1)
    spreads[0].wait()
    g1[1].s1()

    def attend(m, hooks):
        joined = nn(first[m].reshape(rows, D), wq[...].reshape(D, -1))
        q_o[m] = rotate(joined[:, 0:128], turn[0], turn[1], 1.0).astype(BF) * BF(0.125)
        k_o[m] = rotate(joined[:, 128:256], turn[0], turn[1], 1.0).astype(BF)
        v = joined[:, 256:384]
        v_o[m] = v.astype(BF)
        v_t[...] = v.T.astype(BF)
        lane = lax.broadcasted_iota(jnp.int32, (rows, 128), 1)
        alive = lax.broadcasted_iota(jnp.int32, (rows, rows), 0) < lengths[m, f]

        def head(h, carry):
            at = pl.ds(pl.multiple_of(h * HEAD_DIM, HEAD_DIM), HEAD_DIM)
            qh = jnp.where(lane // HEAD_DIM == h, q_o[m], BF(0.0))
            s = jnp.where(alive, nt(k_o[m], qh), masked_score)
            top = jnp.max(s, axis=0, keepdims=True)
            p = jnp.exp(s - top)
            total = jnp.sum(p, axis=0, keepdims=True)
            out_o[m, at, :] = nn(v_t[at, :], p.astype(BF)) / total
            lse_o[m, pl.ds(h, 1), :] = top + jnp.log(total)
            for i, hook in enumerate(hooks):
                pl.when(h == i)(hook)
            return carry

        lax.fori_loop(0, 2, head, 0)
        mixed_o[m] = out_o[m].T.astype(BF)

    def product(m):
        def step(i, carry):
            span = red1[m].span(i)
            block = mixed_o[m, pl.ds(pl.multiple_of(span * 4 * half, 4 * half), 4 * half), :]
            part[m, span] = nt(block, wo[...].reshape(D, -1)).astype(BF).reshape(2, 2, half, D)
            red1[m].crossing(i).start()
            return carry

        lax.fori_loop(0, 4, step, 0)

    def norm2(m):
        hidden = tok_o[m].reshape(-1, D).astype(F32) + red1[m].s4()
        hidden_o[m] = hidden
        hat, _ = norm_stats(hidden)
        full[m, c, t] = (hat * gains_o[1:2, :]).astype(BF).reshape(2, half, D)
        g2[m].s0()

    def hook0():
        g1[1].s2()
        spreads[1].step(2)

    attend(0, (hook0, g1[1].s3))
    spreads[1].wait()
    product(0)
    g1[1].s4()
    swaps[2].wait()
    swaps[3].wait()
    spreads[2].start()
    spreads[3].start()
    for src, dst in ((first, first_h), (tok_o, tok_h), (wq, wq_h), (wo, wo_h)):
        keep.move(src, dst)
    red1[0].s1()

    def hook1():
        red1[0].s2()

    def hook2():
        red1[0].s3()
        deal_cot.wait(0)
        cotf[0, c, t] = cot_o[0].reshape(2, half, D)

    attend(1, (hook1, hook2))
    product(1)
    gc[0].s0()
    red1[1].s1()
    deal_cot.wait(1)
    cotf[1, c, t] = cot_o[1].reshape(2, half, D)
    norm2(0)
    red1[1].s2()
    spreads[2].step(1)
    spreads[3].step(1)
    red1[1].s3()
    gc[0].s1()
    gc[1].s0()
    g2[0].s1()
    norm2(1)
    spreads[2].step(2)
    spreads[3].step(2)
    gc[0].s2()
    g2[0].s2()
    gc[0].s3()
    g2[0].s3()
    g2[1].s1()
    gc[1].s1()
    for m in range(2):
        red1[m].end()
    for src, dst in ((q_o, q_h), (k_o, k_h), (v_o, v_h), (mixed_o, mixed_h), (out_o, out_h),
                     (lse_o, lse_h), (hidden_o, hidden_h)):
        keep.move(src, dst)
    gc[0].s4()
    g2[0].s4()
    spreads[2].wait()
    spreads[3].wait()
    keep.move(w3, w3_h)

    def mlp(m, hooks):
        def step(i, carry):
            span = red2[m].span(i)
            low = full[m, span].reshape(4 * half, D)
            win = w2[...].reshape(D, 2 * hp)
            u = nn(low, win[:, :hp])
            g = nn(low, win[:, hp:])
            a = nn(cotf[m, span].reshape(4 * half, D), w3[...].reshape(D, hp))
            phi = 0.5 * (1.0 + lax.erf(u * 0.7071067811865476))
            gelu = u * phi
            slope = phi + u * (jnp.exp(-0.5 * u * u) * 0.3989422804014327)
            act_o[m, span] = (gelu * g).astype(BF)
            gg[m, span, :, 0:hp] = (a * g * slope).astype(BF)
            gg[m, span, :, hp:] = (a * gelu).astype(BF)
            part[m, span] = nt(gg[m, span], win).astype(BF).reshape(2, 2, half, D)
            red2[m].crossing(i).start()
            for j, hook in enumerate(hooks):
                pl.when(i == j)(hook)
            return carry

        lax.fori_loop(0, 4, step, 0)

    def rest2():
        gc[1].s2()
        g2[1].s2()

    def rest3():
        gc[1].s3()
        g2[1].s3()

    mlp(0, (rest2, rest3))
    red2[0].s1()
    gc[1].s4()
    g2[1].s4()
    mlp(1, (red2[0].s2, red2[0].s3))
    red2[1].s1()
    keep.move(act_o, act_h)
    flat_act = act_o[...].reshape(2 * rows, hp)
    flat_gg = gg[...].reshape(2 * rows, 2 * hp)
    n_d = 256

    def sums(source, weight, first_column, columns):
        def step(b, carry):
            at = pl.ds(pl.multiple_of(b * n_d, n_d), n_d)
            x = source[:, :, :, :, :, at].reshape(2 * rows, n_d)
            gi_o[at, first_column : first_column + columns] = tn(x, weight).astype(BF)
            return carry

        lax.fori_loop(0, D // n_d, step, 0)

    sums(cotf, flat_act, 2 * hp, hp)
    red2[1].s2()

    def norm3(m):
        grad = red2[m].s4()
        hat, inv = norm_stats(hidden_o[m])
        hg = cot_o[m].reshape(-1, D).astype(F32) + norm_back(grad, hat, inv, gains_o[1:2, :])
        hg_o[m] = hg
        attn_o[m] = hg.astype(BF).reshape(2, half, D)
        return jnp.sum(grad * hat, axis=0, keepdims=True)

    gain = norm3(0)
    red2[1].s3()

    sums(full, flat_gg, 0, 2 * hp)
    gain = gain + norm3(1)
    gain_o[...] = jnp.broadcast_to(gain, gain_o.shape)
    each(gs + gps, "wait_send")
    for x in [deal_tok, deal_cot] + swaps + spreads + g1 + gc + g2 + red2:
        x.end()
    each(keep.copies, "wait")


def third_kernel(
    n_f, owners, lengths, attn, wo_h, wq_h, w3_h, act_h, q_h, k_h, v_h, mixed_h, out_h, lse_h,
    first_h, hg_h, hidden_h, tok_h, gains, gain2, gi, small,
    out_o, grad_o, gain_o, early_o, late_o,
    wo, wq, w3, act, q, k, v, mixed, out, lse, hg, hidden, tok, turn,
    full, first, dk, dv, dq_t, mg, delta, k_t, joined, part, r0, rx, ry, r0b, rxb, ryb,
    gl, gotl, gotg, accl, accg, ssend, slate, orow, grow, oback, gback, oother, gother, gz, gp, gt,
    sems, lsem,
):
    f, c, t = here()
    ids = Ids()
    half = full.shape[4]
    rows = 16 * half
    hp = w3.shape[3]
    nl, ng = accl.shape[1], accg.shape[1]
    plane = [(f, c ^ k_, t) for k_ in (1, 2, 3)]
    zs = [(lax.rem(f + k_, n_f), c, t) for k_ in range(1, n_f)]
    po = (f, c, 1 - t)
    g3 = [Gather(full, m, sems, ids) for m in range(2)]
    red4 = [Reduce(part.at[m], r0.at[m], rx.at[m], ry.at[m], sems, ids) for m in range(2)]
    red3 = [Reduce(part.at[m], r0b.at[m], rxb.at[m], ryb.at[m], sems, ids) for m in range(2)]
    collect_g = Collect(gi, gotg, n_f, sems, ids)
    collect_l = Collect(gl, gotl, n_f, sems, ids)
    ret_o = Return(orow, oback, oother, n_f, sems, ids)
    ret_g = Return(grow, gback, gother, n_f, sems, ids)
    swap = Swap(ssend, early_o, sems, ids)
    swap_late = Swap(slate, late_o, sems, ids)
    base = ids.take(1 + 3 + n_f - 1)
    s0 = remote(gt.at[0], gt.at[1], sems, base, po)
    gps = [remote(gp.at[c], gp.at[c], sems, base + 1 + j, plane[j]) for j in range(3)]
    gzs = [remote(gz.at[f], gz.at[f], sems, base + 4 + j, zs[j]) for j in range(n_f - 1)]
    keep = Keep(lsem)
    l_act, l_w3, l_wo, l_out, l_q, l_k, l_v, l_lse, l_hidden, l_wq, l_mixed, l_first, l_tok, l_hg = [
        keep.move(src, dst)
        for src, dst in ((act_h, act), (w3_h, w3), (wo_h, wo), (out_h, out), (q_h, q), (k_h, k),
                         (v_h, v), (lse_h, lse), (hidden_h, hidden), (wq_h, wq),
                         (mixed_h, mixed), (first_h, first), (tok_h, tok), (hg_h, hg))
    ]
    for m in range(2):
        full[m, c, t] = attn[m]
    greet(everyone(n_f))
    g3[0].s0()
    collect_g.start()

    def product(red, m, source, weight):
        def step(i, carry):
            span = red[m].span(i)
            part[m, span] = nt(source(m, span), weight()).astype(BF).reshape(2, 2, half, D)
            red[m].crossing(i).start()
            return carry

        lax.fori_loop(0, 4, step, 0)

    def act_rows(m, span):
        return act[m, span]

    def joined_rows(m, span):
        return joined[m, pl.ds(pl.multiple_of(span * 4 * half, 4 * half), 4 * half), :]

    table(small, turn)
    l_act.wait()
    l_w3.wait()
    g3[0].s1()
    g3[1].s0()
    product(red4, 0, act_rows, lambda: w3[...].reshape(D, hp))
    product(red4, 1, act_rows, lambda: w3[...].reshape(D, hp))
    g3[0].rest()
    collect_g.relay()
    each([l_wo, l_out, l_q, l_k, l_v, l_lse], "wait")
    QB = 512

    def attend_back(m, hooks):
        grad = nn(full[m].reshape(rows, D), wo[...].reshape(D, -1)).astype(BF)
        mg[...] = grad
        weighted = grad.astype(F32).T * out[m]
        delta[0:1, :] = jnp.sum(weighted[:HEAD_DIM], axis=0, keepdims=True)
        delta[1:2, :] = jnp.sum(weighted[HEAD_DIM:], axis=0, keepdims=True)
        k_t[...] = k[m].astype(F32).T.astype(BF)
        dk[...] = jnp.zeros_like(dk)
        dv[...] = jnp.zeros_like(dv)
        lane = lax.broadcasted_iota(jnp.int32, (QB, 128), 1)
        alive = lax.broadcasted_iota(jnp.int32, (rows, QB), 0) < lengths[m, f]
        n_b = rows // QB

        def block(i, carry):
            h = i // n_b
            at = pl.ds(pl.multiple_of(lax.rem(i, n_b) * QB, QB), QB)
            hs = pl.ds(pl.multiple_of(h * HEAD_DIM, HEAD_DIM), HEAD_DIM)
            keep = lane // HEAD_DIM == h
            qh = jnp.where(keep, q[m, at, :], BF(0.0))
            gh = jnp.where(keep, mg[at, :], BF(0.0))
            s = nt(k[m], qh)
            p = jnp.where(alive, jnp.exp(s - lse[m, pl.ds(h, 1), at]), 0.0)
            dp = nt(v[m], gh)
            ds = (p * (dp - delta[pl.ds(h, 1), at])).astype(BF)
            dv[...] += nn(p.astype(BF), gh)
            dk[...] += nn(ds, qh)
            dq_t[hs, at] = nn(k_t[hs, :], ds)
            for j, hook in enumerate(hooks):
                pl.when(i == j)(hook)
            return carry

        lax.fori_loop(0, 2 * n_b, block, 0)
        dq = dq_t[...].T * 0.125
        joined[m, :, 0:128] = rotate(dq, turn[0], turn[1], -1.0).astype(BF)
        joined[m, :, 128:256] = rotate(dk[...], turn[0], turn[1], -1.0).astype(BF)
        joined[m, :, 256:384] = dv[...].astype(BF)

    def nothing():
        pass

    def h0():
        g3[1].s1()
        red4[0].s1()

    def h1():
        g3[1].s2()
        red4[0].s2()

    def h2():
        g3[1].s3()
        red4[0].s3()

    def h3():
        red4[1].s1()

    attend_back(0, (h0, h1, h2, h3))
    g3[1].s4()
    l_hidden.wait()
    l_wq.wait()

    def finish_out(m):
        rows_out = hidden[m] + red4[m].s4()
        orow[m] = rows_out.astype(BF).reshape(orow.shape[1:])
        ret_o.start(m)
        red4[m].end()

    finish_out(0)
    product(red3, 0, joined_rows, lambda: wq[...].reshape(D, -1))

    def k0():
        red4[1].s2()
        red3[0].s1()

    def k1():
        red4[1].s3()
        red3[0].s2()

    def k2():
        red3[0].s3()

    attend_back(1, (k0, k1, k2))
    finish_out(1)
    product(red3, 1, joined_rows, lambda: wq[...].reshape(D, -1))
    red3[1].s1()
    each([l_mixed, l_first, l_tok, l_hg], "wait")
    flat_j = joined[...].reshape(2 * rows, -1)
    flat_m = mixed[...].reshape(2 * rows, -1)
    n_d = max(256, gl.shape[1])

    def late(b, carry):
        at = pl.ds(pl.multiple_of(b * n_d, n_d), n_d)
        x = first[:, :, :, :, :, at].reshape(2 * rows, n_d)
        y = full[:, :, :, :, :, at].reshape(2 * rows, n_d)
        gq = tn(x, flat_j).astype(BF)
        go = tn(y, flat_m).astype(BF)
        if gl.shape[1] == n_d:
            gl[b, :, 0:384] = gq
            gl[b, :, 384:512] = go
        else:
            blk = n_d // gl.shape[1]
            gl[pl.ds(b * blk, blk), :, 0:384] = gq.reshape(blk, gl.shape[1], 384)
            gl[pl.ds(b * blk, blk), :, 384:512] = go.reshape(blk, gl.shape[1], 128)
        return carry

    lax.fori_loop(0, D // n_d, late, 0)
    collect_l.start()
    red3[1].s2()

    def norm4(m):
        grad = red3[m].s4()
        hat, inv = norm_stats(tok[m].reshape(-1, D).astype(F32))
        new = hg[m] + norm_back(grad, hat, inv, gains[0:1, :])
        grow[m] = new.astype(BF).reshape(grow.shape[1:])
        ret_g.start(m)
        return jnp.sum(grad * hat, axis=0, keepdims=True)

    gain1 = norm4(0)
    red3[1].s3()
    collect_g.total(accg)
    ssend[...] = accg[...].astype(BF).reshape(4, -1, ng)
    swap.start()
    collect_l.relay()
    gain1 = gain1 + norm4(1)
    row = lax.broadcasted_iota(jnp.int32, gain2.shape, 0)
    gt[0] = jnp.where(row == 0, gain1, jnp.where(row == 1, gain2[...], 0.0))
    s0.start()
    ret_o.wait()
    s0.wait_recv()
    gp[c] = gt[0] + gt[1]
    each(gps, "start")
    collect_l.total(accl)
    slate[...] = accl[...].astype(BF).reshape(4, -1, nl)
    swap_late.start()
    each(gps, "wait_recv")
    gz[f] = jnp.sum(gp[...], axis=0)
    each(gzs, "start")
    swap.keep()
    swap_late.keep()
    ret_g.wait()
    ret_o.end()

    def unpack(dst, back, other):
        for s in range(n_f):
            dst[t, s] = back[owners[t, s]]
            dst[1 - t, s] = other[owners[1 - t, s]]

    unpack(out_o, oback, oother)
    each(gzs, "wait_recv")
    gain_o[...] = jnp.sum(gz[...], axis=0)
    ret_g.end()
    unpack(grad_o, gback, gother)
    swap.wait()
    swap_late.wait()
    each([s0] + gps + gzs, "wait_send")
    for x in g3 + red3 + [collect_g, collect_l, swap, swap_late]:
        x.end()


def rope_tables(rows):
    lane = jnp.arange(128, dtype=jnp.int32)
    exponent = (2 * (lane % (HEAD_DIM // 2))).astype(F32)
    inverse = rope_base ** (-exponent / HEAD_DIM)
    sign = jnp.where(lane % HEAD_DIM < HEAD_DIM // 2, -1.0, 1.0)
    fine = jnp.arange(32, dtype=jnp.int32)
    coarse = fine * (rows // 32)
    both = jnp.stack([coarse, fine]).astype(F32)[:, :, None] * inverse[None, None, :]
    cos, sin = jnp.cos(both), jnp.sin(both)
    return jnp.stack([cos[0], sin[0], cos[1], sin[1], jnp.broadcast_to(sign, cos[0].shape)])


def per_device(n_f, n_c, n_t, tokens, cotangent, lengths, owners,
               norm_attn, norm_mlp, w_qkv, w_out, w_in, w_down):
    f, c, t = here()
    micro, seqs, _, piece, _ = tokens.shape
    span = piece * n_f
    half = span // 4
    rows = span * n_c
    assert n_c == 4 and n_t == 2 and micro == 2 and seqs == n_f and rows == 1024
    n_h = n_f // 2
    wr = w_qkv.shape[0]
    hid = w_in.shape[2]
    hp = -(-hid // (n_c * 128)) * 128
    heads = w_qkv.shape[2] // n_c
    wb = n_c * wr

    slots = jnp.arange(n_f, dtype=jnp.int32)
    same = owners[:, :, None] == slots[None, None, :]
    order = jnp.sum(jnp.where(same, slots[None, :, None], 0), axis=1, dtype=jnp.int32)
    place = (f * n_c + c) * wr
    gains_own = jnp.stack([norm_attn, norm_mlp]).astype(F32)
    gains_row = lax.dynamic_update_slice(jnp.zeros((8, D), F32), gains_own, (0, place))

    def quarters(a):
        return a.transpose(2, 0, 1, 3).reshape(n_c, wr, -1)

    more = n_c * hp - hid
    p_qkv = quarters(w_qkv.reshape(wr, 3, n_c, heads))
    p_out = w_out.reshape(n_c, heads, wr).transpose(0, 2, 1)
    p_in = quarters(jnp.pad(w_in, [(0, 0), (0, 0), (0, more)]).reshape(wr, 2, n_c, hp))
    p_down = jnp.pad(w_down, [(0, more), (0, 0)]).reshape(n_c, hp, wr).transpose(0, 2, 1)
    n_q = 3 * heads
    small = rope_tables(rows)

    full_shape = (micro, n_c, 2, 2, half, D)
    own_shape = (micro, n_h, piece, D)
    row_shape = (micro, 2 * half, D)
    head_shape = (micro, rows, 128)
    act_shape = (micro, n_c, span, hp)
    stat_shape, wide_shape = (micro, 8, rows), (micro, 128, rows)
    V = pltpu.VMEM
    w_shapes = [(n_f, n_c, wr, n) for n in (n_q, heads, 2 * hp, hp)]
    send = (micro, n_f, piece, D // 2)
    (gains, tok, hidden, wq, wo, w3, q, k, v, mixed, out_t, lse, first, act, hg, attn, gain2,
     g_in) = comm_call(
        functools.partial(front_kernel, n_f),
        [(shaped((8, D), F32), vm())]
        + [
            (shaped(a, d), hb())
            for a, d in (
                (own_shape, BF), (row_shape, F32), (w_shapes[0], BF), (w_shapes[1], BF),
                (w_shapes[3], BF), (head_shape, BF), (head_shape, BF), (head_shape, BF),
                (head_shape, BF), (wide_shape, F32), (stat_shape, F32), (full_shape, BF),
                (act_shape, BF),
            )
        ]
        + [
            (shaped(row_shape, F32), vm()), (shaped((micro, 2, half, D), BF), vm()),
            (shaped((8, D), F32), vm()), (shaped((D, 3 * hp), BF), vm()),
        ],
        [sm(), sm()] + [vm()] * 8,
        [V(own_shape, BF), V(own_shape, BF), V(row_shape, F32)]
        + [V(a, BF) for a in w_shapes]
        + [V(head_shape, BF)] * 4
        + [V(wide_shape, F32), V(stat_shape, F32), V(act_shape, BF)]
        + [
            V(send, BF), V(send, BF), V((n_f, 8, D), F32), V((n_c, 8, D), F32),
            V(full_shape, BF), V(full_shape, BF), V(full_shape, BF),
            V((micro, n_c, span, 2 * hp), BF),
        ]
        + reduce_scratch(half)
        + [V((128, rows), BF), V((2, rows, 128), F32)],
        6 * n_f + 160, 16, 0, 10**10,
    )(order, lengths, tokens[:, :, 0], cotangent[:, :, 0], gains_row, p_qkv, p_out, p_in, p_down,
      small)

    outs, grads, gain_grads, early, late = comm_call(
        functools.partial(third_kernel, n_f),
        [
            (shaped((micro, n_f, piece, D), BF), vm()), (shaped((micro, n_f, piece, D), BF), vm()),
            (shaped((8, D), F32), vm()), (shaped((n_c, wr, 3 * hp), BF), vm()),
            (shaped((n_c, wr, n_q + heads), BF), vm()),
        ],
        [sm(), sm(), vm()] + [hb()] * 14 + [vm()] * 4,
        [V(w_shapes[1], BF), V(w_shapes[0], BF), V(w_shapes[3], BF), V(act_shape, BF)]
        + [V(head_shape, BF)] * 4
        + [V(wide_shape, F32), V(stat_shape, F32), V(row_shape, F32), V(row_shape, F32),
           V(own_shape, BF), V((2, rows, 128), F32)]
        + [
            V(full_shape, BF), V(full_shape, BF), V((rows, 128), F32), V((rows, 128), F32),
            V((128, rows), F32), V((rows, 128), BF), V((8, rows), F32), V((128, rows), BF),
            V((micro, rows, 384), BF),
        ]
        + reduce_scratch(half)
        + reduce_scratch(half)[1:]
        + [
            V((n_f, wb, n_q + heads), BF),
            V((collect_slots(n_f), wb, n_q + heads), BF), V((collect_slots(n_f), wb, 3 * hp), BF),
            V((wb, n_q + heads), F32), V((wb, 3 * hp), F32),
            V((n_c, wr, 3 * hp), BF), V((n_c, wr, n_q + heads), BF),
            V(own_shape, BF), V(own_shape, BF),
            V((n_f, piece, D), BF), V((n_f, piece, D), BF),
            V((n_f, piece, D), BF), V((n_f, piece, D), BF),
            V((n_f, 8, D), F32), V((n_c, 8, D), F32), V((2, 8, D), F32),
        ],
        6 * n_f + 100, 16, 1, 10**10,
    )(owners, lengths, attn, wo, wq, w3, act, q, k, v, mixed, out_t, lse, first, hg, hidden, tok,
      gains, gain2, g_in.reshape(n_f, wb, 3 * hp), small)

    grad_qkv = late[:, :, :n_q].astype(F32).reshape(n_c, wr, 3, heads).transpose(1, 2, 0, 3)
    grad_qkv = grad_qkv.reshape(wr, 3, n_c * heads)
    grad_out = late[:, :, n_q:].astype(F32).transpose(0, 2, 1).reshape(n_c * heads, wr)
    grad_in = early[:, :, : 2 * hp].astype(F32).reshape(n_c, wr, 2, hp)
    grad_in = grad_in.transpose(1, 2, 0, 3).reshape(wr, 2, n_c * hp)[..., :hid]
    grad_down = early[:, :, 2 * hp :].astype(F32).transpose(0, 2, 1).reshape(n_c * hp, wr)[:hid]
    mine = lax.dynamic_slice(gain_grads, (0, place), (2, wr))
    return (outs[:, :, None], grads[:, :, None], mine[0], mine[1],
            grad_qkv, grad_out, grad_in, grad_down)


def solution(mesh):
    rows = P(None, None, "ctx", "fsdp", None)
    gain = P(("fsdp", "ctx"))
    tall = P(("fsdp", "ctx"), None, "tp")
    wide = P("tp", ("fsdp", "ctx"))
    return jax.shard_map(
        functools.partial(per_device, mesh.shape["fsdp"], mesh.shape["ctx"], mesh.shape["tp"]),
        mesh=mesh,
        in_specs=(rows, rows, P(), P(), gain, gain, tall, wide, tall, wide),
        out_specs=(rows, rows, gain, gain, tall, wide, tall, wide),
        check_vma=False,
    )
```

```python
import functools

import jax
import jax.numpy as jnp
from jax import lax
from jax.experimental import pallas as pl
from jax.experimental.pallas import tpu as pltpu
from jax.sharding import PartitionSpec as P

D = 1024
HEAD_DIM = 64
norm_eps = 1e-05
rope_base = 160000.0
masked_score = -1e30
MESH = pl.DeviceIdType.MESH
BF = jnp.bfloat16
F32 = jnp.float32
VLIMIT = 56 << 20


def nn(a, b):
    return lax.dot_general(a, b, (((1,), (0,)), ((), ())), preferred_element_type=F32)


def nt(a, b):
    return lax.dot_general(a, b, (((1,), (1,)), ((), ())), preferred_element_type=F32)


def tn(a, b):
    return lax.dot_general(a, b, (((0,), (0,)), ((), ())), preferred_element_type=F32)


def norm_stats(values):
    center = values - jnp.mean(values, axis=-1, keepdims=True)
    spread = jnp.mean(center * center, axis=-1, keepdims=True)
    inverse_std = lax.rsqrt(spread + norm_eps)
    return center * inverse_std, inverse_std


def norm_back(upstream, normed, inverse_std, gain):
    scaled = upstream * gain
    adjusted = (
        scaled
        - jnp.mean(scaled, axis=-1, keepdims=True)
        - normed * jnp.mean(scaled * normed, axis=-1, keepdims=True)
    )
    return adjusted * inverse_std


def here():
    return lax.axis_index("fsdp"), lax.axis_index("ctx"), lax.axis_index("tp")


def remote(src, dst, sems, i, where, j=None):
    return pltpu.make_async_remote_copy(
        src_ref=src,
        dst_ref=dst,
        send_sem=sems.at[0, i],
        recv_sem=sems.at[1, i if j is None else j],
        device_id=where,
        device_id_type=MESH,
    )


def greet(peers):
    bar = pltpu.get_barrier_semaphore()
    for p in peers:
        pl.semaphore_signal(bar, inc=1, device_id=p, device_id_type=MESH)
    pl.semaphore_wait(bar, len(peers))


class Ids:
    def __init__(self):
        self.next = 0

    def take(self, count):
        self.next += count
        return self.next - count


def each(copies, what):
    for copy in copies:
        getattr(copy, what)()


class Gather:
    def __init__(self, full, m, sems, ids):
        f, c, t = here()
        px, py, po = (f, c ^ 1, t), (f, c ^ 2, t), (f, c, 1 - t)
        cx, cy, cd = c ^ 1, c ^ 2, c ^ 3
        base = ids.take(10)

        def cp(i, view, where):
            return remote(view, view, sems, base + i, where)

        self.bx = cp(0, full.at[m, c, t, 1], px)
        self.ay = cp(1, full.at[m, c, t, 0], py)
        self.ax = cp(2, full.at[m, c, t, 0], px)
        self.by = cp(3, full.at[m, c, t, 1], py)
        self.oo = cp(4, full.at[m, c, t], po)
        self.fy = cp(5, full.at[m, cx, t, 1], py)
        self.fx = cp(6, full.at[m, cy, t, 0], px)
        self.ox = cp(7, full.at[m, cx, t], po)
        self.oy = cp(8, full.at[m, cy, t], po)
        self.od = cp(9, full.at[m, cd, t], po)

    def s0(self):
        each([self.bx, self.ay, self.ax, self.by, self.oo], "start")

    def s1(self):
        self.bx.wait_recv()
        self.fy.start()
        self.ay.wait_recv()
        self.fx.start()

    def s2(self):
        self.ax.wait_recv()
        self.ox.start()
        self.by.wait_recv()
        self.oy.start()

    def s3(self):
        self.fy.wait_recv()
        self.fx.wait_recv()
        self.od.start()

    def s4(self):
        each([self.oo, self.ox, self.oy, self.od], "wait_recv")

    def rest(self):
        self.s2()
        self.s3()
        self.s4()

    def end(self):
        each(
            [self.bx, self.ay, self.ax, self.by, self.oo, self.fy, self.fx, self.ox, self.oy,
             self.od],
            "wait_send",
        )


class Reduce:
    def __init__(self, part, r0, rx, ry, sems, ids):
        f, c, t = here()
        px, py, self.po = (f, c ^ 1, t), (f, c ^ 2, t), (f, c, 1 - t)
        cx, cy, cd = c ^ 1, c ^ 2, c ^ 3
        self.base = ids.take(10)
        self.part, self.r0, self.rx, self.ry, self.sems = part, r0, rx, ry, sems
        self.own, self.t, self.cx, self.cy, self.cd = c, t, cx, cy, cd

        def cp(i, src, dst, where):
            return remote(src, dst, sems, self.base + i, where)

        self.cross = [self.crossing(i) for i in range(4)]
        self.a0 = cp(4, part.at[cd, t, 0], rx.at[0], px)
        self.b0 = cp(5, part.at[cd, t, 1], ry.at[0], py)
        self.a1 = cp(6, part.at[cx, t, 0], rx.at[1], px)
        self.b1 = cp(7, part.at[cy, t, 1], ry.at[1], py)
        self.b2 = cp(8, part.at[cy, t, 0], ry.at[2], py)
        self.a2 = cp(9, part.at[cx, t, 1], rx.at[2], px)

    def span(self, i):
        return self.own ^ (3 - i - jnp.where(jnp.int32(i) == 1, 1, 0) + jnp.where(jnp.int32(i) == 2, 1, 0))

    def crossing(self, i):
        return remote(
            self.part.at[self.span(i), 1 - self.t], self.r0.at[i], self.sems, self.base + i, self.po
        )

    def add(self, i, span):
        self.cross[i].wait_recv()
        part, t = self.part, self.t
        part[span, t] = (part[span, t].astype(F32) + self.r0[i].astype(F32)).astype(BF)

    def s1(self):
        self.add(0, self.cd)
        self.a0.start()
        self.b0.start()

    def s2(self):
        self.add(1, self.cx)
        self.a1.start()
        self.add(2, self.cy)
        self.b1.start()

    def s3(self):
        part, t = self.part, self.t
        self.a0.wait_recv()
        part[self.cy, t, 0] = (part[self.cy, t, 0].astype(F32) + self.rx[0].astype(F32)).astype(BF)
        self.b2.start()
        self.b0.wait_recv()
        part[self.cx, t, 1] = (part[self.cx, t, 1].astype(F32) + self.ry[0].astype(F32)).astype(BF)
        self.a2.start()

    def s4(self):
        self.cross[3].wait_recv()
        own = self.part[self.own, self.t].astype(F32) + self.r0[3].astype(F32)
        each([self.a1, self.b1, self.b2, self.a2], "wait_recv")
        top = own[0] + self.rx[1].astype(F32) + self.ry[2].astype(F32)
        bottom = own[1] + self.ry[1].astype(F32) + self.rx[2].astype(F32)
        return jnp.concatenate([top, bottom], axis=0)

    def end(self):
        each(self.cross + [self.a0, self.b0, self.a1, self.b1, self.b2, self.a2], "wait_send")


def reduce_scratch(half):
    return [
        pltpu.VMEM((2, 4, 2, 2, half, D), BF),
        pltpu.VMEM((2, 4, 2, half, D), BF),
        pltpu.VMEM((2, 3, half, D), BF),
        pltpu.VMEM((2, 3, half, D), BF),
    ]


class Spread:
    def __init__(self, ref, n_f, sems, ids):
        f, c, t = here()
        self.f, self.n_f = f, n_f
        if n_f == 4:
            base = ids.take(6)
            up, down = (lax.rem(f + 1, n_f), c, t), (lax.rem(f + n_f - 1, n_f), c, t)
            self.up, self.down = [], []
            for k in range(3):
                low, high = ref.at[lax.rem(f - k + n_f, n_f)], ref.at[lax.rem(f + k, n_f)]
                self.up.append(remote(low, low, sems, base + k, up))
                self.down.append(remote(high, high, sems, base + 3 + k, down))
        else:
            base = ids.take(1)
            self.copies = [
                remote(ref.at[f], ref.at[f], sems, base, (lax.rem(f + k, n_f), c, t))
                for k in range(1, n_f)
            ]
            most = ref.at[pl.ds(0, n_f - 1)]
            self.all = remote(most, most, sems, base, (f, c, 1 - t))

    def sends_up(self, k):
        return (self.f >= k) & (self.f <= 2)

    def sends_down(self, k):
        return (self.f <= 3 - k) & (self.f >= 1)

    def start(self):
        if self.n_f != 4:
            return each(self.copies, "start")
        pl.when(self.sends_up(0))(self.up[0].start)
        pl.when(self.sends_down(0))(self.down[0].start)

    def arrive(self, k):
        pl.when(self.f >= k + 1)(self.up[k].wait_recv)
        pl.when(self.f <= 2 - k)(self.down[k].wait_recv)

    def step(self, k):
        if self.n_f != 4:
            return
        self.arrive(k - 1)
        pl.when(self.sends_up(k))(self.up[k].start)
        pl.when(self.sends_down(k))(self.down[k].start)

    def wait(self):
        if self.n_f != 4:
            return self.all.wait_recv()
        self.arrive(2)

    def end(self):
        if self.n_f != 4:
            return self.all.wait_send()
        for k in range(3):
            pl.when(self.sends_up(k))(self.up[k].wait_send)
            pl.when(self.sends_down(k))(self.down[k].wait_send)


class Collect:
    def __init__(self, ref, got, n_f, sems, ids, passed=True):
        f, c, t = here()
        n_f = n_f if passed or n_f != 4 else -n_f
        self.f, self.n_f, self.ref, self.got = f, n_f, ref, got
        if n_f == 4:
            base = ids.take(5)
            self.steps = (-1, -2, 1, 2)
            self.copies = []
            for i, d in enumerate(self.steps):
                j = lax.rem(f - d + n_f, n_f)
                self.copies.append(remote(ref.at[j], got.at[i], sems, base + i, (j, c, t)))
            away = jnp.where(f == 0, 3, 0)
            self.far = remote(
                ref.at[away], got.at[4], sems, base + 4, (jnp.where(f == 0, 1, 2), c, t)
            )
        else:
            base = ids.take(1)
            self.copies = []
            n_f = abs(n_f)
            for k in range(1, n_f):
                j = lax.rem(f + k, n_f)
                self.copies.append(remote(ref.at[j], got.at[k - 1], sems, base, (j, c, t)))
            most = ref.at[pl.ds(0, n_f - 1)]
            self.all = remote(most, got.at[pl.ds(0, n_f - 1)], sems, base, (f, c, 1 - t))

    def there(self, d):
        return (self.f - d >= 0) & (self.f - d < 4)

    def late(self, d):
        if d == 2:
            return self.f == 2
        if d == -2:
            return self.f == 1
        return self.f < 0

    def start(self):
        if self.n_f != 4:
            return each(self.copies, "start")
        pl.when((self.f == 0) | (self.f == 3))(self.far.start)
        for d, cp in zip(self.steps, self.copies):
            pl.when(self.there(d) & ~self.late(d))(cp.start)

    def relay(self):
        if self.n_f != 4:
            return
        for d, cp, j in ((2, self.copies[3], 0), (-2, self.copies[1], 3)):

            @pl.when(self.late(d))
            def _():
                self.far.wait_recv()
                self.ref[j] = (self.ref[j].astype(F32) + self.got[4].astype(F32)).astype(BF)
                cp.start()

    def total(self, acc):
        acc[...] = self.ref[self.f].astype(F32)
        if self.n_f != 4:
            self.all.wait_recv()
            for k in range(abs(self.n_f) - 1):
                acc[...] += self.got[k].astype(F32)
            return
        for i, d in enumerate(self.steps):

            @pl.when((self.f + d >= 0) & (self.f + d < 4))
            def _():
                self.copies[i].wait_recv()
                acc[...] += self.got[i].astype(F32)

    def end(self):
        if self.n_f != 4:
            return self.all.wait_send()
        for d, cp in zip(self.steps, self.copies):
            pl.when(self.there(d))(cp.wait_send)
        pl.when((self.f == 0) | (self.f == 3))(self.far.wait_send)


def collect_slots(n_f):
    return 5 if n_f == 4 else n_f - 1


class Deal:
    def __init__(self, stage, own, n_f, sems, ids):
        f, c, t = here()
        n_h = n_f // 2
        self.base = ids.take(2 * n_f)
        self.f, self.t, self.n_f, self.n_h, self.own, self.sems = f, t, n_f, n_h, own, sems
        self.side, at = f // n_h, lax.rem(f, n_h)
        self.mine = self.side == t
        self.moves = []
        for m in range(2):
            dst = self.piece(m, at, t)
            recv = self.base + (m * n_h + at) * 2 + t
            sent = self.base + m * n_f
            away = [
                remote(stage.at[m, lax.rem(f + k, n_f)], dst, sems, sent + k,
                       (lax.rem(f + k, n_f), c, self.side), recv)
                for k in range(1, n_f)
            ]
            over = remote(stage.at[m, f], dst, sems, sent, (f, c, 1 - t), recv)
            keep = pltpu.make_async_copy(stage.at[m, f], dst, sems.at[1, recv])
            self.moves.append((away, over, keep))

    def piece(self, m, j, core):
        wide = D // 2
        return self.own.at[m, j, :, pl.ds(pl.multiple_of(core * wide, wide), wide)]

    def start(self, m):
        away, over, keep = self.moves[m]
        each(away, "start")
        pl.when(self.mine)(keep.start)
        pl.when(~self.mine)(over.start)

    def wait(self, m):
        f, c, t = here()
        for j in range(self.n_h):
            for core in range(2):
                i = self.base + (m * self.n_h + j) * 2 + core
                view = self.piece(m, j, core)
                local = (t == core) & (f == t * self.n_h + j)
                pl.when(local)(pltpu.make_async_copy(view, view, self.sems.at[1, i]).wait)
                pl.when(~local)(remote(view, view, self.sems, i, (f, c, 1 - t)).wait_recv)

    def end(self):
        for away, over, _ in self.moves:
            each(away, "wait_send")
            pl.when(~self.mine)(over.wait_send)


class Return:
    def __init__(self, own, back, other, n_f, sems, ids):
        f, c, t = here()
        n_h = n_f // 2
        self.base = ids.take(2 * n_f + 1)
        self.f, self.t, self.n_f, self.back, self.sems = f, t, n_f, back, sems
        self.moves = []
        for m in range(2):
            for j in range(n_h):
                to = t * n_h + j
                i = self.base + m * n_h + j
                far = remote(own.at[m, j], back.at[f], sems, i, (to, c, m), self.base + f)
                keep = pltpu.make_async_copy(own.at[m, j], back.at[f], sems.at[1, self.base + f])
                self.moves.append((m, (to == f) & (t == m), far, keep))
        self.swap = remote(back, other, sems, self.base + 2 * n_f, (f, c, 1 - t))

    def start(self, m):
        for which, local, far, keep in self.moves:
            if which == m:
                pl.when(local)(keep.start)
                pl.when(~local)(far.start)

    def wait(self):
        n_h = self.n_f // 2
        f, c, t = here()
        for s in range(self.n_f):
            local = (f == s) & (f // n_h == t)
            view = self.back.at[s]
            i = self.base + s
            pl.when(local)(pltpu.make_async_copy(view, view, self.sems.at[1, i]).wait)
            pl.when(~local)(remote(view, view, self.sems, i, (f, c, 1 - t)).wait_recv)
        self.swap.start()

    def end(self):
        self.swap.wait_recv()
        for _, local, far, _ in self.moves:
            pl.when(~local)(far.wait_send)
        self.swap.wait_send()


class Swap:
    def __init__(self, src, dst, sems, ids):
        f, c, t = here()
        base = ids.take(3)
        self.src, self.dst, self.c = src, dst, c
        self.copies = [
            remote(src.at[c ^ k], dst.at[c], sems, base + k - 1, (f, c ^ k, t)) for k in (1, 2, 3)
        ]

    def start(self):
        each(self.copies, "start")

    def keep(self):
        self.dst[self.c] = self.src[self.c]

    def wait(self):
        each(self.copies, "wait_recv")

    def end(self):
        each(self.copies, "wait_send")


def everyone(n_f):
    f, c, t = here()
    peers = [(f, c ^ 1, t), (f, c ^ 2, t), (f, c ^ 3, t), (f, c, 1 - t)]
    for k in range(1, n_f):
        for core in range(2):
            peers.append((lax.rem(f + k, n_f), c, core))
    return peers


def vm():
    return pl.BlockSpec(memory_space=pltpu.VMEM)


def sm():
    return pl.BlockSpec(memory_space=pltpu.SMEM)


def hb():
    return pl.BlockSpec(memory_space=pl.ANY)


def shaped(shape, dtype):
    return jax.ShapeDtypeStruct(shape, dtype)


def comm_call(kernel, outs, ins, scratch, n_sems, n_local, cid, flops):
    return pl.pallas_call(
        kernel,
        out_shape=[s for s, _ in outs],
        in_specs=ins,
        out_specs=[b for _, b in outs],
        scratch_shapes=scratch
        + [pltpu.SemaphoreType.DMA((2, n_sems)), pltpu.SemaphoreType.DMA((n_local,))],
        compiler_params=pltpu.CompilerParams(
            collective_id=cid, has_side_effects=True, vmem_limit_bytes=VLIMIT
        ),
        cost_estimate=pl.CostEstimate(flops=flops, bytes_accessed=1 << 20, transcendentals=0),
    )


def rotate(u, cos, sin, sign):
    lane = lax.broadcasted_iota(jnp.int32, u.shape, 1)
    partner = jnp.where(lane % HEAD_DIM < HEAD_DIM // 2, pltpu.roll(u, 96, 1), pltpu.roll(u, 32, 1))
    return u * cos + partner * (sin * sign)


class Keep:
    def __init__(self, sems):
        self.sems, self.copies = sems, []

    def move(self, src, dst):
        copy = pltpu.make_async_copy(src, dst, self.sems.at[len(self.copies)])
        copy.start()
        self.copies.append(copy)
        return copy


def table(small, dst):
    fine_cos, fine_sin = small[2], small[3]
    steps = fine_cos.shape[0]
    for i in range(dst.shape[1] // steps):
        coarse_cos, coarse_sin = small[0, i : i + 1, :], small[1, i : i + 1, :]
        at = pl.ds(i * steps, steps)
        dst[0, at, :] = coarse_cos * fine_cos - coarse_sin * fine_sin
        dst[1, at, :] = (coarse_sin * fine_cos + coarse_cos * fine_sin) * small[4]


def front_kernel(
    n_f, order, lengths, tok, cot_h, gains, pq, po, p2, p3, small,
    gains_o, tok_h, hidden_h, wq_h, wo_h, w3_h, q_h, k_h, v_h, mixed_h, out_h, lse_h, first_h,
    act_h, hg_h, attn_o, gain_o, gi_h,
    tok_o, cot_o, hidden_o, wq, wo, w2, w3, q_o, k_o, v_o, mixed_o, out_o, lse_o, act_o,
    stage, scot, gz, gp, first, cotf, full, gg, hg_o, gi_o, cot, part, r0, rx, ry, v_t, turn,
    sems, lsem,
):
    f, c, t = here()
    ids = Ids()
    plane = [(f, c ^ k, t) for k in (1, 2, 3)]
    zs = [(lax.rem(f + k, n_f), c, t) for k in range(1, n_f)]
    half = first.shape[4]
    rows = 16 * half
    hp = w3.shape[3]
    wide = D // 2

    deal_tok = Deal(stage, tok_o, n_f, sems, ids)
    deal_cot = Deal(scot, cot_o, n_f, sems, ids)
    base = ids.take(n_f - 1)
    gs = [remote(gains, gz.at[f], sems, base + k, zs[k]) for k in range(n_f - 1)]
    base = ids.take(3)
    gps = [remote(gp.at[c], gp.at[c], sems, base + k, plane[k]) for k in range(3)]
    swaps = [Swap(src, w.at[f], sems, ids)
             for src, w in ((pq, wq), (po, wo), (p2, w2), (p3, w3))]
    spreads = [Spread(w, n_f, sems, ids) for w in (wq, wo, w2, w3)]
    g1, gc, g2 = ([Gather(x, m, sems, ids) for m in range(2)] for x in (first, cotf, full))
    red1, red2 = (
        [Reduce(part.at[m], r0.at[m], rx.at[m], ry.at[m], sems, ids) for m in range(2)]
        for _ in range(2)
    )
    keep = Keep(lsem)
    mine = pl.ds(pl.multiple_of(t * wide, wide), wide)

    def stage_rows(src, dst, m):
        for j in range(n_f):
            dst[m, j] = src[m, order[m, j], :, mine]

    load = keep.move(cot_h, cot)
    stage_rows(tok, stage, 0)
    greet(everyone(n_f))
    deal_tok.start(0)
    each(gs, "start")
    each(swaps[:2], "start")
    stage_rows(tok, stage, 1)
    deal_tok.start(1)
    each(swaps[2:], "start")
    each(swaps, "keep")
    gz[f] = gains[...]
    load.wait()
    stage_rows(cot, scot, 0)
    stage_rows(cot, scot, 1)
    table(small, turn)
    each(gs, "wait_recv")
    gp[c] = jnp.sum(gz[...], axis=0)
    each(gps, "start")

    def norm1(m):
        deal_tok.wait(m)
        hat, _ = norm_stats(tok_o[m].reshape(-1, D).astype(F32))
        first[m, c, t] = (hat * gains_o[0:1, :]).astype(BF).reshape(2, half, D)

    each(gps, "wait_recv")
    gains_o[...] = jnp.sum(gp[...], axis=0)
    norm1(0)
    g1[0].s0()
    swaps[0].wait()
    norm1(1)
    spreads[0].start()
    g1[0].s1()
    g1[1].s0()
    spreads[0].step(1)
    swaps[1].wait()
    spreads[1].start()
    g1[0].s2()
    g1[0].s3()
    spreads[0].step(2)
    deal_cot.start(0)
    deal_cot.start(1)
    g1[0].s4()
    spreads[1].step(1)
    spreads[0].wait()
    g1[1].s1()

    def attend(m, hooks):
        joined = nn(first[m].reshape(rows, D), wq[...].reshape(D, -1))
        q_o[m] = rotate(joined[:, 0:128], turn[0], turn[1], 1.0).astype(BF) * BF(0.125)
        k_o[m] = rotate(joined[:, 128:256], turn[0], turn[1], 1.0).astype(BF)
        v = joined[:, 256:384]
        v_o[m] = v.astype(BF)
        v_t[...] = v.T.astype(BF)
        lane = lax.broadcasted_iota(jnp.int32, (rows, 128), 1)
        alive = lax.broadcasted_iota(jnp.int32, (rows, rows), 0) < lengths[m, f]

        def head(h, carry):
            at = pl.ds(pl.multiple_of(h * HEAD_DIM, HEAD_DIM), HEAD_DIM)
            qh = jnp.where(lane // HEAD_DIM == h, q_o[m], BF(0.0))
            s = jnp.where(alive, nt(k_o[m], qh), masked_score)
            top = jnp.max(s, axis=0, keepdims=True)
            p = jnp.exp(s - top)
            total = jnp.sum(p, axis=0, keepdims=True)
            out_o[m, at, :] = nn(v_t[at, :], p.astype(BF)) / total
            lse_o[m, pl.ds(h, 1), :] = top + jnp.log(total)
            for i, hook in enumerate(hooks):
                pl.when(h == i)(hook)
            return carry

        lax.fori_loop(0, 2, head, 0)
        mixed_o[m] = out_o[m].T.astype(BF)

    def product(m):
        def step(i, carry):
            span = red1[m].span(i)
            block = mixed_o[m, pl.ds(pl.multiple_of(span * 4 * half, 4 * half), 4 * half), :]
            part[m, span] = nt(block, wo[...].reshape(D, -1)).astype(BF).reshape(2, 2, half, D)
            red1[m].crossing(i).start()
            return carry

        lax.fori_loop(0, 4, step, 0)

    def norm2(m):
        hidden = tok_o[m].reshape(-1, D).astype(F32) + red1[m].s4()
        hidden_o[m] = hidden
        hat, _ = norm_stats(hidden)
        full[m, c, t] = (hat * gains_o[1:2, :]).astype(BF).reshape(2, half, D)
        g2[m].s0()

    def hook0():
        g1[1].s2()
        spreads[1].step(2)

    attend(0, (hook0, g1[1].s3))
    spreads[1].wait()
    product(0)
    g1[1].s4()
    swaps[2].wait()
    swaps[3].wait()
    spreads[2].start()
    spreads[3].start()
    for src, dst in ((first, first_h), (tok_o, tok_h), (wq, wq_h), (wo, wo_h)):
        keep.move(src, dst)
    red1[0].s1()

    def hook1():
        red1[0].s2()

    def hook2():
        red1[0].s3()
        deal_cot.wait(0)
        cotf[0, c, t] = cot_o[0].reshape(2, half, D)

    attend(1, (hook1, hook2))
    product(1)
    gc[0].s0()
    red1[1].s1()
    deal_cot.wait(1)
    cotf[1, c, t] = cot_o[1].reshape(2, half, D)
    norm2(0)
    red1[1].s2()
    spreads[2].step(1)
    spreads[3].step(1)
    red1[1].s3()
    gc[0].s1()
    gc[1].s0()
    g2[0].s1()
    norm2(1)
    spreads[2].step(2)
    spreads[3].step(2)
    gc[0].s2()
    g2[0].s2()
    gc[0].s3()
    g2[0].s3()
    g2[1].s1()
    gc[1].s1()
    for m in range(2):
        red1[m].end()
    for src, dst in ((q_o, q_h), (k_o, k_h), (v_o, v_h), (mixed_o, mixed_h), (out_o, out_h),
                     (lse_o, lse_h), (hidden_o, hidden_h)):
        keep.move(src, dst)
    gc[0].s4()
    g2[0].s4()
    spreads[2].wait()
    spreads[3].wait()
    keep.move(w3, w3_h)

    def mlp(m, hooks):
        def step(i, carry):
            span = red2[m].span(i)
            low = full[m, span].reshape(4 * half, D)
            win = w2[...].reshape(D, 2 * hp)
            u = nn(low, win[:, :hp])
            g = nn(low, win[:, hp:])
            a = nn(cotf[m, span].reshape(4 * half, D), w3[...].reshape(D, hp))
            phi = 0.5 * (1.0 + lax.erf(u * 0.7071067811865476))
            gelu = u * phi
            slope = phi + u * (jnp.exp(-0.5 * u * u) * 0.3989422804014327)
            act_o[m, span] = (gelu * g).astype(BF)
            gg[m, span, :, 0:hp] = (a * g * slope).astype(BF)
            gg[m, span, :, hp:] = (a * gelu).astype(BF)
            part[m, span] = nt(gg[m, span], win).astype(BF).reshape(2, 2, half, D)
            red2[m].crossing(i).start()
            for j, hook in enumerate(hooks):
                pl.when(i == j)(hook)
            return carry

        lax.fori_loop(0, 4, step, 0)

    def rest2():
        gc[1].s2()
        g2[1].s2()

    def rest3():
        gc[1].s3()
        g2[1].s3()

    mlp(0, (rest2, rest3))
    red2[0].s1()
    gc[1].s4()
    g2[1].s4()
    mlp(1, (red2[0].s2, red2[0].s3))
    red2[1].s1()
    keep.move(act_o, act_h)
    flat_act = act_o[...].reshape(2 * rows, hp)
    flat_gg = gg[...].reshape(2 * rows, 2 * hp)
    n_d = 256

    def sums(source, weight, first_column, columns):
        def step(b, carry):
            at = pl.ds(pl.multiple_of(b * n_d, n_d), n_d)
            x = source[:, :, :, :, :, at].reshape(2 * rows, n_d)
            gi_o[at, first_column : first_column + columns] = tn(x, weight).astype(BF)
            return carry

        lax.fori_loop(0, D // n_d, step, 0)

    red2[1].s2()
    sums(cotf, flat_act, 2 * hp, hp)

    def norm3(m):
        grad = red2[m].s4()
        hat, inv = norm_stats(hidden_o[m])
        hg = cot_o[m].reshape(-1, D).astype(F32) + norm_back(grad, hat, inv, gains_o[1:2, :])
        hg_o[m] = hg
        keep.move(hg_o.at[m], hg_h.at[m])
        attn_o[m] = hg.astype(BF).reshape(2, half, D)
        return jnp.sum(grad * hat, axis=0, keepdims=True)

    gain = norm3(0)
    red2[1].s3()

    sums(full, flat_gg, 0, 2 * hp)
    keep.move(gi_o, gi_h)
    gain = gain + norm3(1)
    gain_o[...] = jnp.broadcast_to(gain, gain_o.shape)
    each(gs + gps, "wait_send")
    for x in [deal_tok, deal_cot] + swaps + spreads + g1 + gc + g2 + red2:
        x.end()
    each(keep.copies[1:], "wait")


def third_kernel(
    n_f, owners, lengths, attn, wo_h, wq_h, w3_h, act_h, q_h, k_h, v_h, mixed_h, out_h, lse_h,
    first_h, hg_h, hidden_h, tok_h, gains, gain2, gi_h, small,
    out_o, grad_o, gain_o, early_o, late_o,
    wo, wq, w3, act, q, k, v, mixed, out, lse, hg, hidden, tok, turn, gi,
    full, first, dk, dv, dq_t, mg, delta, k_t, joined, part, r0, rx, ry, r0b, rxb, ryb,
    gl, gotl, gotg, accl, accg, ssend, slate, orow, grow, oback, gback, oother, gother, gz, gp, gt,
    sems, lsem,
):
    f, c, t = here()
    ids = Ids()
    half = full.shape[4]
    rows = 16 * half
    hp = w3.shape[3]
    nl, ng = accl.shape[1], accg.shape[1]
    plane = [(f, c ^ k_, t) for k_ in (1, 2, 3)]
    zs = [(lax.rem(f + k_, n_f), c, t) for k_ in range(1, n_f)]
    po = (f, c, 1 - t)
    g3 = [Gather(full, m, sems, ids) for m in range(2)]
    red4 = [Reduce(part.at[m], r0.at[m], rx.at[m], ry.at[m], sems, ids) for m in range(2)]
    red3 = [Reduce(part.at[m], r0b.at[m], rxb.at[m], ryb.at[m], sems, ids) for m in range(2)]
    collect_g = Collect(gi, gotg, n_f, sems, ids)
    collect_l = Collect(gl, gotl, n_f, sems, ids)
    ret_o = Return(orow, oback, oother, n_f, sems, ids)
    ret_g = Return(grow, gback, gother, n_f, sems, ids)
    swap = Swap(ssend, early_o, sems, ids)
    swap_late = Swap(slate, late_o, sems, ids)
    base = ids.take(1 + 3 + n_f - 1)
    s0 = remote(gt.at[0], gt.at[1], sems, base, po)
    gps = [remote(gp.at[c], gp.at[c], sems, base + 1 + j, plane[j]) for j in range(3)]
    gzs = [remote(gz.at[f], gz.at[f], sems, base + 4 + j, zs[j]) for j in range(n_f - 1)]
    keep = Keep(lsem)
    l_gi, l_act, l_w3, l_wo, l_out, l_q, l_k, l_v, l_lse, l_hidden, l_wq, l_mixed, l_first, l_tok, l_hg = [
        keep.move(src, dst)
        for src, dst in ((gi_h, gi), (act_h, act), (w3_h, w3), (wo_h, wo), (out_h, out), (q_h, q), (k_h, k),
                         (v_h, v), (lse_h, lse), (hidden_h, hidden), (wq_h, wq),
                         (mixed_h, mixed), (first_h, first), (tok_h, tok), (hg_h, hg))
    ]
    for m in range(2):
        full[m, c, t] = attn[m]
    greet(everyone(n_f))
    g3[0].s0()
    l_gi.wait()
    collect_g.start()

    def product(red, m, source, weight):
        def step(i, carry):
            span = red[m].span(i)
            part[m, span] = nt(source(m, span), weight()).astype(BF).reshape(2, 2, half, D)
            red[m].crossing(i).start()
            return carry

        lax.fori_loop(0, 4, step, 0)

    def act_rows(m, span):
        return act[m, span]

    def joined_rows(m, span):
        return joined[m, pl.ds(pl.multiple_of(span * 4 * half, 4 * half), 4 * half), :]

    table(small, turn)
    l_act.wait()
    l_w3.wait()
    g3[0].s1()
    g3[1].s0()
    product(red4, 0, act_rows, lambda: w3[...].reshape(D, hp))
    product(red4, 1, act_rows, lambda: w3[...].reshape(D, hp))
    g3[0].rest()
    collect_g.relay()
    each([l_wo, l_out, l_q, l_k, l_v, l_lse], "wait")
    QB = 512

    def attend_back(m, hooks):
        grad = nn(full[m].reshape(rows, D), wo[...].reshape(D, -1)).astype(BF)
        mg[...] = grad
        weighted = grad.astype(F32).T * out[m]
        delta[0:1, :] = jnp.sum(weighted[:HEAD_DIM], axis=0, keepdims=True)
        delta[1:2, :] = jnp.sum(weighted[HEAD_DIM:], axis=0, keepdims=True)
        k_t[...] = k[m].astype(F32).T.astype(BF)
        dk[...] = jnp.zeros_like(dk)
        dv[...] = jnp.zeros_like(dv)
        lane = lax.broadcasted_iota(jnp.int32, (QB, 128), 1)
        alive = lax.broadcasted_iota(jnp.int32, (rows, QB), 0) < lengths[m, f]
        n_b = rows // QB

        def block(i, carry):
            h = i // n_b
            at = pl.ds(pl.multiple_of(lax.rem(i, n_b) * QB, QB), QB)
            hs = pl.ds(pl.multiple_of(h * HEAD_DIM, HEAD_DIM), HEAD_DIM)
            keep = lane // HEAD_DIM == h
            qh = jnp.where(keep, q[m, at, :], BF(0.0))
            gh = jnp.where(keep, mg[at, :], BF(0.0))
            s = nt(k[m], qh)
            p = jnp.where(alive, jnp.exp(s - lse[m, pl.ds(h, 1), at]), 0.0)
            dp = nt(v[m], gh)
            ds = (p * (dp - delta[pl.ds(h, 1), at])).astype(BF)
            dv[...] += nn(p.astype(BF), gh)
            dk[...] += nn(ds, qh)
            dq_t[hs, at] = nn(k_t[hs, :], ds)
            for j, hook in enumerate(hooks):
                pl.when(i == j)(hook)
            return carry

        lax.fori_loop(0, 2 * n_b, block, 0)
        dq = dq_t[...].T * 0.125
        joined[m, :, 0:128] = rotate(dq, turn[0], turn[1], -1.0).astype(BF)
        joined[m, :, 128:256] = rotate(dk[...], turn[0], turn[1], -1.0).astype(BF)
        joined[m, :, 256:384] = dv[...].astype(BF)

    def nothing():
        pass

    def h0():
        g3[1].s1()
        red4[0].s1()

    def h1():
        g3[1].s2()
        red4[0].s2()

    def h2():
        g3[1].s3()
        red4[0].s3()

    def h3():
        red4[1].s1()

    attend_back(0, (h0, h1, h2, h3))
    g3[1].s4()
    l_hidden.wait()
    l_wq.wait()

    def finish_out(m):
        rows_out = hidden[m] + red4[m].s4()
        orow[m] = rows_out.astype(BF).reshape(orow.shape[1:])
        ret_o.start(m)
        red4[m].end()

    finish_out(0)
    product(red3, 0, joined_rows, lambda: wq[...].reshape(D, -1))

    def k0():
        red4[1].s2()
        red3[0].s1()

    def k1():
        red4[1].s3()
        red3[0].s2()

    def k2():
        red3[0].s3()

    attend_back(1, (k0, k1, k2))
    finish_out(1)
    product(red3, 1, joined_rows, lambda: wq[...].reshape(D, -1))
    red3[1].s1()
    each([l_mixed, l_first, l_tok, l_hg], "wait")
    flat_j = joined[...].reshape(2 * rows, -1)
    flat_m = mixed[...].reshape(2 * rows, -1)
    n_d = max(256, gl.shape[1])

    def late(b, carry):
        at = pl.ds(pl.multiple_of(b * n_d, n_d), n_d)
        x = first[:, :, :, :, :, at].reshape(2 * rows, n_d)
        y = full[:, :, :, :, :, at].reshape(2 * rows, n_d)
        gq = tn(x, flat_j).astype(BF)
        go = tn(y, flat_m).astype(BF)
        if gl.shape[1] == n_d:
            gl[b, :, 0:384] = gq
            gl[b, :, 384:512] = go
        else:
            blk = n_d // gl.shape[1]
            gl[pl.ds(b * blk, blk), :, 0:384] = gq.reshape(blk, gl.shape[1], 384)
            gl[pl.ds(b * blk, blk), :, 384:512] = go.reshape(blk, gl.shape[1], 128)
        return carry

    lax.fori_loop(0, D // n_d, late, 0)
    collect_l.start()
    red3[1].s2()

    def norm4(m):
        grad = red3[m].s4()
        hat, inv = norm_stats(tok[m].reshape(-1, D).astype(F32))
        new = hg[m] + norm_back(grad, hat, inv, gains[0:1, :])
        grow[m] = new.astype(BF).reshape(grow.shape[1:])
        ret_g.start(m)
        return jnp.sum(grad * hat, axis=0, keepdims=True)

    gain1 = norm4(0)
    red3[1].s3()
    collect_g.total(accg)
    ssend[...] = accg[...].astype(BF).reshape(4, -1, ng)
    swap.start()
    collect_l.relay()
    gain1 = gain1 + norm4(1)
    row = lax.broadcasted_iota(jnp.int32, gain2.shape, 0)
    gt[0] = jnp.where(row == 0, gain1, jnp.where(row == 1, gain2[...], 0.0))
    s0.start()
    ret_o.wait()
    s0.wait_recv()
    gp[c] = gt[0] + gt[1]
    each(gps, "start")
    collect_l.total(accl)
    slate[...] = accl[...].astype(BF).reshape(4, -1, nl)
    swap_late.start()
    each(gps, "wait_recv")
    gz[f] = jnp.sum(gp[...], axis=0)
    each(gzs, "start")
    swap.keep()
    swap_late.keep()
    ret_g.wait()
    ret_o.end()

    def unpack(dst, back, other):
        for s in range(n_f):
            dst[t, s] = back[owners[t, s]]
            dst[1 - t, s] = other[owners[1 - t, s]]

    unpack(out_o, oback, oother)
    each(gzs, "wait_recv")
    gain_o[...] = jnp.sum(gz[...], axis=0)
    ret_g.end()
    unpack(grad_o, gback, gother)
    swap.wait()
    swap_late.wait()
    each([s0] + gps + gzs, "wait_send")
    for x in g3 + red3 + [collect_g, collect_l, swap, swap_late]:
        x.end()


def rope_tables(rows):
    lane = jnp.arange(128, dtype=jnp.int32)
    exponent = (2 * (lane % (HEAD_DIM // 2))).astype(F32)
    inverse = rope_base ** (-exponent / HEAD_DIM)
    sign = jnp.where(lane % HEAD_DIM < HEAD_DIM // 2, -1.0, 1.0)
    fine = jnp.arange(32, dtype=jnp.int32)
    coarse = fine * (rows // 32)
    both = jnp.stack([coarse, fine]).astype(F32)[:, :, None] * inverse[None, None, :]
    cos, sin = jnp.cos(both), jnp.sin(both)
    return jnp.stack([cos[0], sin[0], cos[1], sin[1], jnp.broadcast_to(sign, cos[0].shape)])


def per_device(n_f, n_c, n_t, tokens, cotangent, lengths, owners,
               norm_attn, norm_mlp, w_qkv, w_out, w_in, w_down):
    f, c, t = here()
    micro, seqs, _, piece, _ = tokens.shape
    span = piece * n_f
    half = span // 4
    rows = span * n_c
    assert n_c == 4 and n_t == 2 and micro == 2 and seqs == n_f and rows == 1024
    n_h = n_f // 2
    wr = w_qkv.shape[0]
    hid = w_in.shape[2]
    hp = -(-hid // (n_c * 128)) * 128
    heads = w_qkv.shape[2] // n_c
    wb = n_c * wr

    slots = jnp.arange(n_f, dtype=jnp.int32)
    same = owners[:, :, None] == slots[None, None, :]
    order = jnp.sum(jnp.where(same, slots[None, :, None], 0), axis=1, dtype=jnp.int32)
    place = (f * n_c + c) * wr
    gains_own = jnp.stack([norm_attn, norm_mlp]).astype(F32)
    gains_row = lax.dynamic_update_slice(jnp.zeros((8, D), F32), gains_own, (0, place))

    def quarters(a):
        return a.transpose(2, 0, 1, 3).reshape(n_c, wr, -1)

    more = n_c * hp - hid
    p_qkv = quarters(w_qkv.reshape(wr, 3, n_c, heads))
    p_out = w_out.reshape(n_c, heads, wr).transpose(0, 2, 1)
    p_in = quarters(jnp.pad(w_in, [(0, 0), (0, 0), (0, more)]).reshape(wr, 2, n_c, hp))
    p_down = jnp.pad(w_down, [(0, more), (0, 0)]).reshape(n_c, hp, wr).transpose(0, 2, 1)
    n_q = 3 * heads
    small = rope_tables(rows)

    full_shape = (micro, n_c, 2, 2, half, D)
    own_shape = (micro, n_h, piece, D)
    row_shape = (micro, 2 * half, D)
    head_shape = (micro, rows, 128)
    act_shape = (micro, n_c, span, hp)
    stat_shape, wide_shape = (micro, 8, rows), (micro, 128, rows)
    V = pltpu.VMEM
    w_shapes = [(n_f, n_c, wr, n) for n in (n_q, heads, 2 * hp, hp)]
    send = (micro, n_f, piece, D // 2)
    (gains, tok, hidden, wq, wo, w3, q, k, v, mixed, out_t, lse, first, act, hg, attn, gain2,
     g_in) = comm_call(
        functools.partial(front_kernel, n_f),
        [(shaped((8, D), F32), vm())]
        + [
            (shaped(a, d), hb())
            for a, d in (
                (own_shape, BF), (row_shape, F32), (w_shapes[0], BF), (w_shapes[1], BF),
                (w_shapes[3], BF), (head_shape, BF), (head_shape, BF), (head_shape, BF),
                (head_shape, BF), (wide_shape, F32), (stat_shape, F32), (full_shape, BF),
                (act_shape, BF),
            )
        ]
        + [
            (shaped(row_shape, F32), hb()), (shaped((micro, 2, half, D), BF), vm()),
            (shaped((8, D), F32), vm()), (shaped((D, 3 * hp), BF), hb()),
        ],
        [sm(), sm(), vm(), hb()] + [vm()] * 6,
        [V(own_shape, BF), V(own_shape, BF), V(row_shape, F32)]
        + [V(a, BF) for a in w_shapes]
        + [V(head_shape, BF)] * 4
        + [V(wide_shape, F32), V(stat_shape, F32), V(act_shape, BF)]
        + [
            V(send, BF), V(send, BF), V((n_f, 8, D), F32), V((n_c, 8, D), F32),
            V(full_shape, BF), V(full_shape, BF), V(full_shape, BF),
            V((micro, n_c, span, 2 * hp), BF), V(row_shape, F32), V((D, 3 * hp), BF),
            V((micro, seqs, piece, D), BF),
        ]
        + reduce_scratch(half)
        + [V((128, rows), BF), V((2, rows, 128), F32)],
        6 * n_f + 160, 20, 0, 10**10,
    )(order, lengths, tokens[:, :, 0], cotangent[:, :, 0], gains_row, p_qkv, p_out, p_in, p_down,
      small)

    outs, grads, gain_grads, early, late = comm_call(
        functools.partial(third_kernel, n_f),
        [
            (shaped((micro, n_f, piece, D), BF), vm()), (shaped((micro, n_f, piece, D), BF), vm()),
            (shaped((8, D), F32), vm()), (shaped((n_c, wr, 3 * hp), BF), vm()),
            (shaped((n_c, wr, n_q + heads), BF), vm()),
        ],
        [sm(), sm(), vm()] + [hb()] * 14 + [vm(), vm(), hb(), vm()],
        [V(w_shapes[1], BF), V(w_shapes[0], BF), V(w_shapes[3], BF), V(act_shape, BF)]
        + [V(head_shape, BF)] * 4
        + [V(wide_shape, F32), V(stat_shape, F32), V(row_shape, F32), V(row_shape, F32),
           V(own_shape, BF), V((2, rows, 128), F32), V((n_f, wb, 3 * hp), BF)]
        + [
            V(full_shape, BF), V(full_shape, BF), V((rows, 128), F32), V((rows, 128), F32),
            V((128, rows), F32), V((rows, 128), BF), V((8, rows), F32), V((128, rows), BF),
            V((micro, rows, 384), BF),
        ]
        + reduce_scratch(half)
        + reduce_scratch(half)[1:]
        + [
            V((n_f, wb, n_q + heads), BF),
            V((collect_slots(n_f), wb, n_q + heads), BF), V((collect_slots(n_f), wb, 3 * hp), BF),
            V((wb, n_q + heads), F32), V((wb, 3 * hp), F32),
            V((n_c, wr, 3 * hp), BF), V((n_c, wr, n_q + heads), BF),
            V(own_shape, BF), V(own_shape, BF),
            V((n_f, piece, D), BF), V((n_f, piece, D), BF),
            V((n_f, piece, D), BF), V((n_f, piece, D), BF),
            V((n_f, 8, D), F32), V((n_c, 8, D), F32), V((2, 8, D), F32),
        ],
        6 * n_f + 100, 16, 1, 10**10,
    )(owners, lengths, attn, wo, wq, w3, act, q, k, v, mixed, out_t, lse, first, hg, hidden, tok,
      gains, gain2, g_in.reshape(n_f, wb, 3 * hp), small)

    grad_qkv = late[:, :, :n_q].astype(F32).reshape(n_c, wr, 3, heads).transpose(1, 2, 0, 3)
    grad_qkv = grad_qkv.reshape(wr, 3, n_c * heads)
    grad_out = late[:, :, n_q:].astype(F32).transpose(0, 2, 1).reshape(n_c * heads, wr)
    grad_in = early[:, :, : 2 * hp].astype(F32).reshape(n_c, wr, 2, hp)
    grad_in = grad_in.transpose(1, 2, 0, 3).reshape(wr, 2, n_c * hp)[..., :hid]
    grad_down = early[:, :, 2 * hp :].astype(F32).transpose(0, 2, 1).reshape(n_c * hp, wr)[:hid]
    mine = lax.dynamic_slice(gain_grads, (0, place), (2, wr))
    return (outs[:, :, None], grads[:, :, None], mine[0], mine[1],
            grad_qkv, grad_out, grad_in, grad_down)


def solution(mesh):
    rows = P(None, None, "ctx", "fsdp", None)
    gain = P(("fsdp", "ctx"))
    tall = P(("fsdp", "ctx"), None, "tp")
    wide = P("tp", ("fsdp", "ctx"))
    return jax.shard_map(
        functools.partial(per_device, mesh.shape["fsdp"], mesh.shape["ctx"], mesh.shape["tp"]),
        mesh=mesh,
        in_specs=(rows, rows, P(), P(), gain, gain, tall, wide, tall, wide),
        out_specs=(rows, rows, gain, gain, tall, wide, tall, wide),
        check_vma=False,
    )
```
